32 devices in a mesh: ex: 8 (over y, x, core), feat: 4 (over z).
Axes of the slice: x: 2, y: 2, z: 4, core: 2. Of those that a mesh axis runs over, the one named last changes fastest.
Arguments:
- activations: bfloat16 [512, 64, 4096], P('ex', None, 'feat'), may hold values from -6 to 6
- output_gradient_rows: bfloat16 [512, 64, 4096], P('ex', None, 'feat'), may hold values from -6 to 6
- adapter_down_matrix: bfloat16 [4096, 128], P('feat'), may hold values from -0.09375 to 0.09375
- rank_side_sketch: bfloat16 [128, 64], replicated, may hold values from -0.5 to 0.5
- output_side_sketch: bfloat16 [4096, 128], P('feat'), may hold values from -0.09375 to 0.09375
- heldout_gradient_features: float32 [256, 8192], P('ex', 'feat'), may hold values from -6 to 6
- heldout_language_permutation: int32 [256], P('ex'), may hold values from 0 to 255, each once
Outputs:
- scores: float32 [512, 64], P('ex')
The draws below stay inside these ranges and needn't reach their ends.
Inputs may be any that keep to these rules, and one draw needn't show every extreme that they name: `heldout_language_permutation`: every value of 0 to 255 appears once, so every language has 4 validation examples.
All inputs are finite; a program needn't handle non-finite values.
Results may differ from the reference program's by a relative error of at most 0.0029.
Values sent between devices are 32-bit elements; how exact they have to be, the bound alone decides.
No kernel may reach another device: no remote copies, remote signals or barrier semaphores. Data moves between devices by JAX's collectives and lax.ppermute only.
A program may use at most 64 MiB of HBM per device.

```python
import jax
import jax.numpy as jnp
from jax import lax

INPUT_WIDTH = 4096
DOUT = 4096
ADAPTER_RANK = 128
KF = 8192
KO = 128
KR = 64
LANGS = 64
SEQ = 64
EXAMPLES = 512
NVAL = 256
PER_LANG = 4


def block_levels(stream_key, dims, split, low, top_value):
    gain, own = 1.0, jax.random.fold_in(stream_key, 6)
    for dim, shards_of in split:
        draws = jnp.exp(jax.random.uniform(jax.random.fold_in(own, dim), (shards_of,), jnp.float32, low / len(split), top_value / len(split)))
        gain = gain * jnp.repeat(draws, dims[dim] // shards_of).reshape([-1 if axis == dim else 1 for axis in range(len(dims))])
    return gain


def gaussian(own_key, dims, width, bound, cuts=(), kind=jnp.bfloat16):
    loudness = block_levels(own_key, dims, cuts, -0.22, 0.18) if cuts else 1.0
    result = jax.random.normal(own_key, dims, jnp.float32) * width * loudness
    return jnp.minimum(jnp.maximum(result, -bound), bound).astype(kind)


def setup_inputs(seed: int = 0) -> dict:
    arg_keys = jax.random.split(jax.random.key(seed), 8)
    activations = gaussian(arg_keys[0], (EXAMPLES, SEQ, INPUT_WIDTH), 1.0, 6.0, ((0, 8), (2, 4)))
    output_gradient_rows = gaussian(arg_keys[1], (EXAMPLES, SEQ, DOUT), 1.0, 6.0, ((0, 8), (2, 4)))
    adapter_down_matrix = gaussian(arg_keys[2], (INPUT_WIDTH, ADAPTER_RANK), INPUT_WIDTH ** -0.5, 0.09375, ((0, 4),))
    rank_side_sketch = gaussian(arg_keys[3], (ADAPTER_RANK, KR), ADAPTER_RANK ** -0.5, 0.5)
    output_side_sketch = gaussian(arg_keys[4], (DOUT, KO), DOUT ** -0.5, 0.09375, ((0, 4),))
    heldout_gradient_features = gaussian(arg_keys[5], (NVAL, KF), 1.0, 6.0, ((0, 8), (1, 4)), jnp.float32)
    heldout_language_permutation = jax.random.permutation(arg_keys[6], NVAL).astype(jnp.int32)
    return {"activations": activations, "output_gradient_rows": output_gradient_rows, "adapter_down_matrix": adapter_down_matrix, "rank_side_sketch": rank_side_sketch, "output_side_sketch": output_side_sketch, "heldout_gradient_features": heldout_gradient_features, "heldout_language_permutation": heldout_language_permutation}


def reference(activations, output_gradient_rows, adapter_down_matrix, rank_side_sketch, output_side_sketch, heldout_gradient_features, heldout_language_permutation):
    highest = lax.Precision.HIGHEST
    down_projection_name = jnp.dot(adapter_down_matrix, rank_side_sketch, preferred_element_type=jnp.float32).astype(jnp.bfloat16)
    rank_side = jnp.dot(activations.reshape(-1, INPUT_WIDTH), down_projection_name, preferred_element_type=jnp.float32).reshape(EXAMPLES, SEQ, KR)
    out_side = jnp.dot(output_gradient_rows.reshape(-1, DOUT), output_side_sketch, preferred_element_type=jnp.float32).reshape(EXAMPLES, SEQ, KO)
    grad_feat = jnp.einsum('esk,esr->ekr', out_side, rank_side, precision=highest).reshape(EXAMPLES, KF)
    val_unit = heldout_gradient_features * lax.rsqrt(lax.optimization_barrier(jnp.sum(heldout_gradient_features * heldout_gradient_features, axis=1, keepdims=True)) + 1e-06)
    lang = heldout_language_permutation % LANGS
    onehot = (lang[:, None] == jnp.arange(LANGS, dtype=jnp.int32)[None, :]).astype(jnp.float32)
    lang_mean = jnp.dot(onehot.T, val_unit, precision=highest) / PER_LANG
    inner = jnp.dot(grad_feat, lang_mean.T, precision=highest)
    squares = lax.optimization_barrier(jnp.sum(grad_feat * grad_feat, axis=1))
    scale = jnp.sqrt(jnp.float32(KF * PER_LANG))
    return scale * inner * lax.rsqrt(squares + 1e-06)[:, None]
```

```python
import functools

import jax
import jax.numpy as jnp
from jax import lax
from jax.experimental import pallas as pl
from jax.experimental.pallas import tpu as pltpu
from jax.sharding import PartitionSpec as P

KF = 8192
LANGS = 64
UNIT = 4
HIGHEST = lax.Precision.HIGHEST


def project_kernel(units, act_ref, og_ref, down_ref, sketch_ref, o_ref):
    del units
    rows = act_ref.shape[0]
    o_ref[0, :rows, :] = jnp.dot(og_ref[...], sketch_ref[...], preferred_element_type=jnp.float32)
    half = rows // 2
    wide = down_ref.shape[1] // 2
    o_ref[0, rows:, :] = jnp.dot(
        act_ref[:half], down_ref[:, :wide], preferred_element_type=jnp.float32
    ) + jnp.dot(act_ref[half:], down_ref[:, wide:], preferred_element_type=jnp.float32)


def project(units, acts, grads, down, sketch, rows):
    count, width, ko = units.shape[0], acts.shape[1], sketch.shape[1]
    return pl.pallas_call(
        project_kernel,
        out_shape=jax.ShapeDtypeStruct((count, rows + rows // 2, ko), jnp.float32),
        grid_spec=pltpu.PrefetchScalarGridSpec(
            num_scalar_prefetch=1,
            grid=(count,),
            in_specs=[
                pl.BlockSpec((rows, width), lambda i, u: (u[i], 0)),
                pl.BlockSpec((rows, width), lambda i, u: (u[i], 0)),
                pl.BlockSpec(down.shape, lambda i, u: (0, 0)),
                pl.BlockSpec(sketch.shape, lambda i, u: (0, 0)),
            ],
            out_specs=pl.BlockSpec((1, rows + rows // 2, ko), lambda i, u: (i, 0, 0)),
        ),
        cost_estimate=pl.CostEstimate(
            flops=count * rows * width * ko * 4,
            bytes_accessed=count * rows * (width * 4 + ko * 6),
            transcendentals=0,
        ),
        name="project",
    )(units, acts, grads, down, sketch)


def lang_kernel(me_ref, held_ref, square_ref, lang_ref, *o_refs):
    parts = len(o_refs)
    piece = held_ref.shape[1] // parts
    rows = held_ref.shape[0]
    hit = lang_ref[...] == lax.broadcasted_iota(jnp.int32, (LANGS, rows), 0)
    weight = jnp.where(hit, lax.rsqrt(square_ref[...] + 1e-06), 0.0)
    for mask in range(parts):
        part = me_ref[0] ^ mask
        columns = pl.ds(pl.multiple_of(part * piece, piece), piece)
        o_refs[mask][...] = jnp.dot(
            weight, held_ref[:, columns], precision=HIGHEST, preferred_element_type=jnp.float32
        )


def lang_parts(me, held, squares, lang, parts):
    piece = held.shape[1] // parts
    rows = held.shape[0]
    return pl.pallas_call(
        lang_kernel,
        out_shape=[jax.ShapeDtypeStruct((LANGS, piece), jnp.float32)] * parts,
        in_specs=[pl.BlockSpec(memory_space=pltpu.SMEM)] + [pl.BlockSpec(memory_space=pltpu.VMEM)] * 3,
        out_specs=[pl.BlockSpec(memory_space=pltpu.VMEM)] * parts,
        name="lang_parts",
    )(me.reshape(1), held, squares.reshape(1, rows), lang.reshape(1, rows))


def swap(x, axis, mask):
    return lax.ppermute(x, axis, [(i, i ^ mask) for i in range(lax.axis_size(axis))])


def gather_order(me, count):
    return me ^ jnp.arange(count, dtype=jnp.int32)


def fast(acts, grads, adapter, rank_sketch, out_sketch, held, perm):
    feat, ex = lax.axis_index("feat"), lax.axis_index("ex")
    n_feat, n_ex = lax.axis_size("feat"), lax.axis_size("ex")
    ex_dev, seq, width = acts.shape
    ko, kr = out_sketch.shape[1], rank_sketch.shape[1]
    rows = UNIT * seq
    chunk = ex_dev // n_feat // UNIT
    half = chunk // 2
    middle = (feat == 1) | (feat == 2)
    left = feat < 2

    own_square = jnp.sum(held * held, axis=1)
    squares = own_square + sum(swap(own_square, "feat", mask) for mask in (1, 2, 3))

    down = jnp.dot(adapter, rank_sketch, preferred_element_type=jnp.float32).astype(jnp.bfloat16)
    zero = jnp.zeros_like(down)
    down = jnp.concatenate([down, zero, zero, down], axis=1)
    acts2, grads2 = acts.reshape(-1, width), grads.reshape(-1, width)
    flip = lambda c: jnp.where(left, c, 3 - c)
    order = [
        jnp.where(middle, flip(0), flip(3)),
        jnp.where(middle, flip(3), flip(2)),
        jnp.where(middle, flip(2), flip(1)),
        feat,
    ]

    def part(which, start, count):
        units = order[which] * chunk + start + jnp.arange(count, dtype=jnp.int32)
        return project(units.astype(jnp.int32), acts2, grads2, down, out_sketch, rows)

    ends_in = [(0, 1), (3, 2)]
    raw0 = [part(0, i * half, half) for i in range(2)]
    got0 = [swap(x, "feat", 1) for x in raw0]
    raw1 = [part(1, i * half, half) for i in range(2)]
    got1 = [lax.ppermute(x, "feat", ends_in) for x in raw1]
    raw2 = [part(2, i * half, half) for i in range(2)]
    got2 = [lax.ppermute(x, "feat", ends_in) for x in raw2]
    own = part(3, 0, chunk)
    far = [lax.ppermute(g + r, "feat", [(1, 3), (2, 0)]) for g, r in zip(got0, raw1)]
    near = [lax.ppermute(g + r, "feat", [(1, 2), (2, 1)]) for g, r in zip(got1, raw2)]

    parts = lang_parts(ex, held, squares, perm % LANGS, n_ex)
    lang = parts[0] + sum(swap(parts[mask], "ex", mask) for mask in range(1, n_ex))
    lang = jnp.stack([lang] + [swap(lang, "feat", mask) for mask in (1, 2, 3)])
    held_by = [lang]
    cross = [
        [(i, i ^ (2 if i % 2 == 0 else 4)) for i in range(n_ex)],
        [(i, i ^ (4 if i % 2 == 0 else 2)) for i in range(n_ex)],
        [(i, i ^ 1) for i in range(n_ex)],
    ]
    for pairs in cross:
        held_by = held_by + [lax.ppermute(x, "ex", pairs) for x in held_by]
    first = jnp.where(ex % 2 == 0, 2, 4)
    second = 6 - first
    masks = [0, first, second, 6]
    masks = masks + [1, 1 ^ second, 1 ^ first, 7]
    stacked = jnp.stack(held_by)
    place = jnp.stack([jnp.asarray(m, jnp.int32) for m in masks])
    where = jnp.zeros((n_ex,), jnp.int32).at[place].set(jnp.arange(n_ex, dtype=jnp.int32))
    stacked = stacked[where[gather_order(ex, n_ex)]][:, gather_order(feat, n_feat)]
    lang_mean = stacked.transpose(2, 1, 0, 3).reshape(LANGS, KF)

    total = own + jnp.where(
        middle,
        jnp.concatenate(got2) + jnp.concatenate(near),
        jnp.concatenate(got0) + jnp.concatenate(far),
    )
    mine = chunk * UNIT
    out_side = total[:, :rows].reshape(mine, seq, ko)
    rank_side = total[:, rows:].reshape(chunk, UNIT // 2, seq, 2, kr).transpose(0, 3, 1, 2, 4).reshape(mine, seq, kr)
    grad = jnp.einsum("esk,esr->ekr", out_side, rank_side, precision=HIGHEST).reshape(mine, KF)
    inner = jnp.dot(grad, lang_mean.T, precision=HIGHEST)
    norm = jnp.sum(grad * grad, axis=1)
    per_lang = perm.shape[0] * n_ex // LANGS
    scale = jnp.sqrt(jnp.float32(KF * per_lang)) / per_lang
    score = scale * inner * lax.rsqrt(norm + 1e-06)[:, None]
    score = score.reshape(mine // 2, 2 * LANGS)
    scores = jnp.stack([score] + [swap(score, "feat", mask) for mask in (1, 2, 3)])
    return scores[gather_order(feat, n_feat)].reshape(ex_dev, LANGS)


def general(acts, grads, adapter, rank_sketch, out_sketch, held, perm):
    ex_dev = acts.shape[0]
    down = jnp.dot(adapter, rank_sketch, preferred_element_type=jnp.float32).astype(jnp.bfloat16)
    rank_part = jnp.einsum("esd,dr->esr", acts, down, preferred_element_type=jnp.float32)
    rank_side = lax.psum(rank_part, "feat")
    out_part = jnp.einsum("esd,dk->esk", grads, out_sketch, preferred_element_type=jnp.float32)
    out_side = lax.psum_scatter(out_part, "feat", scatter_dimension=2, tiled=True)
    grad = jnp.einsum("esk,esr->ekr", out_side, rank_side, precision=HIGHEST).reshape(ex_dev, -1)
    squares = lax.psum(jnp.sum(held * held, axis=1), "feat")
    unit = held * lax.rsqrt(squares + 1e-06)[:, None]
    onehot = ((perm % LANGS)[:, None] == jnp.arange(LANGS, dtype=jnp.int32)[None, :]).astype(jnp.float32)
    per_lang = perm.shape[0] * lax.axis_size("ex") // LANGS
    lang_mean = lax.psum(jnp.dot(onehot.T, unit, precision=HIGHEST), "ex") / per_lang
    inner, norm = lax.psum(
        (jnp.dot(grad, lang_mean.T, precision=HIGHEST), jnp.sum(grad * grad, axis=1)), "feat"
    )
    scale = jnp.sqrt(jnp.float32(KF * per_lang))
    return scale * inner * lax.rsqrt(norm + 1e-06)[:, None]


def solution(mesh):
    placed = (
        P("ex", None, "feat"),
        P("ex", None, "feat"),
        P("feat", None),
        P(),
        P("feat", None),
        P("ex", "feat"),
        P("ex"),
    )
    body = fast if mesh.shape["feat"] == 4 and mesh.shape["ex"] == 8 else general
    return jax.shard_map(body, mesh=mesh, in_specs=placed, out_specs=P("ex", None), check_vma=False)
```

```python
import functools

import jax
import jax.numpy as jnp
from jax import lax
from jax.experimental import pallas as pl
from jax.experimental.pallas import tpu as pltpu
from jax.sharding import PartitionSpec as P


KF = 8192
LANGS = 64
UNIT = 4
PIECE = 2
HIGHEST = lax.Precision.HIGHEST
SMALL = 24 * 1024 * 1024
VMEM = pl.BlockSpec(memory_space=pltpu.VMEM)
SMEM = pl.BlockSpec(memory_space=pltpu.SMEM)


def project_piece(act, grad, down, sketch, o_ref):
    rows = act.shape[0] // PIECE
    half = rows // 2
    out = jnp.dot(grad, sketch, preferred_element_type=jnp.float32)
    rank = jnp.dot(act, down, preferred_element_type=jnp.float32)
    low = lax.broadcasted_iota(jnp.int32, (half, down.shape[1]), 1) < down.shape[1] // 2
    for unit in range(PIECE):
        start = unit * rows
        o_ref[unit, :rows, :] = out[start : start + rows]
        o_ref[unit, rows:, :] = jnp.where(low, rank[start : start + half], rank[start + half : start + rows])


def first_kernel(order, act_ref, grad_ref, adapter_ref, rank_ref, sketch_ref, held_ref, *o_refs):
    del order
    *piece_refs, down_ref, square_ref = o_refs
    step = pl.program_id(0)

    @pl.when(step == 0)
    def _():
        down = lax.dot_general(
            adapter_ref[...], rank_ref[...], (((1,), (1,)), ((), ())), preferred_element_type=jnp.float32
        )
        down_ref[...] = jnp.concatenate([down, down], axis=1).astype(jnp.bfloat16)
        held = held_ref[...]
        square_ref[...] = jnp.sum(held * held, axis=1, keepdims=True)

    for index, ref in enumerate(piece_refs):

        @pl.when(step == index)
        def _(ref=ref):
            project_piece(act_ref[...], grad_ref[...], down_ref[...], sketch_ref[...], ref)


def more_kernel(order, act_ref, grad_ref, down_ref, sketch_ref, *piece_refs):
    del order
    step = pl.program_id(0)
    for index, ref in enumerate(piece_refs):

        @pl.when(step == index)
        def _(ref=ref):
            project_piece(act_ref[...], grad_ref[...], down_ref[...], sketch_ref[...], ref)


def whole(shape):
    return pl.BlockSpec(shape, lambda i, order: (0,) * len(shape))


def project(kernel, order, first, count, acts, grads, operands, extra):
    ko = operands[-1 if kernel is more_kernel else 2].shape[1]
    width = acts.shape[1]
    rows = acts.shape[0] // order.shape[0]
    piece = (PIECE, rows // PIECE * 3 // 2, ko)
    block = pl.BlockSpec((rows, width), lambda i, order: (order[first + i], 0))
    return pl.pallas_call(
        kernel,
        out_shape=[jax.ShapeDtypeStruct(piece, jnp.float32)] * count + extra,
        grid_spec=pltpu.PrefetchScalarGridSpec(
            num_scalar_prefetch=1,
            grid=(count,),
            in_specs=[block, block] + [whole(x.shape) for x in operands],
            out_specs=[whole(piece)] * count + [whole(x.shape) for x in extra],
        ),
        cost_estimate=pl.CostEstimate(
            flops=count * rows * width * ko * 4,
            bytes_accessed=count * rows * (width * 4 + ko * 6),
            transcendentals=0,
        ),
        name="project",
    )(order, acts, grads, *operands)


def lang_kernel(me_ref, held_ref, lang_ref, *refs):
    *square_refs, other_ref = refs[:5]
    own_refs = refs[5:]
    count = len(own_refs)
    rows, width = held_ref.shape
    piece = width // (2 * count)
    hit = lang_ref[...] == lax.broadcasted_iota(jnp.int32, (LANGS, rows), 0)
    hit = jnp.where(hit, 1.0, 0.0)
    inverse = lax.rsqrt(sum(ref[...] for ref in square_refs) + 1e-06)

    def sums(part):
        columns = pl.ds(pl.multiple_of(part * piece, piece), piece)
        return jnp.dot(
            hit, held_ref[:, columns] * inverse, precision=HIGHEST, preferred_element_type=jnp.float32
        )

    for index in range(count):
        other_ref[index] = sums(me_ref[0] ^ 1 ^ (2 * index))
        own_refs[index][...] = sums(me_ref[0] ^ (2 * index))


def lang_parts(me, held, squares, lang, n_ex):
    rows, width = held.shape
    piece = width // n_ex
    half = n_ex // 2
    return pl.pallas_call(
        lang_kernel,
        out_shape=[jax.ShapeDtypeStruct((half, LANGS, piece), jnp.float32)]
        + [jax.ShapeDtypeStruct((LANGS, piece), jnp.float32)] * half,
        in_specs=[SMEM] + [VMEM] * 6,
        out_specs=[VMEM] * (1 + half),
        compiler_params=pltpu.CompilerParams(vmem_limit_bytes=SMALL),
        name="lang_parts",
    )(me, held, lang.reshape(1, rows), *squares)


def product_kernel(middle_ref, *refs):
    *part_refs, o_ref, square_ref, own_ref, one_ref, two_ref, grad_ref, sem = refs
    own = pltpu.make_async_copy(part_refs[0], own_ref, sem.at[0])
    own.start()

    def fetch(one, two):
        copies = [
            pltpu.make_async_copy(one, one_ref, sem.at[1]),
            pltpu.make_async_copy(two, two_ref, sem.at[2]),
        ]
        for copy in copies:
            copy.start()
        for copy in copies:
            copy.wait()

    @pl.when(middle_ref[0] == 1)
    def _():
        fetch(part_refs[1], part_refs[2])

    @pl.when(middle_ref[0] != 1)
    def _():
        fetch(part_refs[3], part_refs[4])

    own.wait()
    rows = own_ref.shape[1] * 2 // 3
    seq = rows // UNIT
    wide = own_ref.shape[2]
    low = lax.broadcasted_iota(jnp.int32, (seq, wide), 1) < wide // 2

    def split(x, order):
        high = x.astype(jnp.bfloat16)
        rest = (x - high.astype(jnp.float32)).astype(jnp.bfloat16)
        return jnp.concatenate([high, rest, high] if order else [high, high, rest], axis=0)

    def total(unit, start):
        block = (unit, pl.ds(start, seq), slice(None))
        return own_ref[block] + one_ref[block] + two_ref[block]

    for unit in range(PIECE):
        for pair in range(UNIT // 2):
            both = total(unit, rows + pair * seq)
            turned = pltpu.roll(both, wide // 2, 1)
            for side in range(2):
                example = pair + side * (UNIT // 2)
                rank = jnp.where(low, turned, both) if side else jnp.where(low, both, turned)
                grad_ref[unit * UNIT + example] = lax.dot_general(
                    split(total(unit, example * seq), True),
                    split(rank, False),
                    (((0,), (0,)), ((), ())),
                    preferred_element_type=jnp.float32,
                )
    count = PIECE * UNIT
    low = lax.broadcasted_iota(jnp.int32, (count, wide), 1) < wide // 2
    square = jnp.zeros((count, 2 * wide), jnp.float32)
    for index in range(o_ref.shape[0]):
        rows_of = [grad_ref[:, 4 * index + j, :] for j in range(4)]
        part = jnp.concatenate(
            [jnp.where(low, rows_of[0], rows_of[1]), jnp.where(low, rows_of[2], rows_of[3])], axis=1
        )
        square += part * part
        rest = part - part.astype(jnp.bfloat16).astype(jnp.float32)
        o_ref[index] = jnp.concatenate([part, rest], axis=0).astype(jnp.bfloat16)
    square_ref[...] = jnp.sum(square, axis=1, keepdims=True)


def product(middle, parts):
    count, wide = PIECE * UNIT, parts[0].shape[2]
    return pl.pallas_call(
        product_kernel,
        out_shape=[
            jax.ShapeDtypeStruct((wide // 4, 2 * count, 2 * wide), jnp.bfloat16),
            jax.ShapeDtypeStruct((count, 1), jnp.float32),
        ],
        in_specs=[SMEM] + [pl.BlockSpec(memory_space=pl.ANY)] * len(parts),
        out_specs=[VMEM] * 2,
        scratch_shapes=[pltpu.VMEM(parts[0].shape, jnp.float32)] * 3
        + [pltpu.VMEM((count, wide, wide), jnp.float32), pltpu.SemaphoreType.DMA((3,))],
        compiler_params=pltpu.CompilerParams(vmem_limit_bytes=SMALL),
        name="product",
    )(middle, *parts)


def score_kernel(places_ref, *refs, scale, n_lang):
    lang_refs, grad_refs, square_refs, o_ref = refs[:n_lang], refs[n_lang:-1:2], refs[n_lang + 1 : -1 : 2], refs[-1]
    zs = lang_refs[0].shape[0]
    total = None
    for j, ref in enumerate(lang_refs):
        for m in range(zs):
            index = places_ref[n_lang + m] * n_lang + places_ref[j]
            lang = ref[m]
            rest = lang - lang.astype(jnp.bfloat16).astype(jnp.float32)
            lang = jnp.concatenate([lang, rest], axis=0).astype(jnp.bfloat16)
            grad = jnp.concatenate([g[index] for g in grad_refs], axis=0)
            term = lax.dot_general(
                grad, lang, (((1,), (1,)), ((), ())), preferred_element_type=jnp.float32
            )
            total = term if total is None else total + term
    total = total + pltpu.roll(total, LANGS, 1)
    count = square_refs[0].shape[0]
    for index, square_ref in enumerate(square_refs):
        start = 2 * count * index
        inner = total[start : start + count, :LANGS] + total[start + count : start + 2 * count, :LANGS]
        o_ref[index * count : (index + 1) * count] = inner * (lax.rsqrt(square_ref[...] + 1e-06) * scale)


def score(places, langs, products, scale):
    flat = [x for pair in products for x in pair]
    mine = sum(square.shape[0] for _, square in products)
    return pl.pallas_call(
        functools.partial(score_kernel, scale=scale, n_lang=len(langs)),
        out_shape=jax.ShapeDtypeStruct((mine, LANGS), jnp.float32),
        in_specs=[SMEM] + [VMEM] * (len(langs) + len(flat)),
        out_specs=VMEM,
        compiler_params=pltpu.CompilerParams(vmem_limit_bytes=SMALL),
        name="score",
    )(places, *langs, *flat)


def place_kernel(me_ref, *refs):
    *parts, o_ref = refs
    rows = parts[0].shape[0]
    for mask, ref in enumerate(parts):
        o_ref[pl.ds(pl.multiple_of((me_ref[0] ^ mask) * rows, rows), rows), :] = ref[...]


def place(me, parts):
    rows, columns = parts[0].shape
    return pl.pallas_call(
        place_kernel,
        out_shape=jax.ShapeDtypeStruct((rows * len(parts), columns), jnp.float32),
        in_specs=[SMEM] + [VMEM] * len(parts),
        out_specs=VMEM,
        compiler_params=pltpu.CompilerParams(vmem_limit_bytes=SMALL),
        name="place",
    )(me, *parts)


def swap(x, axis, mask):
    return lax.ppermute(x, axis, [(i, i ^ mask) for i in range(lax.axis_size(axis))])


def after(x, *others):
    return lax.optimization_barrier((x, *others))[0]


def fast(*args):
    return ordered(*args)


def ordered(acts, grads, adapter, rank_sketch, out_sketch, held, perm):
    feat, ex = lax.axis_index("feat"), lax.axis_index("ex")
    n_ex = lax.axis_size("ex")
    _, _, width = acts.shape
    middle = (feat == 1) | (feat == 2)
    left = feat < 2
    me_ex = ex.astype(jnp.int32).reshape(1)
    me_feat = feat.astype(jnp.int32).reshape(1)

    base = jnp.array([3, 2, 1, 0, 0, 3, 2, 1, 3, 0, 1, 2, 0, 1, 2, 3], jnp.int32).reshape(4, 4)
    chunks = lax.dynamic_index_in_dim(base, feat, 0, keepdims=False)
    order = (chunks[:, None] * 2 + jnp.arange(2, dtype=jnp.int32)).reshape(-1)
    acts2, grads2 = acts.reshape(-1, width), grads.reshape(-1, width)
    down_like = jax.ShapeDtypeStruct((width, 2 * rank_sketch.shape[1]), jnp.bfloat16)
    square_like = jax.ShapeDtypeStruct((held.shape[0], 1), jnp.float32)
    ends_in = [(0, 1), (3, 2)]
    far_pairs = [(1, 3), (2, 0)]
    near_pairs = [(1, 2), (2, 1)]
    cross = [
        [(i, i ^ (2 if i % 2 == 0 else 4)) for i in range(n_ex)],
        [(i, i ^ (4 if i % 2 == 0 else 2)) for i in range(n_ex)],
        [(i, i ^ 1) for i in range(n_ex)],
    ]

    *raw0, down, own_square = project(
        first_kernel, order, 0, 2, acts2, grads2, [adapter, rank_sketch.T, out_sketch, held], [down_like, square_like]
    )
    squares = [own_square] + [swap(own_square, "feat", mask) for mask in (1, 2, 3)]
    got0 = [swap(x, "feat", 1) for x in raw0]

    other, *parts = lang_parts(me_ex, held, squares, perm % LANGS, n_ex)
    other = swap(other, "ex", 1)
    parts = [x + other[i] for i, x in enumerate(parts)]
    scattered = [swap(parts[i], "ex", 2 * i) for i in range(1, n_ex // 2)]

    raw1 = project(more_kernel, order, 2, 2, acts2, grads2, [after(down, *parts), out_sketch], [])
    sums = [got0[0] + raw1[0]]
    far = [lax.ppermute(sums[0], "feat", far_pairs)]
    lang = after(parts[0], sums[0]) + sum(scattered)
    pair = swap(lang, "feat", 1)
    raw1 = [after(x, lang) for x in raw1]
    got1 = [lax.ppermute(x, "feat", ends_in) for x in raw1]
    sums.append(got0[1] + raw1[1])
    far.append(lax.ppermute(sums[1], "feat", far_pairs))
    *raw2, own_a, own_b = project(
        more_kernel, order, 4, 4, acts2, grads2, [after(down, sums[1]), out_sketch], []
    )
    own = [own_a, own_b]
    got2 = [lax.ppermute(x, "feat", ends_in) for x in raw2]
    pair = jnp.stack([after(lang, own_a), pair])
    far_pair = [lax.ppermute(pair, "feat", far_pairs), lax.ppermute(pair, "feat", near_pairs)]
    sums.append(got1[0] + after(raw2[0], pair))
    near = [lax.ppermute(sums[2], "feat", near_pairs)]
    langs = [jnp.concatenate([after(pair, sums[2]), far_pair[0] + far_pair[1]])]
    langs = langs + [lax.ppermute(x, "ex", cross[0]) for x in langs]
    sums.append(got1[1] + after(raw2[1], langs[0]))
    near.append(lax.ppermute(sums[3], "feat", near_pairs))
    langs[1] = after(langs[1], sums[3])
    langs = langs + [lax.ppermute(x, "ex", cross[1]) for x in langs]
    is_middle = middle.astype(jnp.int32).reshape(1)
    products = [product(is_middle, [after(own[0], langs[1]), got2[0], near[0], got0[0], far[0]])]
    langs[2:] = [after(x, products[0][1]) for x in langs[2:]]
    langs = langs + [lax.ppermute(x, "ex", cross[2]) for x in langs]
    products.append(product(is_middle, [after(own[1], products[0][1]), got2[1], near[1], got0[1], far[1]]))
    one = jnp.where(ex % 2 == 0, 2, 4)
    two = 6 - one
    masks = [0, one, two, 6, 1, 1 ^ two, 1 ^ one, 7]
    second = jnp.where(left, 2, 1)
    places = jnp.stack(
        [jnp.asarray(x, jnp.int32) for x in [ex ^ m for m in masks] + [feat, feat ^ 1, second, second ^ 1]]
    )
    per_lang = perm.shape[0] * n_ex // LANGS
    scale = (KF * per_lang) ** 0.5 / per_lang
    mine = score(places, langs, products, scale)
    return place(me_feat, [mine] + [swap(mine, "feat", mask) for mask in (1, 2, 3)])


def general(acts, grads, adapter, rank_sketch, out_sketch, held, perm):
    ex_dev = acts.shape[0]
    down = jnp.dot(adapter, rank_sketch, preferred_element_type=jnp.float32).astype(jnp.bfloat16)
    rank_part = jnp.einsum("esd,dr->esr", acts, down, preferred_element_type=jnp.float32)
    rank_side = lax.psum(rank_part, "feat")
    out_part = jnp.einsum("esd,dk->esk", grads, out_sketch, preferred_element_type=jnp.float32)
    out_side = lax.psum_scatter(out_part, "feat", scatter_dimension=2, tiled=True)
    grad = jnp.einsum("esk,esr->ekr", out_side, rank_side, precision=HIGHEST).reshape(ex_dev, -1)
    squares = lax.psum(jnp.sum(held * held, axis=1), "feat")
    unit = held * lax.rsqrt(squares + 1e-06)[:, None]
    onehot = ((perm % LANGS)[:, None] == jnp.arange(LANGS, dtype=jnp.int32)[None, :]).astype(jnp.float32)
    per_lang = perm.shape[0] * lax.axis_size("ex") // LANGS
    lang_mean = lax.psum(jnp.dot(onehot.T, unit, precision=HIGHEST), "ex") / per_lang
    inner, norm = lax.psum(
        (jnp.dot(grad, lang_mean.T, precision=HIGHEST), jnp.sum(grad * grad, axis=1)), "feat"
    )
    scale = jnp.sqrt(jnp.float32(KF * per_lang))
    return scale * inner * lax.rsqrt(norm + 1e-06)[:, None]


def solution(mesh):
    placed = (
        P("ex", None, "feat"),
        P("ex", None, "feat"),
        P("feat", None),
        P(),
        P("feat", None),
        P("ex", "feat"),
        P("ex"),
    )
    is_fast = mesh.shape["feat"] == 4 and mesh.shape["ex"] == 8
    body = fast if is_fast else general
    return jax.shard_map(body, mesh=mesh, in_specs=placed, out_specs=P("ex", None), check_vma=False)
```

```python
import functools

import jax
import jax.numpy as jnp
from jax import lax
from jax.experimental import pallas as pl
from jax.experimental.pallas import tpu as pltpu
from jax.sharding import PartitionSpec as P


KF = 8192
LANGS = 64
UNIT = 4
PIECE = 2
HIGHEST = lax.Precision.HIGHEST
SMALL = 24 * 1024 * 1024
VMEM = pl.BlockSpec(memory_space=pltpu.VMEM)
SMEM = pl.BlockSpec(memory_space=pltpu.SMEM)


def project_piece(act, grad, down, sketch, o_ref):
    rows = act.shape[0] // PIECE
    half = rows // 2
    out = jnp.dot(grad, sketch, preferred_element_type=jnp.float32)
    rank = jnp.dot(act, down, preferred_element_type=jnp.float32)
    low = lax.broadcasted_iota(jnp.int32, (half, down.shape[1]), 1) < down.shape[1] // 2
    for unit in range(PIECE):
        start = unit * rows
        o_ref[unit, :rows, :] = out[start : start + rows]
        o_ref[unit, rows:, :] = jnp.where(low, rank[start : start + half], rank[start + half : start + rows])


def first_kernel(order, act_ref, grad_ref, adapter_ref, rank_ref, sketch_ref, held_ref, *o_refs):
    del order
    *piece_refs, down_ref, square_ref = o_refs
    step = pl.program_id(0)

    @pl.when(step == 0)
    def _():
        down = lax.dot_general(
            adapter_ref[...], rank_ref[...], (((1,), (1,)), ((), ())), preferred_element_type=jnp.float32
        )
        down_ref[...] = jnp.concatenate([down, down], axis=1).astype(jnp.bfloat16)
        held = held_ref[...]
        square_ref[...] = jnp.sum(held * held, axis=1, keepdims=True)

    for index, ref in enumerate(piece_refs):

        @pl.when(step == index)
        def _(ref=ref):
            project_piece(act_ref[...], grad_ref[...], down_ref[...], sketch_ref[...], ref)


def more_kernel(order, act_ref, grad_ref, down_ref, sketch_ref, *piece_refs):
    del order
    step = pl.program_id(0)
    for index, ref in enumerate(piece_refs):

        @pl.when(step == index)
        def _(ref=ref):
            project_piece(act_ref[...], grad_ref[...], down_ref[...], sketch_ref[...], ref)


def whole(shape):
    return pl.BlockSpec(shape, lambda i, order: (0,) * len(shape))


def project(kernel, order, first, count, acts, grads, operands, extra):
    ko = operands[-1 if kernel is more_kernel else 2].shape[1]
    width = acts.shape[1]
    rows = acts.shape[0] // order.shape[0]
    piece = (PIECE, rows // PIECE * 3 // 2, ko)
    block = pl.BlockSpec((rows, width), lambda i, order: (order[first + i], 0))
    return pl.pallas_call(
        kernel,
        out_shape=[jax.ShapeDtypeStruct(piece, jnp.float32)] * count + extra,
        grid_spec=pltpu.PrefetchScalarGridSpec(
            num_scalar_prefetch=1,
            grid=(count,),
            in_specs=[block, block] + [whole(x.shape) for x in operands],
            out_specs=[whole(piece)] * count + [whole(x.shape) for x in extra],
        ),
        cost_estimate=pl.CostEstimate(
            flops=count * rows * width * ko * 4,
            bytes_accessed=count * rows * (width * 4 + ko * 6),
            transcendentals=0,
        ),
        compiler_params=pltpu.CompilerParams(vmem_limit_bytes=SMALL),
        name="project",
    )(order, acts, grads, *operands)


def lang_kernel(me_ref, held_ref, lang_ref, *refs):
    *square_refs, other_ref = refs[:5]
    own_refs = refs[5:]
    count = len(own_refs)
    rows, width = held_ref.shape
    piece = width // (2 * count)
    hit = lang_ref[...] == lax.broadcasted_iota(jnp.int32, (LANGS, rows), 0)
    hit = jnp.where(hit, 1.0, 0.0)
    inverse = lax.rsqrt(sum(ref[...] for ref in square_refs) + 1e-06)

    def sums(part):
        columns = pl.ds(pl.multiple_of(part * piece, piece), piece)
        return jnp.dot(
            hit, held_ref[:, columns] * inverse, precision=HIGHEST, preferred_element_type=jnp.float32
        )

    for index in range(count):
        other_ref[index] = sums(me_ref[0] ^ 1 ^ (2 * index))
        own_refs[index][...] = sums(me_ref[0] ^ (2 * index))


def lang_parts(me, held, squares, lang, n_ex):
    rows, width = held.shape
    piece = width // n_ex
    half = n_ex // 2
    return pl.pallas_call(
        lang_kernel,
        out_shape=[jax.ShapeDtypeStruct((half, LANGS, piece), jnp.float32)]
        + [jax.ShapeDtypeStruct((LANGS, piece), jnp.float32)] * half,
        in_specs=[SMEM] + [VMEM] * 6,
        out_specs=[VMEM] * (1 + half),
        compiler_params=pltpu.CompilerParams(vmem_limit_bytes=SMALL),
        name="lang_parts",
    )(me, held, lang.reshape(1, rows), *squares)


def product_kernel(middle_ref, own_ref, r1_ref, r2_ref, r3_ref, r4_ref, o_ref, square_ref, grad_ref):
    middle = middle_ref[0] == 1
    rows = own_ref.shape[1] * 2 // 3
    seq = rows // UNIT
    wide = own_ref.shape[2]
    low = lax.broadcasted_iota(jnp.int32, (seq, wide), 1) < wide // 2

    def split(x, order):
        high = x.astype(jnp.bfloat16)
        rest = (x - high.astype(jnp.float32)).astype(jnp.bfloat16)
        return jnp.concatenate([high, rest, high] if order else [high, high, rest], axis=0)

    def total(unit, start):
        block = (unit, pl.ds(start, seq), slice(None))
        return own_ref[block] + jnp.where(middle, r3_ref[block] + r4_ref[block], r1_ref[block] + r2_ref[block])

    for unit in range(PIECE):
        for pair in range(UNIT // 2):
            both = total(unit, rows + pair * seq)
            turned = pltpu.roll(both, wide // 2, 1)
            for side in range(2):
                example = pair + side * (UNIT // 2)
                rank = jnp.where(low, turned, both) if side else jnp.where(low, both, turned)
                grad_ref[unit * UNIT + example] = lax.dot_general(
                    split(total(unit, example * seq), True),
                    split(rank, False),
                    (((0,), (0,)), ((), ())),
                    preferred_element_type=jnp.float32,
                )
    count = PIECE * UNIT
    low = lax.broadcasted_iota(jnp.int32, (count, wide), 1) < wide // 2
    square = jnp.zeros((count, 2 * wide), jnp.float32)
    for index in range(o_ref.shape[0]):
        rows_of = [grad_ref[:, 4 * index + j, :] for j in range(4)]
        part = jnp.concatenate(
            [jnp.where(low, rows_of[0], rows_of[1]), jnp.where(low, rows_of[2], rows_of[3])], axis=1
        )
        square += part * part
        rest = part - part.astype(jnp.bfloat16).astype(jnp.float32)
        o_ref[index] = jnp.concatenate([part, rest], axis=0).astype(jnp.bfloat16)
    square_ref[...] = jnp.sum(square, axis=1, keepdims=True)


def product(middle, parts):
    count, wide = PIECE * UNIT, parts[0].shape[2]
    return pl.pallas_call(
        product_kernel,
        out_shape=[
            jax.ShapeDtypeStruct((wide // 4, 2 * count, 2 * wide), jnp.bfloat16),
            jax.ShapeDtypeStruct((count, 1), jnp.float32),
        ],
        in_specs=[SMEM] + [VMEM] * len(parts),
        out_specs=[VMEM] * 2,
        scratch_shapes=[pltpu.VMEM((count, wide, wide), jnp.float32)],
        compiler_params=pltpu.CompilerParams(vmem_limit_bytes=SMALL),
        name="product",
    )(middle, *parts)


def score_kernel(places_ref, *refs, scale, n_lang):
    lang_refs, grad_refs, square_refs, o_ref = refs[:n_lang], refs[n_lang:-1:2], refs[n_lang + 1 : -1 : 2], refs[-1]
    zs = lang_refs[0].shape[0]
    total = None
    for j, ref in enumerate(lang_refs):
        for m in range(zs):
            index = places_ref[n_lang + m] * n_lang + places_ref[j]
            lang = ref[m]
            rest = lang - lang.astype(jnp.bfloat16).astype(jnp.float32)
            lang = jnp.concatenate([lang, rest], axis=0).astype(jnp.bfloat16)
            grad = jnp.concatenate([g[index] for g in grad_refs], axis=0)
            term = lax.dot_general(
                grad, lang, (((1,), (1,)), ((), ())), preferred_element_type=jnp.float32
            )
            total = term if total is None else total + term
    total = total + pltpu.roll(total, LANGS, 1)
    count = square_refs[0].shape[0]
    for index, square_ref in enumerate(square_refs):
        start = 2 * count * index
        inner = total[start : start + count, :LANGS] + total[start + count : start + 2 * count, :LANGS]
        o_ref[index * count : (index + 1) * count] = inner * (lax.rsqrt(square_ref[...] + 1e-06) * scale)


def score(places, langs, products, scale):
    flat = [x for pair in products for x in pair]
    mine = sum(square.shape[0] for _, square in products)
    return pl.pallas_call(
        functools.partial(score_kernel, scale=scale, n_lang=len(langs)),
        out_shape=jax.ShapeDtypeStruct((mine, LANGS), jnp.float32),
        in_specs=[SMEM] + [VMEM] * (len(langs) + len(flat)),
        out_specs=VMEM,
        compiler_params=pltpu.CompilerParams(vmem_limit_bytes=SMALL),
        name="score",
    )(places, *langs, *flat)


def place_kernel(me_ref, *refs):
    *parts, o_ref = refs
    rows = parts[0].shape[0]
    for mask, ref in enumerate(parts):
        o_ref[pl.ds(pl.multiple_of((me_ref[0] ^ mask) * rows, rows), rows), :] = ref[...]


def place(me, parts):
    rows, columns = parts[0].shape
    return pl.pallas_call(
        place_kernel,
        out_shape=jax.ShapeDtypeStruct((rows * len(parts), columns), jnp.float32),
        in_specs=[SMEM] + [VMEM] * len(parts),
        out_specs=VMEM,
        compiler_params=pltpu.CompilerParams(vmem_limit_bytes=SMALL),
        name="place",
    )(me, *parts)


def swap(x, axis, mask):
    return lax.ppermute(x, axis, [(i, i ^ mask) for i in range(lax.axis_size(axis))])


def after(x, *others):
    return lax.optimization_barrier((x, *others))[0]


def fast(*args):
    return ordered(*args)


def ordered(acts, grads, adapter, rank_sketch, out_sketch, held, perm):
    feat, ex = lax.axis_index("feat"), lax.axis_index("ex")
    n_ex = lax.axis_size("ex")
    _, _, width = acts.shape
    middle = (feat == 1) | (feat == 2)
    me_ex = ex.astype(jnp.int32).reshape(1)
    me_feat = feat.astype(jnp.int32).reshape(1)

    base = jnp.array([3, 2, 1, 0, 0, 3, 2, 1, 3, 0, 1, 2, 0, 1, 2, 3], jnp.int32).reshape(4, 4)
    chunks = lax.dynamic_index_in_dim(base, feat, 0, keepdims=False)
    order = (chunks[:, None] * 2 + jnp.arange(2, dtype=jnp.int32)).reshape(-1)
    acts2, grads2 = acts.reshape(-1, width), grads.reshape(-1, width)
    adapter, rank_sketch, out_sketch, held, acts2, grads2 = (
        pltpu.with_memory_space_constraint(x, pltpu.HBM)
        for x in (adapter, rank_sketch.T, out_sketch, held, acts2, grads2)
    )
    down_like = jax.ShapeDtypeStruct((width, 2 * rank_sketch.shape[0]), jnp.bfloat16)
    square_like = jax.ShapeDtypeStruct((held.shape[0], 1), jnp.float32)
    round_pairs = [(0, 1), (1, 3), (3, 2), (2, 0)]
    inner_pairs = [(1, 2), (2, 1), (0, 0), (3, 3)]
    cross = [
        [(i, i ^ (2 if i % 2 == 0 else 4)) for i in range(n_ex)],
        [(i, i ^ (4 if i % 2 == 0 else 2)) for i in range(n_ex)],
        [(i, i ^ 1) for i in range(n_ex)],
    ]

    def onward(raw, got):
        return raw + jnp.where(middle, got, 0.0)

    *raw0, down, own_square = project(
        first_kernel, order, 0, 2, acts2, grads2, [adapter, rank_sketch, out_sketch, held], [down_like, square_like]
    )
    squares = [own_square] + [swap(own_square, "feat", mask) for mask in (1, 2, 3)]
    got1 = [swap(x, "feat", 1) for x in raw0]
    raw1 = project(more_kernel, order, 2, 2, acts2, grads2, [down, out_sketch], [])

    other, *parts = lang_parts(me_ex, held, [squares[0]] + [after(x, raw1[0]) for x in squares[1:]], perm % LANGS, n_ex)
    other = swap(other, "ex", 1)
    parts = [x + other[i] for i, x in enumerate(parts)]
    scattered = [swap(parts[i], "ex", 2 * i) for i in range(1, n_ex // 2)]
    sent2 = [onward(after(raw1[0], parts[1]), got1[0])]
    lang = after(parts[0], sent2[0]) + sum(scattered)
    pair = swap(lang, "feat", 1)
    got2 = [lax.ppermute(after(sent2[0], lang), "feat", round_pairs)]
    pair = jnp.stack([lang, pair])
    far_pair = swap(pair, "feat", 2)
    sent2.append(onward(after(raw1[1], pair), got1[1]))
    got2.append(lax.ppermute(sent2[1], "feat", round_pairs))
    *raw2, own_a, own_b = project(
        more_kernel, order, 4, 4, acts2, grads2, [after(down, sent2[1]), out_sketch], []
    )
    own = [own_a, own_b]
    sent3 = [onward(raw2[0], got2[0])]
    got3 = [swap(sent3[0], "feat", 1)]
    got4 = [lax.ppermute(sent3[0], "feat", inner_pairs)]
    langs = [jnp.concatenate([after(pair, sent3[0]), far_pair])]
    langs = langs + [lax.ppermute(x, "ex", cross[0]) for x in langs]
    sent3.append(onward(after(raw2[1], langs[0]), got2[1]))
    got3.append(swap(sent3[1], "feat", 1))
    got4.append(lax.ppermute(sent3[1], "feat", inner_pairs))
    langs[1] = after(langs[1], sent3[1])
    langs = langs + [lax.ppermute(x, "ex", cross[1]) for x in langs]
    is_middle = middle.astype(jnp.int32).reshape(1)
    products = [product(is_middle, [after(own[0], langs[1]), got1[0], got2[0], got3[0], got4[0]])]
    langs[2:] = [after(x, products[0][1]) for x in langs[2:]]
    langs = langs + [lax.ppermute(x, "ex", cross[2]) for x in langs]
    products.append(product(is_middle, [after(own[1], products[0][1]), got1[1], got2[1], got3[1], got4[1]]))
    one = jnp.where(ex % 2 == 0, 2, 4)
    two = 6 - one
    masks = [0, one, two, 6, 1, 1 ^ two, 1 ^ one, 7]
    places = jnp.stack(
        [jnp.asarray(x, jnp.int32) for x in [ex ^ m for m in masks] + [feat, feat ^ 1, feat ^ 2, feat ^ 3]]
    )
    per_lang = perm.shape[0] * n_ex // LANGS
    scale = (KF * per_lang) ** 0.5 / per_lang
    mine = score(places, langs, products, scale)
    return place(me_feat, [mine] + [swap(mine, "feat", mask) for mask in (1, 2, 3)])


def general(acts, grads, adapter, rank_sketch, out_sketch, held, perm):
    ex_dev = acts.shape[0]
    down = jnp.dot(adapter, rank_sketch, preferred_element_type=jnp.float32).astype(jnp.bfloat16)
    rank_part = jnp.einsum("esd,dr->esr", acts, down, preferred_element_type=jnp.float32)
    rank_side = lax.psum(rank_part, "feat")
    out_part = jnp.einsum("esd,dk->esk", grads, out_sketch, preferred_element_type=jnp.float32)
    out_side = lax.psum_scatter(out_part, "feat", scatter_dimension=2, tiled=True)
    grad = jnp.einsum("esk,esr->ekr", out_side, rank_side, precision=HIGHEST).reshape(ex_dev, -1)
    squares = lax.psum(jnp.sum(held * held, axis=1), "feat")
    unit = held * lax.rsqrt(squares + 1e-06)[:, None]
    onehot = ((perm % LANGS)[:, None] == jnp.arange(LANGS, dtype=jnp.int32)[None, :]).astype(jnp.float32)
    per_lang = perm.shape[0] * lax.axis_size("ex") // LANGS
    lang_mean = lax.psum(jnp.dot(onehot.T, unit, precision=HIGHEST), "ex") / per_lang
    inner, norm = lax.psum(
        (jnp.dot(grad, lang_mean.T, precision=HIGHEST), jnp.sum(grad * grad, axis=1)), "feat"
    )
    scale = jnp.sqrt(jnp.float32(KF * per_lang))
    return scale * inner * lax.rsqrt(norm + 1e-06)[:, None]


def solution(mesh):
    placed = (
        P("ex", None, "feat"),
        P("ex", None, "feat"),
        P("feat", None),
        P(),
        P("feat", None),
        P("ex", "feat"),
        P("ex"),
    )
    is_fast = mesh.shape["feat"] == 4 and mesh.shape["ex"] == 8
    body = fast if is_fast else general
    return jax.shard_map(body, mesh=mesh, in_specs=placed, out_specs=P("ex", None), check_vma=False)
```

```python
import functools

import jax
import jax.numpy as jnp
from jax import lax
from jax.experimental import pallas as pl
from jax.experimental.pallas import tpu as pltpu
from jax.sharding import PartitionSpec as P


KF = 8192
LANGS = 64
UNIT = 4
PIECE = 2
HIGHEST = lax.Precision.HIGHEST
SMALL = 24 * 1024 * 1024
VMEM = pl.BlockSpec(memory_space=pltpu.VMEM)
SMEM = pl.BlockSpec(memory_space=pltpu.SMEM)


def project_piece(act, grad, down, sketch, o_ref):
    rows = act.shape[0] // PIECE
    half = rows // 2
    out = jnp.dot(grad, sketch, preferred_element_type=jnp.float32)
    rank = jnp.dot(act, down, preferred_element_type=jnp.float32)
    low = lax.broadcasted_iota(jnp.int32, (half, down.shape[1]), 1) < down.shape[1] // 2
    for unit in range(PIECE):
        start = unit * rows
        o_ref[unit, :rows, :] = out[start : start + rows]
        o_ref[unit, rows:, :] = jnp.where(low, rank[start : start + half], rank[start + half : start + rows])


def first_kernel(order, act_ref, grad_ref, adapter_ref, rank_ref, sketch_ref, held_ref, *o_refs):
    del order
    *piece_refs, down_ref, square_ref = o_refs
    step = pl.program_id(0)

    @pl.when(step == 0)
    def _():
        down = lax.dot_general(
            adapter_ref[...], rank_ref[...], (((1,), (1,)), ((), ())), preferred_element_type=jnp.float32
        )
        down_ref[...] = jnp.concatenate([down, down], axis=1).astype(jnp.bfloat16)
        held = held_ref[...]
        square_ref[...] = jnp.sum(held * held, axis=1, keepdims=True)

    for index, ref in enumerate(piece_refs):

        @pl.when(step == index)
        def _(ref=ref):
            project_piece(act_ref[...], grad_ref[...], down_ref[...], sketch_ref[...], ref)


def more_kernel(order, act_ref, grad_ref, down_ref, sketch_ref, *piece_refs):
    del order
    step = pl.program_id(0)
    for index, ref in enumerate(piece_refs):

        @pl.when(step == index)
        def _(ref=ref):
            project_piece(act_ref[...], grad_ref[...], down_ref[...], sketch_ref[...], ref)


def whole(shape):
    return pl.BlockSpec(shape, lambda i, order: (0,) * len(shape))


def project(kernel, order, first, count, acts, grads, operands, extra):
    ko = operands[-1 if kernel is more_kernel else 2].shape[1]
    width = acts.shape[1]
    rows = acts.shape[0] // order.shape[0]
    piece = (PIECE, rows // PIECE * 3 // 2, ko)
    block = pl.BlockSpec((rows, width), lambda i, order: (order[first + i], 0))
    return pl.pallas_call(
        kernel,
        out_shape=[jax.ShapeDtypeStruct(piece, jnp.float32)] * count + extra,
        grid_spec=pltpu.PrefetchScalarGridSpec(
            num_scalar_prefetch=1,
            grid=(count,),
            in_specs=[block, block] + [whole(x.shape) for x in operands],
            out_specs=[whole(piece)] * count + [whole(x.shape) for x in extra],
        ),
        cost_estimate=pl.CostEstimate(
            flops=count * rows * width * ko * 4,
            bytes_accessed=count * rows * (width * 4 + ko * 6),
            transcendentals=0,
        ),
        compiler_params=pltpu.CompilerParams(vmem_limit_bytes=SMALL),
        name="project",
    )(order, acts, grads, *operands)


def lang_kernel(me_ref, held_ref, lang_ref, *refs):
    *square_refs, other_ref = refs[:5]
    own_refs = refs[5:]
    count = len(own_refs)
    rows, width = held_ref.shape
    piece = width // (2 * count)
    hit = lang_ref[...] == lax.broadcasted_iota(jnp.int32, (LANGS, rows), 0)
    hit = jnp.where(hit, 1.0, 0.0)
    inverse = lax.rsqrt(sum(ref[...] for ref in square_refs) + 1e-06)

    def sums(part):
        columns = pl.ds(pl.multiple_of(part * piece, piece), piece)
        return jnp.dot(
            hit, held_ref[:, columns] * inverse, precision=HIGHEST, preferred_element_type=jnp.float32
        )

    for index in range(count):
        other_ref[index] = sums(me_ref[0] ^ 1 ^ (2 * index))
        own_refs[index][...] = sums(me_ref[0] ^ (2 * index))


def lang_parts(me, held, squares, lang, n_ex):
    rows, width = held.shape
    piece = width // n_ex
    half = n_ex // 2
    return pl.pallas_call(
        lang_kernel,
        out_shape=[jax.ShapeDtypeStruct((half, LANGS, piece), jnp.float32)]
        + [jax.ShapeDtypeStruct((LANGS, piece), jnp.float32)] * half,
        in_specs=[SMEM] + [VMEM] * 6,
        out_specs=[VMEM] * (1 + half),
        compiler_params=pltpu.CompilerParams(vmem_limit_bytes=SMALL),
        name="lang_parts",
    )(me, held, lang.reshape(1, rows), *squares)


def product_kernel(middle_ref, own_ref, r1_ref, r2_ref, r3_ref, r4_ref, o_ref, square_ref, grad_ref):
    middle = middle_ref[0] == 1
    rows = own_ref.shape[1] * 2 // 3
    seq = rows // UNIT
    wide = own_ref.shape[2]
    low = lax.broadcasted_iota(jnp.int32, (seq, wide), 1) < wide // 2

    def split(x, order):
        high = x.astype(jnp.bfloat16)
        rest = (x - high.astype(jnp.float32)).astype(jnp.bfloat16)
        return jnp.concatenate([high, rest, high] if order else [high, high, rest], axis=0)

    def total(unit, start):
        block = (unit, pl.ds(start, seq), slice(None))
        return own_ref[block] + jnp.where(middle, r3_ref[block] + r4_ref[block], r1_ref[block] + r2_ref[block])

    for unit in range(PIECE):
        for pair in range(UNIT // 2):
            both = total(unit, rows + pair * seq)
            turned = pltpu.roll(both, wide // 2, 1)
            for side in range(2):
                example = pair + side * (UNIT // 2)
                rank = jnp.where(low, turned, both) if side else jnp.where(low, both, turned)
                grad_ref[unit * UNIT + example] = lax.dot_general(
                    split(total(unit, example * seq), True),
                    split(rank, False),
                    (((0,), (0,)), ((), ())),
                    preferred_element_type=jnp.float32,
                )
    count = PIECE * UNIT
    low = lax.broadcasted_iota(jnp.int32, (count, wide), 1) < wide // 2
    square = jnp.zeros((count, 2 * wide), jnp.float32)
    for index in range(o_ref.shape[0]):
        rows_of = [grad_ref[:, 4 * index + j, :] for j in range(4)]
        part = jnp.concatenate(
            [jnp.where(low, rows_of[0], rows_of[1]), jnp.where(low, rows_of[2], rows_of[3])], axis=1
        )
        square += part * part
        rest = part - part.astype(jnp.bfloat16).astype(jnp.float32)
        o_ref[index] = jnp.concatenate([part, rest], axis=0).astype(jnp.bfloat16)
    square_ref[...] = jnp.sum(square, axis=1, keepdims=True)


def product(middle, parts):
    count, wide = PIECE * UNIT, parts[0].shape[2]
    return pl.pallas_call(
        product_kernel,
        out_shape=[
            jax.ShapeDtypeStruct((wide // 4, 2 * count, 2 * wide), jnp.bfloat16),
            jax.ShapeDtypeStruct((count, 1), jnp.float32),
        ],
        in_specs=[SMEM] + [VMEM] * len(parts),
        out_specs=[VMEM] * 2,
        scratch_shapes=[pltpu.VMEM((count, wide, wide), jnp.float32)],
        compiler_params=pltpu.CompilerParams(vmem_limit_bytes=SMALL),
        name="product",
    )(middle, *parts)


def score_kernel(feat_ref, ex_ref, *refs, scale, n_lang):
    lang_refs, grad_refs, square_refs, o_ref = refs[:n_lang], refs[n_lang:-1:2], refs[n_lang + 1 : -1 : 2], refs[-1]
    zs = lang_refs[0].shape[0]
    total = None
    feat, ex = feat_ref[0], ex_ref[0]
    middle = (feat == 1) | (feat == 2)
    second = feat ^ jnp.where(middle, 3, 2)
    rows_from = [feat, feat ^ 1, second, second ^ 1]
    masks = [*range(0, n_lang, 2), *range(1, n_lang, 2)]
    for j, ref in enumerate(lang_refs):
        for m in range(zs):
            index = rows_from[m] * n_lang + (ex ^ masks[j])
            lang = ref[m]
            rest = lang - lang.astype(jnp.bfloat16).astype(jnp.float32)
            lang = jnp.concatenate([lang, rest], axis=0).astype(jnp.bfloat16)
            grad = jnp.concatenate([g[index] for g in grad_refs], axis=0)
            term = lax.dot_general(
                grad, lang, (((1,), (1,)), ((), ())), preferred_element_type=jnp.float32
            )
            total = term if total is None else total + term
    total = total + pltpu.roll(total, LANGS, 1)
    count = square_refs[0].shape[0]
    for index, square_ref in enumerate(square_refs):
        start = 2 * count * index
        inner = total[start : start + count, :LANGS] + total[start + count : start + 2 * count, :LANGS]
        o_ref[index * count : (index + 1) * count] = inner * (lax.rsqrt(square_ref[...] + 1e-06) * scale)


def score(feat, ex, langs, products, scale):
    flat = [x for pair in products for x in pair]
    mine = sum(square.shape[0] for _, square in products)
    return pl.pallas_call(
        functools.partial(score_kernel, scale=scale, n_lang=len(langs)),
        out_shape=jax.ShapeDtypeStruct((mine, LANGS), jnp.float32),
        in_specs=[SMEM] * 2 + [VMEM] * (len(langs) + len(flat)),
        out_specs=VMEM,
        compiler_params=pltpu.CompilerParams(vmem_limit_bytes=SMALL),
        name="score",
    )(feat, ex, *langs, *flat)


def small(kernel, shape, middle, operands):
    return pl.pallas_call(
        kernel,
        out_shape=jax.ShapeDtypeStruct(shape, jnp.float32),
        in_specs=[SMEM] + [VMEM] * len(operands),
        out_specs=VMEM,
        compiler_params=pltpu.CompilerParams(vmem_limit_bytes=SMALL),
    )(middle, *operands)


def onward_kernel(middle_ref, raw_ref, got_ref, o_ref):
    o_ref[...] = raw_ref[...] + jnp.where(middle_ref[0] == 1, got_ref[...], 0.0)


def stack_kernel(middle_ref, one_ref, two_ref, o_ref):
    del middle_ref
    o_ref[0] = one_ref[...]
    o_ref[1] = two_ref[...]


def join_kernel(middle_ref, pair_ref, inner_ref, outer_ref, o_ref):
    o_ref[:2] = pair_ref[...]
    o_ref[2:] = jnp.where(middle_ref[0] == 1, inner_ref[...], outer_ref[...])


def place_kernel(me_ref, *refs):
    *parts, o_ref = refs
    rows = parts[0].shape[0]
    for mask, ref in enumerate(parts):
        o_ref[pl.ds(pl.multiple_of((me_ref[0] ^ mask) * rows, rows), rows), :] = ref[...]


def place(me, parts):
    rows, columns = parts[0].shape
    return pl.pallas_call(
        place_kernel,
        out_shape=jax.ShapeDtypeStruct((rows * len(parts), columns), jnp.float32),
        in_specs=[SMEM] + [VMEM] * len(parts),
        out_specs=VMEM,
        compiler_params=pltpu.CompilerParams(vmem_limit_bytes=SMALL),
        name="place",
    )(me, *parts)


def swap(x, axis, mask):
    return lax.ppermute(x, axis, [(i, i ^ mask) for i in range(lax.axis_size(axis))])


def after(x, *others):
    return lax.optimization_barrier((x, *others))[0]


def fast(*args):
    return ordered(*args)


def ordered(acts, grads, adapter, rank_sketch, out_sketch, held, perm):
    feat, ex = lax.axis_index("feat"), lax.axis_index("ex")
    n_ex = lax.axis_size("ex")
    _, _, width = acts.shape
    middle = (feat == 1) | (feat == 2)
    me_ex = ex.astype(jnp.int32).reshape(1)
    me_feat = feat.astype(jnp.int32).reshape(1)

    base = jnp.array([3, 2, 1, 0, 0, 3, 2, 1, 3, 0, 1, 2, 0, 1, 2, 3], jnp.int32).reshape(4, 4)
    chunks = lax.dynamic_index_in_dim(base, feat, 0, keepdims=False)
    order = (chunks[:, None] * 2 + jnp.arange(2, dtype=jnp.int32)).reshape(-1)
    acts2, grads2 = acts.reshape(-1, width), grads.reshape(-1, width)
    adapter, rank_sketch, out_sketch, held, acts2, grads2 = (
        pltpu.with_memory_space_constraint(x, pltpu.HBM)
        for x in (adapter, rank_sketch.T, out_sketch, held, acts2, grads2)
    )
    down_like = jax.ShapeDtypeStruct((width, 2 * rank_sketch.shape[0]), jnp.bfloat16)
    square_like = jax.ShapeDtypeStruct((held.shape[0], 1), jnp.float32)
    round_pairs = [(0, 1), (1, 3), (3, 2), (2, 0)]
    inner_pairs = [(1, 2), (2, 1), (0, 0), (3, 3)]

    is_middle = middle.astype(jnp.int32).reshape(1)

    def onward(raw, got):
        return small(onward_kernel, raw.shape, is_middle, [raw, got])

    *raw0, down, own_square = project(
        first_kernel, order, 0, 2, acts2, grads2, [adapter, rank_sketch, out_sketch, held], [down_like, square_like]
    )
    squares = [own_square] + [swap(own_square, "feat", mask) for mask in (1, 2, 3)]
    got1 = [swap(x, "feat", 1) for x in raw0]
    other, *parts = lang_parts(me_ex, held, squares, perm % LANGS, n_ex)
    other = swap(other, "ex", 1)
    parts = [x + other[i] for i, x in enumerate(parts)]
    scattered = [swap(parts[i], "ex", 2 * i) for i in range(1, n_ex // 2)]
    raw1 = project(more_kernel, order, 2, 2, acts2, grads2, [after(down, *parts), out_sketch], [])
    lang = after(parts[0], raw1[0]) + sum(scattered)
    pair = swap(lang, "feat", 1)
    sent2 = [onward(after(raw1[0], pair), got1[0])]
    got2 = [lax.ppermute(sent2[0], "feat", round_pairs)]
    pair = small(stack_kernel, (2, *lang.shape), is_middle, [lang, pair])
    far_pair = [lax.ppermute(pair, "feat", pairs) for pairs in (inner_pairs, [(1, 3), (2, 0)])]
    sent2.append(onward(after(raw1[1], pair), got1[1]))
    got2.append(lax.ppermute(sent2[1], "feat", round_pairs))
    *raw2, own_a, own_b = project(
        more_kernel, order, 4, 4, acts2, grads2, [after(down, sent2[1]), out_sketch], []
    )
    own = [own_a, own_b]
    sent3 = [onward(raw2[0], got2[0])]
    got3 = [swap(sent3[0], "feat", 1)]
    got4 = [lax.ppermute(sent3[0], "feat", inner_pairs)]
    pair = after(pair, sent3[0])
    langs = [small(join_kernel, (4, *lang.shape), is_middle, [pair, *far_pair])]
    langs = langs + [swap(langs[0], "ex", mask) for mask in range(2, n_ex, 2)]
    sent3.append(onward(after(raw2[1], langs[0]), got2[1]))
    got3.append(swap(sent3[1], "feat", 1))
    got4.append(lax.ppermute(sent3[1], "feat", inner_pairs))
    grad_a, square_a = product(is_middle, [after(own[0], sent3[1]), got1[0], got2[0], got3[0], got4[0]])
    grad_a = pltpu.with_memory_space_constraint(grad_a, pltpu.VMEM)
    langs[1:] = [after(x, square_a) for x in langs[1:]]
    langs = langs + [swap(x, "ex", 1) for x in langs]
    grad_b, square_b = product(is_middle, [after(own[1], square_a), got1[1], got2[1], got3[1], got4[1]])
    grad_b = pltpu.with_memory_space_constraint(grad_b, pltpu.VMEM)
    products = [(grad_a, square_a), (grad_b, square_b)]
    per_lang = perm.shape[0] * n_ex // LANGS
    scale = (KF * per_lang) ** 0.5 / per_lang
    mine = score(me_feat, me_ex, langs, products, scale)
    return place(me_feat, [mine] + [swap(mine, "feat", mask) for mask in (1, 2, 3)])


def general(acts, grads, adapter, rank_sketch, out_sketch, held, perm):
    ex_dev = acts.shape[0]
    down = jnp.dot(adapter, rank_sketch, preferred_element_type=jnp.float32).astype(jnp.bfloat16)
    rank_part = jnp.einsum("esd,dr->esr", acts, down, preferred_element_type=jnp.float32)
    rank_side = lax.psum(rank_part, "feat")
    out_part = jnp.einsum("esd,dk->esk", grads, out_sketch, preferred_element_type=jnp.float32)
    out_side = lax.psum_scatter(out_part, "feat", scatter_dimension=2, tiled=True)
    grad = jnp.einsum("esk,esr->ekr", out_side, rank_side, precision=HIGHEST).reshape(ex_dev, -1)
    squares = lax.psum(jnp.sum(held * held, axis=1), "feat")
    unit = held * lax.rsqrt(squares + 1e-06)[:, None]
    onehot = ((perm % LANGS)[:, None] == jnp.arange(LANGS, dtype=jnp.int32)[None, :]).astype(jnp.float32)
    per_lang = perm.shape[0] * lax.axis_size("ex") // LANGS
    lang_mean = lax.psum(jnp.dot(onehot.T, unit, precision=HIGHEST), "ex") / per_lang
    inner, norm = lax.psum(
        (jnp.dot(grad, lang_mean.T, precision=HIGHEST), jnp.sum(grad * grad, axis=1)), "feat"
    )
    scale = jnp.sqrt(jnp.float32(KF * per_lang))
    return scale * inner * lax.rsqrt(norm + 1e-06)[:, None]


def solution(mesh):
    placed = (
        P("ex", None, "feat"),
        P("ex", None, "feat"),
        P("feat", None),
        P(),
        P("feat", None),
        P("ex", "feat"),
        P("ex"),
    )
    is_fast = mesh.shape["feat"] == 4 and mesh.shape["ex"] == 8
    body = fast if is_fast else general
    return jax.shard_map(body, mesh=mesh, in_specs=placed, out_specs=P("ex", None), check_vma=False)
```

```python
import functools

import jax
import jax.numpy as jnp
from jax import lax
from jax.experimental import pallas as pl
from jax.experimental.pallas import tpu as pltpu
from jax.sharding import PartitionSpec as P


KF = 8192
LANGS = 64
UNIT = 4
PIECE = 2
PIECES = 8
HIGHEST = lax.Precision.HIGHEST
SMALL = 24 * 1024 * 1024
VMEM = pl.BlockSpec(memory_space=pltpu.VMEM)
SMEM = pl.BlockSpec(memory_space=pltpu.SMEM)


def project_piece(act, grad, down, sketch, o_ref):
    rows = act.shape[0] // PIECE
    half = rows // 2
    out = jnp.dot(grad, sketch, preferred_element_type=jnp.float32)
    rank = jnp.dot(act, down, preferred_element_type=jnp.float32)
    low = lax.broadcasted_iota(jnp.int32, (half, down.shape[1]), 1) < down.shape[1] // 2
    for unit in range(PIECE):
        start = unit * rows
        o_ref[unit, :rows, :] = out[start : start + rows]
        o_ref[unit, rows:, :] = jnp.where(low, rank[start : start + half], rank[start + half : start + rows])


def first_kernel(feat, act_ref, grad_ref, adapter_ref, rank_ref, sketch_ref, held_ref, *o_refs):
    del feat
    *piece_refs, down_ref, square_ref = o_refs
    step = pl.program_id(0)

    @pl.when(step == 0)
    def _():
        down = lax.dot_general(
            adapter_ref[...], rank_ref[...], (((1,), (1,)), ((), ())), preferred_element_type=jnp.float32
        )
        down_ref[...] = jnp.concatenate([down, down], axis=1).astype(jnp.bfloat16)
        held = held_ref[...]
        square_ref[...] = jnp.sum(held * held, axis=1, keepdims=True)

    for index, ref in enumerate(piece_refs):

        @pl.when(step == index)
        def _(ref=ref):
            project_piece(act_ref[...], grad_ref[...], down_ref[...], sketch_ref[...], ref)


def more_kernel(feat, act_ref, grad_ref, down_ref, sketch_ref, *piece_refs):
    del feat
    step = pl.program_id(0)
    for index, ref in enumerate(piece_refs):

        @pl.when(step == index)
        def _(ref=ref):
            project_piece(act_ref[...], grad_ref[...], down_ref[...], sketch_ref[...], ref)


def whole(shape):
    return pl.BlockSpec(shape, lambda i, feat: (0,) * len(shape))


def chunk_of(turn, feat):
    left = feat < 2
    far, near = jnp.where(left, 3, 0), jnp.where(left, 2, 1)
    return jnp.where(turn == 0, far, jnp.where(turn == 1, near, jnp.where(turn == 2, feat ^ 1, feat)))


def project(kernel, feat, first, count, acts, grads, operands, extra):
    ko = operands[-1 if kernel is more_kernel else 2].shape[1]
    width = acts.shape[1]
    rows = acts.shape[0] // PIECES
    piece = (PIECE, rows // PIECE * 3 // 2, ko)
    block = pl.BlockSpec((rows, width), lambda i, feat: (chunk_of((first + i) // 2, feat[0]) * 2 + (first + i) % 2, 0))
    return pl.pallas_call(
        kernel,
        out_shape=[jax.ShapeDtypeStruct(piece, jnp.float32)] * count + extra,
        grid_spec=pltpu.PrefetchScalarGridSpec(
            num_scalar_prefetch=1,
            grid=(count,),
            in_specs=[block, block] + [whole(x.shape) for x in operands],
            out_specs=[whole(piece)] * count + [whole(x.shape) for x in extra],
        ),
        cost_estimate=pl.CostEstimate(
            flops=count * rows * width * ko * 4,
            bytes_accessed=count * rows * (width * 4 + ko * 6),
            transcendentals=0,
        ),
        compiler_params=pltpu.CompilerParams(vmem_limit_bytes=SMALL),
        name="project",
    )(feat, acts, grads, *operands)


def lang_kernel(me_ref, held_ref, lang_ref, *refs):
    *square_refs, other_ref = refs[:5]
    own_refs = refs[5:]
    count = len(own_refs)
    rows, width = held_ref.shape
    piece = width // (2 * count)
    hit = lang_ref[...] == lax.broadcasted_iota(jnp.int32, (LANGS, rows), 0)
    hit = jnp.where(hit, 1.0, 0.0)
    inverse = lax.rsqrt(sum(ref[...] for ref in square_refs) + 1e-06)

    def sums(part):
        columns = pl.ds(pl.multiple_of(part * piece, piece), piece)
        return jnp.dot(
            hit, held_ref[:, columns] * inverse, precision=HIGHEST, preferred_element_type=jnp.float32
        )

    for index in range(count):
        other_ref[index] = sums(me_ref[0] ^ 1 ^ (2 * index))
        own_refs[index][...] = sums(me_ref[0] ^ (2 * index))


def lang_parts(me, held, squares, lang, n_ex):
    rows, width = held.shape
    piece = width // n_ex
    half = n_ex // 2
    return pl.pallas_call(
        lang_kernel,
        out_shape=[jax.ShapeDtypeStruct((half, LANGS, piece), jnp.float32)]
        + [jax.ShapeDtypeStruct((LANGS, piece), jnp.float32)] * half,
        in_specs=[SMEM] + [VMEM] * 6,
        out_specs=[VMEM] * (1 + half),
        compiler_params=pltpu.CompilerParams(vmem_limit_bytes=SMALL),
        name="lang_parts",
    )(me, held, lang.reshape(1, rows), *squares)


def product_kernel(middle_ref, own_ref, raw_ref, far_ref, near_ref, o_ref, square_ref, grad_ref):
    middle = middle_ref[0] == 1
    rows = own_ref.shape[1] * 2 // 3
    seq = rows // UNIT
    wide = own_ref.shape[2]
    low = lax.broadcasted_iota(jnp.int32, (seq, wide), 1) < wide // 2

    def split(x, order):
        high = x.astype(jnp.bfloat16)
        rest = (x - high.astype(jnp.float32)).astype(jnp.bfloat16)
        return jnp.concatenate([high, rest, high] if order else [high, high, rest], axis=0)

    def total(unit, start):
        block = (unit, pl.ds(start, seq), slice(None))
        return own_ref[block] + raw_ref[block] + jnp.where(middle, near_ref[block], far_ref[block])

    for unit in range(PIECE):
        for pair in range(UNIT // 2):
            both = total(unit, rows + pair * seq)
            turned = pltpu.roll(both, wide // 2, 1)
            for side in range(2):
                example = pair + side * (UNIT // 2)
                rank = jnp.where(low, turned, both) if side else jnp.where(low, both, turned)
                grad_ref[unit * UNIT + example] = lax.dot_general(
                    split(total(unit, example * seq), True),
                    split(rank, False),
                    (((0,), (0,)), ((), ())),
                    preferred_element_type=jnp.float32,
                )
    count = PIECE * UNIT
    low = lax.broadcasted_iota(jnp.int32, (count, wide), 1) < wide // 2
    square = jnp.zeros((count, 2 * wide), jnp.float32)
    for index in range(o_ref.shape[0]):
        rows_of = [grad_ref[:, 4 * index + j, :] for j in range(4)]
        part = jnp.concatenate(
            [jnp.where(low, rows_of[0], rows_of[1]), jnp.where(low, rows_of[2], rows_of[3])], axis=1
        )
        square += part * part
        rest = part - part.astype(jnp.bfloat16).astype(jnp.float32)
        o_ref[index] = jnp.concatenate([part, rest], axis=0).astype(jnp.bfloat16)
    square_ref[...] = jnp.sum(square, axis=1, keepdims=True)


def product(middle, parts):
    count, wide = PIECE * UNIT, parts[0].shape[2]
    return pl.pallas_call(
        product_kernel,
        out_shape=[
            jax.ShapeDtypeStruct((wide // 4, 2 * count, 2 * wide), jnp.bfloat16),
            jax.ShapeDtypeStruct((count, 1), jnp.float32),
        ],
        in_specs=[SMEM] + [VMEM] * len(parts),
        out_specs=[VMEM] * 2,
        scratch_shapes=[pltpu.VMEM((count, wide, wide), jnp.float32)],
        compiler_params=pltpu.CompilerParams(vmem_limit_bytes=SMALL),
        name="product",
    )(middle, *parts)


def score_kernel(feat_ref, ex_ref, *refs, scale, n_lang):
    lang_refs, grad_refs, square_refs, o_ref = refs[:n_lang], refs[n_lang:-1:2], refs[n_lang + 1 : -1 : 2], refs[-1]
    total = None
    feat, ex = feat_ref[0], ex_ref[0]
    middle = (feat == 1) | (feat == 2)
    second = feat ^ jnp.where(middle, 3, 2)
    rows_from = [feat, feat ^ 1, second, second ^ 1]
    n_ex = n_lang // 2
    masks = [*range(0, n_ex, 2), *range(1, n_ex, 2)]
    for j, ref in enumerate(lang_refs):
        for m in range(2):
            index = rows_from[j // n_ex * 2 + m] * n_ex + (ex ^ masks[j % n_ex])
            lang = ref[m]
            rest = lang - lang.astype(jnp.bfloat16).astype(jnp.float32)
            lang = jnp.concatenate([lang, rest], axis=0).astype(jnp.bfloat16)
            grad = jnp.concatenate([g[index] for g in grad_refs], axis=0)
            term = lax.dot_general(
                grad, lang, (((1,), (1,)), ((), ())), preferred_element_type=jnp.float32
            )
            total = term if total is None else total + term
    total = total + pltpu.roll(total, LANGS, 1)
    count = square_refs[0].shape[0]
    for index, square_ref in enumerate(square_refs):
        start = 2 * count * index
        inner = total[start : start + count, :LANGS] + total[start + count : start + 2 * count, :LANGS]
        o_ref[index * count : (index + 1) * count] = inner * (lax.rsqrt(square_ref[...] + 1e-06) * scale)


def score(feat, ex, langs, products, scale):
    flat = [x for pair in products for x in pair]
    mine = sum(square.shape[0] for _, square in products)
    return pl.pallas_call(
        functools.partial(score_kernel, scale=scale, n_lang=len(langs)),
        out_shape=jax.ShapeDtypeStruct((mine, LANGS), jnp.float32),
        in_specs=[SMEM] * 2 + [VMEM] * (len(langs) + len(flat)),
        out_specs=VMEM,
        compiler_params=pltpu.CompilerParams(vmem_limit_bytes=SMALL),
        name="score",
    )(feat, ex, *langs, *flat)


def small(kernel, shape, middle, operands):
    return pl.pallas_call(
        kernel,
        out_shape=jax.ShapeDtypeStruct(shape, jnp.float32),
        in_specs=[SMEM] + [VMEM] * len(operands),
        out_specs=VMEM,
        compiler_params=pltpu.CompilerParams(vmem_limit_bytes=SMALL),
    )(middle, *operands)


def onward_kernel(middle_ref, raw_ref, got_ref, o_ref):
    o_ref[...] = raw_ref[...] + jnp.where(middle_ref[0] == 1, got_ref[...], 0.0)


def stack_kernel(middle_ref, one_ref, two_ref, o_ref):
    del middle_ref
    o_ref[0] = one_ref[...]
    o_ref[1] = two_ref[...]


def choose_kernel(middle_ref, inner_ref, outer_ref, o_ref):
    o_ref[...] = jnp.where(middle_ref[0] == 1, inner_ref[...], outer_ref[...])


def place_kernel(me_ref, *refs):
    *parts, o_ref = refs
    rows = parts[0].shape[0]
    for mask, ref in enumerate(parts):
        o_ref[pl.ds(pl.multiple_of((me_ref[0] ^ mask) * rows, rows), rows), :] = ref[...]


def place(me, parts):
    rows, columns = parts[0].shape
    return pl.pallas_call(
        place_kernel,
        out_shape=jax.ShapeDtypeStruct((rows * len(parts), columns), jnp.float32),
        in_specs=[SMEM] + [VMEM] * len(parts),
        out_specs=VMEM,
        compiler_params=pltpu.CompilerParams(vmem_limit_bytes=SMALL),
        name="place",
    )(me, *parts)


def swap(x, axis, mask):
    return lax.ppermute(x, axis, [(i, i ^ mask) for i in range(lax.axis_size(axis))])


def after(x, *others):
    return lax.optimization_barrier((x, *others))[0]


def fast(*args):
    return ordered(*args)


def ordered(acts, grads, adapter, rank_sketch, out_sketch, held, perm):
    feat, ex = lax.axis_index("feat"), lax.axis_index("ex")
    n_ex = lax.axis_size("ex")
    _, _, width = acts.shape
    middle = (feat == 1) | (feat == 2)
    me_ex = ex.astype(jnp.int32).reshape(1)
    me_feat = feat.astype(jnp.int32).reshape(1)
    acts2, grads2 = acts.reshape(-1, width), grads.reshape(-1, width)
    adapter, rank_sketch, out_sketch, held, acts2, grads2 = (
        pltpu.with_memory_space_constraint(x, pltpu.HBM)
        for x in (adapter, rank_sketch.T, out_sketch, held, acts2, grads2)
    )
    down_like = jax.ShapeDtypeStruct((width, 2 * rank_sketch.shape[0]), jnp.bfloat16)
    square_like = jax.ShapeDtypeStruct((held.shape[0], 1), jnp.float32)
    inward = [(0, 1), (3, 2)]
    far_pairs = [(1, 3), (2, 0)]
    near_pairs = [(1, 2), (2, 1), (0, 0), (3, 3)]
    is_middle = middle.astype(jnp.int32).reshape(1)

    def onward(raw, got):
        return small(onward_kernel, raw.shape, is_middle, [raw, got])

    *raw0, down, own_square = project(
        first_kernel, me_feat, 0, 2, acts2, grads2, [adapter, rank_sketch, out_sketch, held], [down_like, square_like]
    )
    squares = [own_square] + [swap(own_square, "feat", mask) for mask in (1, 2, 3)]
    got1 = [lax.ppermute(x, "feat", inward) for x in raw0]
    raw1 = project(more_kernel, me_feat, 2, 2, acts2, grads2, [down, out_sketch], [])

    squares[1:] = [after(x, raw1[0]) for x in squares[1:]]
    other, *parts = lang_parts(me_ex, held, squares, perm % LANGS, n_ex)
    other = swap(other, "ex", 1)
    parts = [x + other[i] for i, x in enumerate(parts)]
    sent1 = [onward(after(raw0[0], parts[0]), got1[0])]
    far = [lax.ppermute(sent1[0], "feat", far_pairs)]
    scattered = [swap(parts[i], "ex", 2 * i) for i in range(1, n_ex // 2)]
    lang = after(parts[0], sent1[0]) + sum(scattered)
    other = swap(lang, "feat", 1)
    raw1 = [after(x, lang) for x in raw1]
    got2 = [lax.ppermute(raw1[0], "feat", inward)]
    sent1.append(onward(after(raw0[1], lang), got1[1]))
    far.append(lax.ppermute(sent1[1], "feat", far_pairs))
    got2.append(lax.ppermute(after(raw1[1], sent1[1]), "feat", inward))
    pair = small(stack_kernel, (2, *lang.shape), is_middle, [after(lang, sent1[1]), other])
    far_pair = [lax.ppermute(pair, "feat", pairs) for pairs in (near_pairs, far_pairs)]
    near_langs = [pair] + [swap(pair, "ex", mask) for mask in range(2, n_ex, 2)]
    *raw2, own_a, own_b = project(
        more_kernel, me_feat, 4, 4, acts2, grads2, [after(down, pair), out_sketch], []
    )
    got3 = [swap(x, "feat", 1) for x in raw2]
    sent2 = [onward(after(raw1[0], own_a), got2[0])]
    near = [lax.ppermute(sent2[0], "feat", near_pairs)]
    far_pair = [after(x, sent2[0]) for x in far_pair]
    pair = small(choose_kernel, pair.shape, is_middle, far_pair)
    far_langs = [pair] + [swap(pair, "ex", mask) for mask in range(2, n_ex, 2)]
    sent2.append(onward(after(raw1[1], pair), got2[1]))
    near.append(lax.ppermute(sent2[1], "feat", near_pairs))
    near_langs[1:] = [after(x, sent2[1]) for x in near_langs[1:]]
    near_langs = near_langs + [swap(x, "ex", 1) for x in near_langs]
    grad_a, square_a = product(is_middle, [after(own_a, sent2[1]), got3[0], far[0], near[0]])
    far_langs[1:] = [after(x, square_a) for x in far_langs[1:]]
    far_langs = far_langs + [swap(x, "ex", 1) for x in far_langs]
    grad_b, square_b = product(is_middle, [after(own_b, square_a), got3[1], far[1], near[1]])
    langs = near_langs + far_langs
    products = [(grad_a, square_a), (grad_b, square_b)]
    per_lang = perm.shape[0] * n_ex // LANGS
    scale = (KF * per_lang) ** 0.5 / per_lang
    mine = score(me_feat, me_ex, langs, products, scale)
    return place(me_feat, [mine] + [swap(mine, "feat", mask) for mask in (1, 2, 3)])


def general(acts, grads, adapter, rank_sketch, out_sketch, held, perm):
    ex_dev = acts.shape[0]
    down = jnp.dot(adapter, rank_sketch, preferred_element_type=jnp.float32).astype(jnp.bfloat16)
    rank_part = jnp.einsum("esd,dr->esr", acts, down, preferred_element_type=jnp.float32)
    rank_side = lax.psum(rank_part, "feat")
    out_part = jnp.einsum("esd,dk->esk", grads, out_sketch, preferred_element_type=jnp.float32)
    out_side = lax.psum_scatter(out_part, "feat", scatter_dimension=2, tiled=True)
    grad = jnp.einsum("esk,esr->ekr", out_side, rank_side, precision=HIGHEST).reshape(ex_dev, -1)
    squares = lax.psum(jnp.sum(held * held, axis=1), "feat")
    unit = held * lax.rsqrt(squares + 1e-06)[:, None]
    onehot = ((perm % LANGS)[:, None] == jnp.arange(LANGS, dtype=jnp.int32)[None, :]).astype(jnp.float32)
    per_lang = perm.shape[0] * lax.axis_size("ex") // LANGS
    lang_mean = lax.psum(jnp.dot(onehot.T, unit, precision=HIGHEST), "ex") / per_lang
    inner, norm = lax.psum(
        (jnp.dot(grad, lang_mean.T, precision=HIGHEST), jnp.sum(grad * grad, axis=1)), "feat"
    )
    scale = jnp.sqrt(jnp.float32(KF * per_lang))
    return scale * inner * lax.rsqrt(norm + 1e-06)[:, None]


def solution(mesh):
    placed = (
        P("ex", None, "feat"),
        P("ex", None, "feat"),
        P("feat", None),
        P(),
        P("feat", None),
        P("ex", "feat"),
        P("ex"),
    )
    is_fast = mesh.shape["feat"] == 4 and mesh.shape["ex"] == 8
    body = fast if is_fast else general
    return jax.shard_map(body, mesh=mesh, in_specs=placed, out_specs=P("ex", None), check_vma=False)
```

```python
import functools

import jax
import jax.numpy as jnp
from jax import lax
from jax.experimental import pallas as pl
from jax.experimental.pallas import tpu as pltpu
from jax.sharding import PartitionSpec as P


KF = 8192
LANGS = 64
UNIT = 4
PIECE = 2
PIECES = 8
HIGHEST = lax.Precision.HIGHEST
SMALL = 24 * 1024 * 1024
VMEM = pl.BlockSpec(memory_space=pltpu.VMEM)
SMEM = pl.BlockSpec(memory_space=pltpu.SMEM)


def project_piece(act, grad, down, sketch, o_ref):
    rows = act.shape[0] // PIECE
    half = rows // 2
    out = jnp.dot(grad, sketch, preferred_element_type=jnp.float32)
    rank = jnp.dot(act, down, preferred_element_type=jnp.float32)
    low = lax.broadcasted_iota(jnp.int32, (half, down.shape[1]), 1) < down.shape[1] // 2
    for unit in range(PIECE):
        start = unit * rows
        o_ref[unit, :rows, :] = out[start : start + rows]
        o_ref[unit, rows:, :] = jnp.where(low, rank[start : start + half], rank[start + half : start + rows])


def first_kernel(feat, act_ref, grad_ref, adapter_ref, rank_ref, sketch_ref, held_ref, *o_refs):
    del feat
    *piece_refs, down_ref, square_ref = o_refs
    step = pl.program_id(0)

    @pl.when(step == 0)
    def _():
        down = lax.dot_general(
            adapter_ref[...], rank_ref[...], (((1,), (1,)), ((), ())), preferred_element_type=jnp.float32
        )
        down_ref[...] = jnp.concatenate([down, down], axis=1).astype(jnp.bfloat16)
        held = held_ref[...]
        square_ref[...] = jnp.sum(held * held, axis=1, keepdims=True)

    for index, ref in enumerate(piece_refs):

        @pl.when(step == index)
        def _(ref=ref):
            project_piece(act_ref[...], grad_ref[...], down_ref[...], sketch_ref[...], ref)


def more_kernel(feat, act_ref, grad_ref, down_ref, sketch_ref, *piece_refs):
    del feat
    step = pl.program_id(0)
    for index, ref in enumerate(piece_refs):

        @pl.when(step == index)
        def _(ref=ref):
            project_piece(act_ref[...], grad_ref[...], down_ref[...], sketch_ref[...], ref)


def whole(shape):
    return pl.BlockSpec(shape, lambda i, feat: (0,) * len(shape))


def chunk_of(turn, feat):
    left = feat < 2
    far, near = jnp.where(left, 3, 0), jnp.where(left, 2, 1)
    return jnp.where(turn == 0, far, jnp.where(turn == 1, near, jnp.where(turn == 2, feat ^ 1, feat)))


def project(kernel, feat, first, count, acts, grads, operands, extra):
    ko = operands[-1 if kernel is more_kernel else 2].shape[1]
    width = acts.shape[1]
    rows = acts.shape[0] // PIECES
    piece = (PIECE, rows // PIECE * 3 // 2, ko)
    block = pl.BlockSpec((rows, width), lambda i, feat: (chunk_of((first + i) // 2, feat[0]) * 2 + (first + i) % 2, 0))
    return pl.pallas_call(
        kernel,
        out_shape=[jax.ShapeDtypeStruct(piece, jnp.float32)] * count + extra,
        grid_spec=pltpu.PrefetchScalarGridSpec(
            num_scalar_prefetch=1,
            grid=(count,),
            in_specs=[block, block] + [whole(x.shape) for x in operands],
            out_specs=[whole(piece)] * count + [whole(x.shape) for x in extra],
        ),
        cost_estimate=pl.CostEstimate(
            flops=count * rows * width * ko * 4,
            bytes_accessed=count * rows * (width * 4 + ko * 6),
            transcendentals=0,
        ),
        compiler_params=pltpu.CompilerParams(vmem_limit_bytes=SMALL),
        name="project",
    )(feat, acts, grads, *operands)


def lang_kernel(me_ref, held_ref, lang_ref, *refs):
    *square_refs, other_ref = refs[:5]
    own_refs = refs[5:]
    count = len(own_refs)
    rows, width = held_ref.shape
    piece = width // (2 * count)
    hit = lang_ref[...] == lax.broadcasted_iota(jnp.int32, (LANGS, rows), 0)
    hit = jnp.where(hit, 1.0, 0.0)
    inverse = lax.rsqrt(sum(ref[...] for ref in square_refs) + 1e-06)

    def sums(part):
        columns = pl.ds(pl.multiple_of(part * piece, piece), piece)
        return jnp.dot(
            hit, held_ref[:, columns] * inverse, precision=HIGHEST, preferred_element_type=jnp.float32
        )

    for index in range(count):
        other_ref[index] = sums(me_ref[0] ^ 1 ^ (2 * index))
        own_refs[index][...] = sums(me_ref[0] ^ (2 * index))


def lang_parts(me, held, squares, lang, n_ex):
    rows, width = held.shape
    piece = width // n_ex
    half = n_ex // 2
    return pl.pallas_call(
        lang_kernel,
        out_shape=[jax.ShapeDtypeStruct((half, LANGS, piece), jnp.float32)]
        + [jax.ShapeDtypeStruct((LANGS, piece), jnp.float32)] * half,
        in_specs=[SMEM] + [VMEM] * 6,
        out_specs=[VMEM] * (1 + half),
        compiler_params=pltpu.CompilerParams(vmem_limit_bytes=SMALL),
        name="lang_parts",
    )(me, held, lang.reshape(1, rows), *squares)


def product_kernel(middle_ref, own_ref, raw_ref, far_ref, near_ref, o_ref, square_ref, grad_ref):
    middle = middle_ref[0] == 1
    rows = own_ref.shape[1] * 2 // 3
    seq = rows // UNIT
    wide = own_ref.shape[2]
    low = lax.broadcasted_iota(jnp.int32, (seq, wide), 1) < wide // 2

    def split(x, order):
        high = x.astype(jnp.bfloat16)
        rest = (x - high.astype(jnp.float32)).astype(jnp.bfloat16)
        return jnp.concatenate([high, rest, high] if order else [high, high, rest], axis=0)

    def total(unit, start):
        block = (unit, pl.ds(start, seq), slice(None))
        return own_ref[block] + raw_ref[block] + jnp.where(middle, near_ref[block], far_ref[block])

    for unit in range(PIECE):
        for pair in range(UNIT // 2):
            both = total(unit, rows + pair * seq)
            turned = pltpu.roll(both, wide // 2, 1)
            for side in range(2):
                example = pair + side * (UNIT // 2)
                rank = jnp.where(low, turned, both) if side else jnp.where(low, both, turned)
                grad_ref[unit * UNIT + example] = lax.dot_general(
                    split(total(unit, example * seq), True),
                    split(rank, False),
                    (((0,), (0,)), ((), ())),
                    preferred_element_type=jnp.float32,
                )
    count = PIECE * UNIT
    low = lax.broadcasted_iota(jnp.int32, (count, wide), 1) < wide // 2
    square = jnp.zeros((count, 2 * wide), jnp.float32)
    for index in range(o_ref.shape[0]):
        rows_of = [grad_ref[:, 4 * index + j, :] for j in range(4)]
        part = jnp.concatenate(
            [jnp.where(low, rows_of[0], rows_of[1]), jnp.where(low, rows_of[2], rows_of[3])], axis=1
        )
        square += part * part
        rest = part - part.astype(jnp.bfloat16).astype(jnp.float32)
        o_ref[index] = jnp.concatenate([part, rest], axis=0).astype(jnp.bfloat16)
    square_ref[...] = jnp.sum(square, axis=1, keepdims=True)


def product(middle, parts):
    count, wide = PIECE * UNIT, parts[0].shape[2]
    return pl.pallas_call(
        product_kernel,
        out_shape=[
            jax.ShapeDtypeStruct((wide // 4, 2 * count, 2 * wide), jnp.bfloat16),
            jax.ShapeDtypeStruct((count, 1), jnp.float32),
        ],
        in_specs=[SMEM] + [VMEM] * len(parts),
        out_specs=[VMEM] * 2,
        scratch_shapes=[pltpu.VMEM((count, wide, wide), jnp.float32)],
        compiler_params=pltpu.CompilerParams(vmem_limit_bytes=SMALL),
        name="product",
    )(middle, *parts)


def score_kernel(feat_ref, ex_ref, *refs, scale, n_lang):
    lang_refs, grad_refs, square_refs, o_ref = refs[:n_lang], refs[n_lang:-1:2], refs[n_lang + 1 : -1 : 2], refs[-1]
    total = None
    feat, ex = feat_ref[0], ex_ref[0]
    middle = (feat == 1) | (feat == 2)
    second = feat ^ jnp.where(middle, 3, 2)
    rows_from = [feat, feat ^ 1, second, second ^ 1]
    masks = [*range(0, n_lang, 2), *range(1, n_lang, 2)]
    for j, ref in enumerate(lang_refs):
        for m in range(4):
            index = rows_from[m] * n_lang + (ex ^ masks[j])
            lang = ref[m]
            rest = lang - lang.astype(jnp.bfloat16).astype(jnp.float32)
            lang = jnp.concatenate([lang, rest], axis=0).astype(jnp.bfloat16)
            grad = jnp.concatenate([g[index] for g in grad_refs], axis=0)
            term = lax.dot_general(
                grad, lang, (((1,), (1,)), ((), ())), preferred_element_type=jnp.float32
            )
            total = term if total is None else total + term
    total = total + pltpu.roll(total, LANGS, 1)
    count = square_refs[0].shape[0]
    for index, square_ref in enumerate(square_refs):
        start = 2 * count * index
        inner = total[start : start + count, :LANGS] + total[start + count : start + 2 * count, :LANGS]
        o_ref[index * count : (index + 1) * count] = inner * (lax.rsqrt(square_ref[...] + 1e-06) * scale)


def score(feat, ex, langs, products, scale):
    flat = [x for pair in products for x in pair]
    mine = sum(square.shape[0] for _, square in products)
    return pl.pallas_call(
        functools.partial(score_kernel, scale=scale, n_lang=len(langs)),
        out_shape=jax.ShapeDtypeStruct((mine, LANGS), jnp.float32),
        in_specs=[SMEM] * 2 + [VMEM] * (len(langs) + len(flat)),
        out_specs=VMEM,
        compiler_params=pltpu.CompilerParams(vmem_limit_bytes=SMALL),
        name="score",
    )(feat, ex, *langs, *flat)


def small(kernel, shape, middle, operands):
    return pl.pallas_call(
        kernel,
        out_shape=jax.ShapeDtypeStruct(shape, jnp.float32),
        in_specs=[SMEM] + [VMEM] * len(operands),
        out_specs=VMEM,
        compiler_params=pltpu.CompilerParams(vmem_limit_bytes=SMALL),
    )(middle, *operands)


def onward_kernel(middle_ref, raw_ref, got_ref, o_ref):
    o_ref[...] = raw_ref[...] + jnp.where(middle_ref[0] == 1, got_ref[...], 0.0)


def stack_kernel(middle_ref, one_ref, two_ref, o_ref):
    del middle_ref
    o_ref[0] = one_ref[...]
    o_ref[1] = two_ref[...]


def route_kernel(middle_ref, raw_ref, got_ref, end_ref, o_ref):
    o_ref[...] = jnp.where(middle_ref[0] == 1, raw_ref[...] + got_ref[...], end_ref[...])


def join_kernel(middle_ref, pair_ref, inner_ref, outer_ref, o_ref):
    o_ref[:2] = pair_ref[...]
    o_ref[2:] = jnp.where(middle_ref[0] == 1, inner_ref[...], outer_ref[...])


def place_kernel(me_ref, *refs):
    *parts, o_ref = refs
    rows = parts[0].shape[0]
    for mask, ref in enumerate(parts):
        o_ref[pl.ds(pl.multiple_of((me_ref[0] ^ mask) * rows, rows), rows), :] = ref[...]


def place(me, parts):
    rows, columns = parts[0].shape
    return pl.pallas_call(
        place_kernel,
        out_shape=jax.ShapeDtypeStruct((rows * len(parts), columns), jnp.float32),
        in_specs=[SMEM] + [VMEM] * len(parts),
        out_specs=VMEM,
        compiler_params=pltpu.CompilerParams(vmem_limit_bytes=SMALL),
        name="place",
    )(me, *parts)


def swap(x, axis, mask):
    return lax.ppermute(x, axis, [(i, i ^ mask) for i in range(lax.axis_size(axis))])


def after(x, *others):
    return lax.optimization_barrier((x, *others))[0]


def fast(*args):
    return ordered(*args)


def ordered(acts, grads, adapter, rank_sketch, out_sketch, held, perm):
    feat, ex = lax.axis_index("feat"), lax.axis_index("ex")
    n_ex = lax.axis_size("ex")
    _, _, width = acts.shape
    middle = (feat == 1) | (feat == 2)
    me_ex = ex.astype(jnp.int32).reshape(1)
    me_feat = feat.astype(jnp.int32).reshape(1)
    acts2, grads2 = acts.reshape(-1, width), grads.reshape(-1, width)
    adapter, rank_sketch, out_sketch, held, acts2, grads2 = (
        pltpu.with_memory_space_constraint(x, pltpu.HBM)
        for x in (adapter, rank_sketch.T, out_sketch, held, acts2, grads2)
    )
    down_like = jax.ShapeDtypeStruct((width, 2 * rank_sketch.shape[0]), jnp.bfloat16)
    square_like = jax.ShapeDtypeStruct((held.shape[0], 1), jnp.float32)
    inward = [(0, 1), (3, 2)]
    far_pairs = [(1, 3), (2, 0)]
    round_pairs = inward + far_pairs
    near_pairs = [(1, 2), (2, 1), (0, 0), (3, 3)]
    is_middle = middle.astype(jnp.int32).reshape(1)

    def onward(raw, got):
        return small(onward_kernel, raw.shape, is_middle, [raw, got])

    *raw0, down, own_square = project(
        first_kernel, me_feat, 0, 2, acts2, grads2, [adapter, rank_sketch, out_sketch, held], [down_like, square_like]
    )
    squares = [own_square] + [swap(own_square, "feat", mask) for mask in (1, 2, 3)]
    got1 = [lax.ppermute(x, "feat", inward) for x in raw0]
    raw1 = project(more_kernel, me_feat, 2, 2, acts2, grads2, [down, out_sketch], [])

    squares[1:] = [after(x, raw1[0]) for x in squares[1:]]
    other, *parts = lang_parts(me_ex, held, squares, perm % LANGS, n_ex)
    other = swap(other, "ex", 1)
    parts = [x + other[i] for i, x in enumerate(parts)]
    sent1 = [onward(after(raw0[0], parts[0]), got1[0])]
    far = [lax.ppermute(sent1[0], "feat", far_pairs)]
    scattered = [swap(parts[i], "ex", 2 * i) for i in range(1, n_ex // 2)]
    lang = after(parts[0], sent1[0]) + sum(scattered)
    other = swap(lang, "feat", 1)
    raw1 = [after(x, lang) for x in raw1]
    sent1.append(small(route_kernel, raw1[0].shape, is_middle, [raw0[1], got1[1], after(raw1[0], other)]))
    round_a = lax.ppermute(sent1[1], "feat", round_pairs)
    pair = small(stack_kernel, (2, *lang.shape), is_middle, [after(lang, sent1[1]), other])
    far_pair = [lax.ppermute(pair, "feat", pairs) for pairs in (near_pairs, far_pairs)]
    got2 = [round_a, lax.ppermute(after(raw1[1], pair), "feat", inward)]
    *raw2, own_a, own_b = project(
        more_kernel, me_feat, 4, 4, acts2, grads2, [after(down, pair), out_sketch], []
    )
    got3 = [swap(raw2[0], "feat", 1)]
    sent2 = [onward(after(raw1[0], own_a), got2[0])]
    near = [lax.ppermute(sent2[0], "feat", near_pairs)]
    langs = [small(join_kernel, (4, *lang.shape), is_middle, [after(pair, sent2[0]), *far_pair])]
    langs = langs + [swap(langs[0], "ex", mask) for mask in range(2, n_ex, 2)]
    got3.append(swap(after(raw2[1], sent2[0]), "feat", 1))
    sent2.append(onward(after(raw1[1], langs[0]), got2[1]))
    near.append(lax.ppermute(sent2[1], "feat", near_pairs))
    grad_a, square_a = product(is_middle, [after(own_a, sent2[1]), got3[0], far[0], near[0]])
    langs[1:] = [after(x, square_a) for x in langs[1:]]
    langs = langs + [swap(x, "ex", 1) for x in langs]
    grad_b, square_b = product(is_middle, [after(own_b, square_a), got3[1], round_a, near[1]])
    products = [(grad_a, square_a), (grad_b, square_b)]
    per_lang = perm.shape[0] * n_ex // LANGS
    scale = (KF * per_lang) ** 0.5 / per_lang
    mine = score(me_feat, me_ex, langs, products, scale)
    return place(me_feat, [mine] + [swap(mine, "feat", mask) for mask in (1, 2, 3)])


def general(acts, grads, adapter, rank_sketch, out_sketch, held, perm):
    ex_dev = acts.shape[0]
    down = jnp.dot(adapter, rank_sketch, preferred_element_type=jnp.float32).astype(jnp.bfloat16)
    rank_part = jnp.einsum("esd,dr->esr", acts, down, preferred_element_type=jnp.float32)
    rank_side = lax.psum(rank_part, "feat")
    out_part = jnp.einsum("esd,dk->esk", grads, out_sketch, preferred_element_type=jnp.float32)
    out_side = lax.psum_scatter(out_part, "feat", scatter_dimension=2, tiled=True)
    grad = jnp.einsum("esk,esr->ekr", out_side, rank_side, precision=HIGHEST).reshape(ex_dev, -1)
    squares = lax.psum(jnp.sum(held * held, axis=1), "feat")
    unit = held * lax.rsqrt(squares + 1e-06)[:, None]
    onehot = ((perm % LANGS)[:, None] == jnp.arange(LANGS, dtype=jnp.int32)[None, :]).astype(jnp.float32)
    per_lang = perm.shape[0] * lax.axis_size("ex") // LANGS
    lang_mean = lax.psum(jnp.dot(onehot.T, unit, precision=HIGHEST), "ex") / per_lang
    inner, norm = lax.psum(
        (jnp.dot(grad, lang_mean.T, precision=HIGHEST), jnp.sum(grad * grad, axis=1)), "feat"
    )
    scale = jnp.sqrt(jnp.float32(KF * per_lang))
    return scale * inner * lax.rsqrt(norm + 1e-06)[:, None]


def solution(mesh):
    placed = (
        P("ex", None, "feat"),
        P("ex", None, "feat"),
        P("feat", None),
        P(),
        P("feat", None),
        P("ex", "feat"),
        P("ex"),
    )
    is_fast = mesh.shape["feat"] == 4 and mesh.shape["ex"] == 8
    body = fast if is_fast else general
    return jax.shard_map(body, mesh=mesh, in_specs=placed, out_specs=P("ex", None), check_vma=False)
```

```python
import functools

import jax
import jax.numpy as jnp
from jax import lax
from jax.experimental import pallas as pl
from jax.experimental.pallas import tpu as pltpu
from jax.sharding import PartitionSpec as P


KF = 8192
LANGS = 64
UNIT = 4
PIECE = 2
PIECES = 8
HIGHEST = lax.Precision.HIGHEST
SMALL = 24 * 1024 * 1024
VMEM = pl.BlockSpec(memory_space=pltpu.VMEM)
SMEM = pl.BlockSpec(memory_space=pltpu.SMEM)


def project_piece(act, grad, down, sketch, o_ref):
    rows = act.shape[0] // PIECE
    half = rows // 2
    out = jnp.dot(grad, sketch, preferred_element_type=jnp.float32)
    rank = jnp.dot(act, down, preferred_element_type=jnp.float32)
    low = lax.broadcasted_iota(jnp.int32, (half, down.shape[1]), 1) < down.shape[1] // 2
    for unit in range(PIECE):
        start = unit * rows
        o_ref[unit, :rows, :] = out[start : start + rows]
        o_ref[unit, rows:, :] = jnp.where(low, rank[start : start + half], rank[start + half : start + rows])


def first_kernel(feat, act_ref, grad_ref, adapter_ref, rank_ref, sketch_ref, held_ref, *o_refs):
    del feat
    *piece_refs, down_ref, square_ref = o_refs
    step = pl.program_id(0)

    @pl.when(step == 0)
    def _():
        down = lax.dot_general(
            adapter_ref[...], rank_ref[...], (((1,), (1,)), ((), ())), preferred_element_type=jnp.float32
        )
        down_ref[...] = jnp.concatenate([down, down], axis=1).astype(jnp.bfloat16)
        held = held_ref[...]
        square_ref[...] = jnp.sum(held * held, axis=1, keepdims=True)

    for index, ref in enumerate(piece_refs):

        @pl.when(step == index)
        def _(ref=ref):
            project_piece(act_ref[...], grad_ref[...], down_ref[...], sketch_ref[...], ref)


def more_kernel(feat, act_ref, grad_ref, down_ref, sketch_ref, *piece_refs):
    del feat
    step = pl.program_id(0)
    for index, ref in enumerate(piece_refs):

        @pl.when(step == index)
        def _(ref=ref):
            project_piece(act_ref[...], grad_ref[...], down_ref[...], sketch_ref[...], ref)


def whole(shape):
    return pl.BlockSpec(shape, lambda i, feat: (0,) * len(shape))


def chunk_of(turn, feat):
    left = feat < 2
    far, near = jnp.where(left, 3, 0), jnp.where(left, 2, 1)
    return jnp.where(turn == 0, far, jnp.where(turn == 1, near, jnp.where(turn == 2, feat ^ 1, feat)))


def project(kernel, feat, first, count, acts, grads, operands, extra):
    ko = operands[-1 if kernel is more_kernel else 2].shape[1]
    width = acts.shape[1]
    rows = acts.shape[0] // PIECES
    piece = (PIECE, rows // PIECE * 3 // 2, ko)
    block = pl.BlockSpec((rows, width), lambda i, feat: (chunk_of((first + i) // 2, feat[0]) * 2 + (first + i) % 2, 0))
    return pl.pallas_call(
        kernel,
        out_shape=[jax.ShapeDtypeStruct(piece, jnp.float32)] * count + extra,
        grid_spec=pltpu.PrefetchScalarGridSpec(
            num_scalar_prefetch=1,
            grid=(count,),
            in_specs=[block, block] + [whole(x.shape) for x in operands],
            out_specs=[whole(piece)] * count + [whole(x.shape) for x in extra],
        ),
        cost_estimate=pl.CostEstimate(
            flops=count * rows * width * ko * 4,
            bytes_accessed=count * rows * (width * 4 + ko * 6),
            transcendentals=0,
        ),
        compiler_params=pltpu.CompilerParams(vmem_limit_bytes=SMALL),
        name="project",
    )(feat, acts, grads, *operands)


def lang_kernel(me_ref, held_ref, lang_ref, *refs):
    *square_refs, other_ref = refs[:5]
    own_refs = refs[5:]
    count = len(own_refs)
    rows, width = held_ref.shape
    piece = width // (2 * count)
    hit = lang_ref[...] == lax.broadcasted_iota(jnp.int32, (LANGS, rows), 0)
    hit = jnp.where(hit, 1.0, 0.0)
    inverse = lax.rsqrt(sum(ref[...] for ref in square_refs) + 1e-06)

    def sums(part):
        columns = pl.ds(pl.multiple_of(part * piece, piece), piece)
        return jnp.dot(
            hit, held_ref[:, columns] * inverse, precision=HIGHEST, preferred_element_type=jnp.float32
        )

    for index in range(count):
        other_ref[index] = sums(me_ref[0] ^ 1 ^ (2 * index))
        own_refs[index][...] = sums(me_ref[0] ^ (2 * index))


def lang_parts(me, held, squares, lang, n_ex):
    rows, width = held.shape
    piece = width // n_ex
    half = n_ex // 2
    return pl.pallas_call(
        lang_kernel,
        out_shape=[jax.ShapeDtypeStruct((half, LANGS, piece), jnp.float32)]
        + [jax.ShapeDtypeStruct((LANGS, piece), jnp.float32)] * half,
        in_specs=[SMEM] + [VMEM] * 6,
        out_specs=[VMEM] * (1 + half),
        compiler_params=pltpu.CompilerParams(vmem_limit_bytes=SMALL),
        name="lang_parts",
    )(me, held, lang.reshape(1, rows), *squares)


def product_kernel(middle_ref, own_ref, end_ref, near_ref, o_ref, square_ref, grad_ref):
    middle = middle_ref[0] == 1
    rows = own_ref.shape[1] * 2 // 3
    seq = rows // UNIT
    wide = own_ref.shape[2]
    low = lax.broadcasted_iota(jnp.int32, (seq, wide), 1) < wide // 2

    def split(x, order):
        high = x.astype(jnp.bfloat16)
        rest = (x - high.astype(jnp.float32)).astype(jnp.bfloat16)
        return jnp.concatenate([high, rest, high] if order else [high, high, rest], axis=0)

    def total(unit, start):
        block = (unit, pl.ds(start, seq), slice(None))
        return own_ref[block] + end_ref[block] + jnp.where(middle, near_ref[block], 0.0)

    for unit in range(PIECE):
        for pair in range(UNIT // 2):
            both = total(unit, rows + pair * seq)
            turned = pltpu.roll(both, wide // 2, 1)
            for side in range(2):
                example = pair + side * (UNIT // 2)
                rank = jnp.where(low, turned, both) if side else jnp.where(low, both, turned)
                grad_ref[unit * UNIT + example] = lax.dot_general(
                    split(total(unit, example * seq), True),
                    split(rank, False),
                    (((0,), (0,)), ((), ())),
                    preferred_element_type=jnp.float32,
                )
    count = PIECE * UNIT
    low = lax.broadcasted_iota(jnp.int32, (count, wide), 1) < wide // 2
    square = jnp.zeros((count, 2 * wide), jnp.float32)
    for index in range(o_ref.shape[0]):
        rows_of = [grad_ref[:, 4 * index + j, :] for j in range(4)]
        part = jnp.concatenate(
            [jnp.where(low, rows_of[0], rows_of[1]), jnp.where(low, rows_of[2], rows_of[3])], axis=1
        )
        square += part * part
        rest = part - part.astype(jnp.bfloat16).astype(jnp.float32)
        o_ref[index] = jnp.concatenate([part, rest], axis=0).astype(jnp.bfloat16)
    square_ref[...] = jnp.sum(square, axis=1, keepdims=True)


def product(middle, parts):
    count, wide = PIECE * UNIT, parts[0].shape[2]
    return pl.pallas_call(
        product_kernel,
        out_shape=[
            jax.ShapeDtypeStruct((wide // 4, 2 * count, 2 * wide), jnp.bfloat16),
            jax.ShapeDtypeStruct((count, 1), jnp.float32),
        ],
        in_specs=[SMEM] + [VMEM] * len(parts),
        out_specs=[VMEM] * 2,
        scratch_shapes=[pltpu.VMEM((count, wide, wide), jnp.float32)],
        compiler_params=pltpu.CompilerParams(vmem_limit_bytes=SMALL),
        name="product",
    )(middle, *parts)


def score_kernel(feat_ref, ex_ref, *refs, scale, n_lang):
    lang_refs, grad_refs, square_refs, o_ref = refs[:n_lang], refs[n_lang:-1:2], refs[n_lang + 1 : -1 : 2], refs[-1]
    total = None
    feat, ex = feat_ref[0], ex_ref[0]
    middle = (feat == 1) | (feat == 2)
    second = feat ^ jnp.where(middle, 3, 2)
    rows_from = [feat, feat ^ 1, second, second ^ 1]
    masks = [*range(0, n_lang, 2), *range(1, n_lang, 2)]
    for j, ref in enumerate(lang_refs):
        for m in range(4):
            index = rows_from[m] * n_lang + (ex ^ masks[j])
            lang = ref[m]
            rest = lang - lang.astype(jnp.bfloat16).astype(jnp.float32)
            lang = jnp.concatenate([lang, rest], axis=0).astype(jnp.bfloat16)
            grad = jnp.concatenate([g[index] for g in grad_refs], axis=0)
            term = lax.dot_general(
                grad, lang, (((1,), (1,)), ((), ())), preferred_element_type=jnp.float32
            )
            total = term if total is None else total + term
    total = total + pltpu.roll(total, LANGS, 1)
    count = square_refs[0].shape[0]
    for index, square_ref in enumerate(square_refs):
        start = 2 * count * index
        inner = total[start : start + count, :LANGS] + total[start + count : start + 2 * count, :LANGS]
        o_ref[index * count : (index + 1) * count] = inner * (lax.rsqrt(square_ref[...] + 1e-06) * scale)


def score(feat, ex, langs, products, scale):
    flat = [x for pair in products for x in pair]
    mine = sum(square.shape[0] for _, square in products)
    return pl.pallas_call(
        functools.partial(score_kernel, scale=scale, n_lang=len(langs)),
        out_shape=jax.ShapeDtypeStruct((mine, LANGS), jnp.float32),
        in_specs=[SMEM] * 2 + [VMEM] * (len(langs) + len(flat)),
        out_specs=VMEM,
        compiler_params=pltpu.CompilerParams(vmem_limit_bytes=SMALL),
        name="score",
    )(feat, ex, *langs, *flat)


def small(kernel, shape, middle, operands):
    return pl.pallas_call(
        kernel,
        out_shape=jax.ShapeDtypeStruct(shape, jnp.float32),
        in_specs=[SMEM] + [VMEM] * len(operands),
        out_specs=VMEM,
        compiler_params=pltpu.CompilerParams(vmem_limit_bytes=SMALL),
    )(middle, *operands)


def onward_kernel(middle_ref, raw_ref, got_ref, o_ref):
    o_ref[...] = raw_ref[...] + jnp.where(middle_ref[0] == 1, got_ref[...], 0.0)


def stack_kernel(middle_ref, one_ref, two_ref, o_ref):
    del middle_ref
    o_ref[0] = one_ref[...]
    o_ref[1] = two_ref[...]


def join_kernel(middle_ref, pair_ref, inner_ref, outer_ref, o_ref):
    o_ref[:2] = pair_ref[...]
    o_ref[2:] = jnp.where(middle_ref[0] == 1, inner_ref[...], outer_ref[...])


def place_kernel(me_ref, *refs):
    *parts, o_ref = refs
    rows = parts[0].shape[0]
    for mask, ref in enumerate(parts):
        o_ref[pl.ds(pl.multiple_of((me_ref[0] ^ mask) * rows, rows), rows), :] = ref[...]


def place(me, parts):
    rows, columns = parts[0].shape
    return pl.pallas_call(
        place_kernel,
        out_shape=jax.ShapeDtypeStruct((rows * len(parts), columns), jnp.float32),
        in_specs=[SMEM] + [VMEM] * len(parts),
        out_specs=VMEM,
        compiler_params=pltpu.CompilerParams(vmem_limit_bytes=SMALL),
        name="place",
    )(me, *parts)


def swap(x, axis, mask):
    return lax.ppermute(x, axis, [(i, i ^ mask) for i in range(lax.axis_size(axis))])


def after(x, *others):
    return lax.optimization_barrier((x, *others))[0]


def fast(*args):
    return ordered(*args)


def ordered(acts, grads, adapter, rank_sketch, out_sketch, held, perm):
    feat, ex = lax.axis_index("feat"), lax.axis_index("ex")
    n_ex = lax.axis_size("ex")
    _, _, width = acts.shape
    middle = (feat == 1) | (feat == 2)
    me_ex = ex.astype(jnp.int32).reshape(1)
    me_feat = feat.astype(jnp.int32).reshape(1)
    acts2, grads2 = acts.reshape(-1, width), grads.reshape(-1, width)
    adapter, rank_sketch, out_sketch, held, acts2, grads2 = (
        pltpu.with_memory_space_constraint(x, pltpu.HBM)
        for x in (adapter, rank_sketch.T, out_sketch, held, acts2, grads2)
    )
    down_like = jax.ShapeDtypeStruct((width, 2 * rank_sketch.shape[0]), jnp.bfloat16)
    square_like = jax.ShapeDtypeStruct((held.shape[0], 1), jnp.float32)
    inward = [(0, 1), (3, 2)]
    outward = [(1, 0), (2, 3)]
    inner = [(1, 2), (2, 1), (0, 0), (3, 3)]
    is_middle = middle.astype(jnp.int32).reshape(1)

    def onward(raw, got):
        return small(onward_kernel, raw.shape, is_middle, [raw, got])

    *raw0, down, own_square = project(
        first_kernel, me_feat, 0, 2, acts2, grads2, [adapter, rank_sketch, out_sketch, held], [down_like, square_like]
    )
    squares = [own_square] + [swap(own_square, "feat", mask) for mask in (1, 2, 3)]
    got1 = [swap(x, "feat", 1) for x in raw0]
    raw1 = project(more_kernel, me_feat, 2, 2, acts2, grads2, [down, out_sketch], [])

    squares[1:] = [after(x, raw1[0]) for x in squares[1:]]
    other, *parts = lang_parts(me_ex, held, squares, perm % LANGS, n_ex)
    other = swap(other, "ex", 1)
    parts = [x + other[i] for i, x in enumerate(parts)]
    scattered = [swap(parts[i], "ex", 2 * i) for i in range(1, n_ex // 2)]
    sent1 = [onward(after(raw0[0], parts[0]), got1[0])]
    far = [lax.ppermute(sent1[0], "feat", inner)]
    lang = after(parts[0], sent1[0]) + sum(scattered)
    other = swap(lang, "feat", 1)
    raw1 = [after(x, lang) for x in raw1]
    got2 = [swap(raw1[0], "feat", 1)]
    pair = small(stack_kernel, (2, *lang.shape), is_middle, [lang, other])
    far_pair = lax.ppermute(pair, "feat", inner)
    sent1.append(onward(after(raw0[1], pair), got1[1]))
    far.append(lax.ppermute(sent1[1], "feat", inner))
    got2.append(lax.ppermute(after(raw1[1], pair), "feat", inward))
    far_pair = after(far_pair, sent1[1])
    outer_pair = lax.ppermute(far_pair, "feat", outward)
    *raw2, own_a, own_b = project(more_kernel, me_feat, 4, 4, acts2, grads2, [after(down, far_pair), out_sketch], [])
    sent2 = [onward(after(raw1[0], own_a), got2[0])]
    near = [lax.ppermute(sent2[0], "feat", inner)]
    sent3 = [onward(after(raw2[0], sent2[0]), far[0])]
    got3 = [swap(sent3[0], "feat", 1)]
    pair = after(pair, sent3[0])
    langs = [small(join_kernel, (4, *lang.shape), is_middle, [pair, far_pair, outer_pair])]
    langs = langs + [swap(langs[0], "ex", mask) for mask in range(2, n_ex, 2)]
    sent3.append(onward(after(raw2[1], langs[0]), far[1]))
    got3.append(swap(sent3[1], "feat", 1))
    sent2.append(onward(after(raw1[1], sent3[1]), got2[1]))
    near.append(lax.ppermute(sent2[1], "feat", inner))
    grad_a, square_a = product(is_middle, [after(own_a, sent2[1]), got3[0], near[0]])
    langs[1:] = [after(x, square_a) for x in langs[1:]]
    langs = langs + [swap(x, "ex", 1) for x in langs]
    grad_b, square_b = product(is_middle, [after(own_b, square_a), got3[1], near[1]])
    products = [(grad_a, square_a), (grad_b, square_b)]
    per_lang = perm.shape[0] * n_ex // LANGS
    scale = (KF * per_lang) ** 0.5 / per_lang
    mine = score(me_feat, me_ex, langs, products, scale)
    return place(me_feat, [mine] + [swap(mine, "feat", mask) for mask in (1, 2, 3)])


def general(acts, grads, adapter, rank_sketch, out_sketch, held, perm):
    ex_dev = acts.shape[0]
    down = jnp.dot(adapter, rank_sketch, preferred_element_type=jnp.float32).astype(jnp.bfloat16)
    rank_part = jnp.einsum("esd,dr->esr", acts, down, preferred_element_type=jnp.float32)
    rank_side = lax.psum(rank_part, "feat")
    out_part = jnp.einsum("esd,dk->esk", grads, out_sketch, preferred_element_type=jnp.float32)
    out_side = lax.psum_scatter(out_part, "feat", scatter_dimension=2, tiled=True)
    grad = jnp.einsum("esk,esr->ekr", out_side, rank_side, precision=HIGHEST).reshape(ex_dev, -1)
    squares = lax.psum(jnp.sum(held * held, axis=1), "feat")
    unit = held * lax.rsqrt(squares + 1e-06)[:, None]
    onehot = ((perm % LANGS)[:, None] == jnp.arange(LANGS, dtype=jnp.int32)[None, :]).astype(jnp.float32)
    per_lang = perm.shape[0] * lax.axis_size("ex") // LANGS
    lang_mean = lax.psum(jnp.dot(onehot.T, unit, precision=HIGHEST), "ex") / per_lang
    inner, norm = lax.psum(
        (jnp.dot(grad, lang_mean.T, precision=HIGHEST), jnp.sum(grad * grad, axis=1)), "feat"
    )
    scale = jnp.sqrt(jnp.float32(KF * per_lang))
    return scale * inner * lax.rsqrt(norm + 1e-06)[:, None]


def solution(mesh):
    placed = (
        P("ex", None, "feat"),
        P("ex", None, "feat"),
        P("feat", None),
        P(),
        P("feat", None),
        P("ex", "feat"),
        P("ex"),
    )
    is_fast = mesh.shape["feat"] == 4 and mesh.shape["ex"] == 8
    body = fast if is_fast else general
    return jax.shard_map(body, mesh=mesh, in_specs=placed, out_specs=P("ex", None), check_vma=False)
```

```python
import functools

import jax
import jax.numpy as jnp
from jax import lax
from jax.experimental import pallas as pl
from jax.experimental.pallas import tpu as pltpu
from jax.sharding import PartitionSpec as P


KF = 8192
LANGS = 64
UNIT = 4
PIECE = 2
PIECES = 8
HIGHEST = lax.Precision.HIGHEST
SMALL = 24 * 1024 * 1024
VMEM = pl.BlockSpec(memory_space=pltpu.VMEM)
SMEM = pl.BlockSpec(memory_space=pltpu.SMEM)


def project_piece(act, grad, down, sketch, o_ref):
    rows = act.shape[0] // PIECE
    half = rows // 2
    out = jnp.dot(grad, sketch, preferred_element_type=jnp.float32)
    rank = jnp.dot(act, down, preferred_element_type=jnp.float32)
    low = lax.broadcasted_iota(jnp.int32, (half, down.shape[1]), 1) < down.shape[1] // 2
    for unit in range(PIECE):
        start = unit * rows
        o_ref[unit, :rows, :] = out[start : start + rows]
        o_ref[unit, rows:, :] = jnp.where(low, rank[start : start + half], rank[start + half : start + rows])


def first_kernel(feat, act_ref, grad_ref, adapter_ref, rank_ref, sketch_ref, held_ref, *o_refs):
    del feat
    *piece_refs, down_ref, square_ref = o_refs
    step = pl.program_id(0)

    @pl.when(step == 0)
    def _():
        down = lax.dot_general(
            adapter_ref[...], rank_ref[...], (((1,), (1,)), ((), ())), preferred_element_type=jnp.float32
        )
        down_ref[...] = jnp.concatenate([down, down], axis=1).astype(jnp.bfloat16)
        held = held_ref[...]
        square_ref[...] = jnp.sum(held * held, axis=1, keepdims=True)

    for index, ref in enumerate(piece_refs):

        @pl.when(step == index)
        def _(ref=ref):
            project_piece(act_ref[...], grad_ref[...], down_ref[...], sketch_ref[...], ref)


def more_kernel(feat, act_ref, grad_ref, down_ref, sketch_ref, *piece_refs):
    del feat
    step = pl.program_id(0)
    for index, ref in enumerate(piece_refs):

        @pl.when(step == index)
        def _(ref=ref):
            project_piece(act_ref[...], grad_ref[...], down_ref[...], sketch_ref[...], ref)


def whole(shape):
    return pl.BlockSpec(shape, lambda i, feat: (0,) * len(shape))


def chunk_of(turn, feat):
    left = feat < 2
    far, near = jnp.where(left, 3, 0), jnp.where(left, 2, 1)
    return jnp.where(turn == 0, far, jnp.where(turn == 1, near, jnp.where(turn == 2, feat ^ 1, feat)))


def project(kernel, feat, first, count, acts, grads, operands, extra):
    ko = operands[-1 if kernel is more_kernel else 2].shape[1]
    width = acts.shape[1]
    rows = acts.shape[0] // PIECES
    piece = (PIECE, rows // PIECE * 3 // 2, ko)
    block = pl.BlockSpec((rows, width), lambda i, feat: (chunk_of((first + i) // 2, feat[0]) * 2 + (first + i) % 2, 0))
    return pl.pallas_call(
        kernel,
        out_shape=[jax.ShapeDtypeStruct(piece, jnp.float32)] * count + extra,
        grid_spec=pltpu.PrefetchScalarGridSpec(
            num_scalar_prefetch=1,
            grid=(count,),
            in_specs=[block, block] + [whole(x.shape) for x in operands],
            out_specs=[whole(piece)] * count + [whole(x.shape) for x in extra],
        ),
        cost_estimate=pl.CostEstimate(
            flops=count * rows * width * ko * 4,
            bytes_accessed=count * rows * (width * 4 + ko * 6),
            transcendentals=0,
        ),
        compiler_params=pltpu.CompilerParams(vmem_limit_bytes=SMALL),
        name="project",
    )(feat, acts, grads, *operands)


def lang_kernel(me_ref, held_ref, lang_ref, *refs):
    *square_refs, other_ref = refs[:5]
    own_refs = refs[5:]
    count = len(own_refs)
    rows, width = held_ref.shape
    piece = width // (2 * count)
    hit = lang_ref[...] == lax.broadcasted_iota(jnp.int32, (LANGS, rows), 0)
    hit = jnp.where(hit, 1.0, 0.0)
    hit = jnp.concatenate([hit, hit], axis=1).astype(jnp.bfloat16)
    inverse = lax.rsqrt(sum(ref[...] for ref in square_refs) + 1e-06)

    def sums(part):
        columns = pl.ds(pl.multiple_of(part * piece, piece), piece)
        unit = held_ref[:, columns] * inverse
        high = unit.astype(jnp.bfloat16)
        rest = (unit - high.astype(jnp.float32)).astype(jnp.bfloat16)
        both = jnp.concatenate([high, rest], axis=0)
        return jnp.dot(hit, both, preferred_element_type=jnp.float32)

    for index in range(count):
        other_ref[index] = sums(me_ref[0] ^ 1 ^ (2 * index))
        own_refs[index][...] = sums(me_ref[0] ^ (2 * index))


def lang_parts(me, held, squares, lang, n_ex):
    rows, width = held.shape
    piece = width // n_ex
    half = n_ex // 2
    return pl.pallas_call(
        lang_kernel,
        out_shape=[jax.ShapeDtypeStruct((half, LANGS, piece), jnp.float32)]
        + [jax.ShapeDtypeStruct((LANGS, piece), jnp.float32)] * half,
        in_specs=[SMEM] + [VMEM] * 6,
        out_specs=[VMEM] * (1 + half),
        compiler_params=pltpu.CompilerParams(vmem_limit_bytes=SMALL),
        name="lang_parts",
    )(me, held, lang.reshape(1, rows), *squares)


def product_kernel(middle_ref, own_ref, end_ref, near_ref, o_ref, square_ref, grad_ref):
    middle = middle_ref[0] == 1
    rows = own_ref.shape[1] * 2 // 3
    seq = rows // UNIT
    wide = own_ref.shape[2]
    low = lax.broadcasted_iota(jnp.int32, (seq, wide), 1) < wide // 2

    def split(x, order):
        high = x.astype(jnp.bfloat16)
        rest = (x - high.astype(jnp.float32)).astype(jnp.bfloat16)
        return jnp.concatenate([high, rest, high] if order else [high, high, rest], axis=0)

    def total(unit, start):
        block = (unit, pl.ds(start, seq), slice(None))
        return own_ref[block] + end_ref[block] + jnp.where(middle, near_ref[block], 0.0)

    for unit in range(PIECE):
        for pair in range(UNIT // 2):
            both = total(unit, rows + pair * seq)
            turned = pltpu.roll(both, wide // 2, 1)
            for side in range(2):
                example = pair + side * (UNIT // 2)
                rank = jnp.where(low, turned, both) if side else jnp.where(low, both, turned)
                grad_ref[unit * UNIT + example] = lax.dot_general(
                    split(total(unit, example * seq), True),
                    split(rank, False),
                    (((0,), (0,)), ((), ())),
                    preferred_element_type=jnp.float32,
                )
    count = PIECE * UNIT
    low = lax.broadcasted_iota(jnp.int32, (count, wide), 1) < wide // 2
    square = jnp.zeros((count, 2 * wide), jnp.float32)
    for index in range(o_ref.shape[0]):
        rows_of = [grad_ref[:, 4 * index + j, :] for j in range(4)]
        part = jnp.concatenate(
            [jnp.where(low, rows_of[0], rows_of[1]), jnp.where(low, rows_of[2], rows_of[3])], axis=1
        )
        square += part * part
        rest = part - part.astype(jnp.bfloat16).astype(jnp.float32)
        o_ref[index] = jnp.concatenate([part, rest], axis=0).astype(jnp.bfloat16)
    square_ref[...] = jnp.sum(square, axis=1, keepdims=True)


def product(middle, parts):
    count, wide = PIECE * UNIT, parts[0].shape[2]
    return pl.pallas_call(
        product_kernel,
        out_shape=[
            jax.ShapeDtypeStruct((wide // 4, 2 * count, 2 * wide), jnp.bfloat16),
            jax.ShapeDtypeStruct((count, 1), jnp.float32),
        ],
        in_specs=[SMEM] + [VMEM] * len(parts),
        out_specs=[VMEM] * 2,
        scratch_shapes=[pltpu.VMEM((count, wide, wide), jnp.float32)],
        compiler_params=pltpu.CompilerParams(vmem_limit_bytes=SMALL),
        name="product",
    )(middle, *parts)


def score_kernel(feat_ref, ex_ref, *refs, scale, n_lang):
    lang_refs, grad_refs, square_refs, o_ref = refs[:n_lang], refs[n_lang:-1:2], refs[n_lang + 1 : -1 : 2], refs[-1]
    total = None
    feat, ex = feat_ref[0], ex_ref[0]
    middle = (feat == 1) | (feat == 2)
    second = feat ^ jnp.where(middle, 3, 2)
    rows_from = [feat, feat ^ 1, second, second ^ 1]
    masks = [*range(0, n_lang, 2), *range(1, n_lang, 2)]
    for j, ref in enumerate(lang_refs):
        for m in range(4):
            index = rows_from[m] * n_lang + (ex ^ masks[j])
            lang = ref[m]
            rest = lang - lang.astype(jnp.bfloat16).astype(jnp.float32)
            lang = jnp.concatenate([lang, rest], axis=0).astype(jnp.bfloat16)
            grad = jnp.concatenate([g[index] for g in grad_refs], axis=0)
            term = lax.dot_general(
                grad, lang, (((1,), (1,)), ((), ())), preferred_element_type=jnp.float32
            )
            total = term if total is None else total + term
    total = total + pltpu.roll(total, LANGS, 1)
    count = square_refs[0].shape[0]
    for index, square_ref in enumerate(square_refs):
        start = 2 * count * index
        inner = total[start : start + count, :LANGS] + total[start + count : start + 2 * count, :LANGS]
        o_ref[index * count : (index + 1) * count] = inner * (lax.rsqrt(square_ref[...] + 1e-06) * scale)


def score(feat, ex, langs, products, scale):
    flat = [x for pair in products for x in pair]
    mine = sum(square.shape[0] for _, square in products)
    return pl.pallas_call(
        functools.partial(score_kernel, scale=scale, n_lang=len(langs)),
        out_shape=jax.ShapeDtypeStruct((mine, LANGS), jnp.float32),
        in_specs=[SMEM] * 2 + [VMEM] * (len(langs) + len(flat)),
        out_specs=VMEM,
        compiler_params=pltpu.CompilerParams(vmem_limit_bytes=SMALL),
        name="score",
    )(feat, ex, *langs, *flat)


def small(kernel, shape, middle, operands):
    return pl.pallas_call(
        kernel,
        out_shape=jax.ShapeDtypeStruct(shape, jnp.float32),
        in_specs=[SMEM] + [VMEM] * len(operands),
        out_specs=VMEM,
        compiler_params=pltpu.CompilerParams(vmem_limit_bytes=SMALL),
    )(middle, *operands)


def onward_kernel(middle_ref, raw_ref, got_ref, o_ref):
    o_ref[...] = raw_ref[...] + jnp.where(middle_ref[0] == 1, got_ref[...], 0.0)


def stack_kernel(middle_ref, one_ref, two_ref, o_ref):
    del middle_ref
    o_ref[0] = one_ref[...]
    o_ref[1] = two_ref[...]


def join_kernel(middle_ref, pair_ref, inner_ref, outer_ref, o_ref):
    o_ref[:2] = pair_ref[...]
    o_ref[2:] = jnp.where(middle_ref[0] == 1, inner_ref[...], outer_ref[...])


def place_kernel(me_ref, *refs):
    *parts, o_ref = refs
    rows = parts[0].shape[0]
    for mask, ref in enumerate(parts):
        o_ref[pl.ds(pl.multiple_of((me_ref[0] ^ mask) * rows, rows), rows), :] = ref[...]


def place(me, parts):
    rows, columns = parts[0].shape
    return pl.pallas_call(
        place_kernel,
        out_shape=jax.ShapeDtypeStruct((rows * len(parts), columns), jnp.float32),
        in_specs=[SMEM] + [VMEM] * len(parts),
        out_specs=VMEM,
        compiler_params=pltpu.CompilerParams(vmem_limit_bytes=SMALL),
        name="place",
    )(me, *parts)


def swap(x, axis, mask):
    return lax.ppermute(x, axis, [(i, i ^ mask) for i in range(lax.axis_size(axis))])


def after(x, *others):
    return lax.optimization_barrier((x, *others))[0]


def fast(*args):
    return ordered(*args)


def ordered(acts, grads, adapter, rank_sketch, out_sketch, held, perm):
    feat, ex = lax.axis_index("feat"), lax.axis_index("ex")
    n_ex = lax.axis_size("ex")
    _, _, width = acts.shape
    middle = (feat == 1) | (feat == 2)
    me_ex = ex.astype(jnp.int32).reshape(1)
    me_feat = feat.astype(jnp.int32).reshape(1)
    acts2, grads2 = acts.reshape(-1, width), grads.reshape(-1, width)
    adapter, rank_sketch, out_sketch, held, acts2, grads2 = (
        pltpu.with_memory_space_constraint(x, pltpu.HBM)
        for x in (adapter, rank_sketch.T, out_sketch, held, acts2, grads2)
    )
    down_like = jax.ShapeDtypeStruct((width, 2 * rank_sketch.shape[0]), jnp.bfloat16)
    square_like = jax.ShapeDtypeStruct((held.shape[0], 1), jnp.float32)
    inward = [(0, 1), (3, 2)]
    outward = [(1, 0), (2, 3)]
    inner = [(1, 2), (2, 1), (0, 0), (3, 3)]
    is_middle = middle.astype(jnp.int32).reshape(1)

    def onward(raw, got):
        return small(onward_kernel, raw.shape, is_middle, [raw, got])

    *raw0, down, own_square = project(
        first_kernel, me_feat, 0, 2, acts2, grads2, [adapter, rank_sketch, out_sketch, held], [down_like, square_like]
    )
    squares = [own_square] + [swap(own_square, "feat", mask) for mask in (1, 2, 3)]
    got1 = [swap(x, "feat", 1) for x in raw0]
    raw1 = project(more_kernel, me_feat, 2, 2, acts2, grads2, [down, out_sketch], [])

    squares[1:] = [after(x, raw1[0]) for x in squares[1:]]
    other, *parts = lang_parts(me_ex, held, squares, perm % LANGS, n_ex)
    other = swap(other, "ex", 1)
    parts = [x + other[i] for i, x in enumerate(parts)]
    scattered = [swap(parts[i], "ex", 2 * i) for i in range(1, n_ex // 2)]
    sent1 = [onward(after(raw0[0], parts[0]), got1[0])]
    far = [lax.ppermute(sent1[0], "feat", inner)]
    lang = after(parts[0], sent1[0]) + sum(scattered)
    other = swap(lang, "feat", 1)
    raw1 = [after(x, lang) for x in raw1]
    got2 = [swap(raw1[0], "feat", 1)]
    raw2 = project(more_kernel, me_feat, 4, 2, acts2, grads2, [after(down, lang), out_sketch], [])
    other = after(other, raw2[0])
    pair = small(stack_kernel, (2, *lang.shape), is_middle, [lang, other])
    far_pair = lax.ppermute(pair, "feat", inner)
    sent1.append(onward(after(raw0[1], pair), got1[1]))
    far.append(lax.ppermute(sent1[1], "feat", inner))
    got2.append(lax.ppermute(after(raw1[1], pair), "feat", inward))
    far_pair = after(far_pair, sent1[1])
    outer_pair = lax.ppermute(far_pair, "feat", outward)
    sent2 = [onward(after(raw1[0], far_pair), got2[0])]
    near = [lax.ppermute(sent2[0], "feat", inner)]
    sent3 = [onward(after(raw2[0], sent2[0]), far[0])]
    got3 = [swap(sent3[0], "feat", 1)]
    pair = after(pair, sent3[0])
    langs = [small(join_kernel, (4, *lang.shape), is_middle, [pair, far_pair, outer_pair])]
    langs = langs + [swap(langs[0], "ex", mask) for mask in range(2, n_ex, 2)]
    sent3.append(onward(after(raw2[1], langs[0]), far[1]))
    got3.append(swap(sent3[1], "feat", 1))
    sent2.append(onward(after(raw1[1], sent3[1]), got2[1]))
    near.append(lax.ppermute(sent2[1], "feat", inner))
    own_a, own_b = project(more_kernel, me_feat, 6, 2, acts2, grads2, [after(down, sent2[1]), out_sketch], [])
    grad_a, square_a = product(is_middle, [own_a, got3[0], near[0]])
    langs[1:] = [after(x, square_a) for x in langs[1:]]
    langs = langs + [swap(x, "ex", 1) for x in langs]
    grad_b, square_b = product(is_middle, [after(own_b, square_a), got3[1], near[1]])
    products = [(grad_a, square_a), (grad_b, square_b)]
    per_lang = perm.shape[0] * n_ex // LANGS
    scale = (KF * per_lang) ** 0.5 / per_lang
    mine = score(me_feat, me_ex, langs, products, scale)
    return place(me_feat, [mine] + [swap(mine, "feat", mask) for mask in (1, 2, 3)])


def general(acts, grads, adapter, rank_sketch, out_sketch, held, perm):
    ex_dev = acts.shape[0]
    down = jnp.dot(adapter, rank_sketch, preferred_element_type=jnp.float32).astype(jnp.bfloat16)
    rank_part = jnp.einsum("esd,dr->esr", acts, down, preferred_element_type=jnp.float32)
    rank_side = lax.psum(rank_part, "feat")
    out_part = jnp.einsum("esd,dk->esk", grads, out_sketch, preferred_element_type=jnp.float32)
    out_side = lax.psum_scatter(out_part, "feat", scatter_dimension=2, tiled=True)
    grad = jnp.einsum("esk,esr->ekr", out_side, rank_side, precision=HIGHEST).reshape(ex_dev, -1)
    squares = lax.psum(jnp.sum(held * held, axis=1), "feat")
    unit = held * lax.rsqrt(squares + 1e-06)[:, None]
    onehot = ((perm % LANGS)[:, None] == jnp.arange(LANGS, dtype=jnp.int32)[None, :]).astype(jnp.float32)
    per_lang = perm.shape[0] * lax.axis_size("ex") // LANGS
    lang_mean = lax.psum(jnp.dot(onehot.T, unit, precision=HIGHEST), "ex") / per_lang
    inner, norm = lax.psum(
        (jnp.dot(grad, lang_mean.T, precision=HIGHEST), jnp.sum(grad * grad, axis=1)), "feat"
    )
    scale = jnp.sqrt(jnp.float32(KF * per_lang))
    return scale * inner * lax.rsqrt(norm + 1e-06)[:, None]


def solution(mesh):
    placed = (
        P("ex", None, "feat"),
        P("ex", None, "feat"),
        P("feat", None),
        P(),
        P("feat", None),
        P("ex", "feat"),
        P("ex"),
    )
    is_fast = mesh.shape["feat"] == 4 and mesh.shape["ex"] == 8
    body = fast if is_fast else general
    return jax.shard_map(body, mesh=mesh, in_specs=placed, out_specs=P("ex", None), check_vma=False)
```

```python
import functools

import jax
import jax.numpy as jnp
from jax import lax
from jax.experimental import pallas as pl
from jax.experimental.pallas import tpu as pltpu
from jax.sharding import PartitionSpec as P


KF = 8192
LANGS = 64
UNIT = 4
PIECE = 2
PIECES = 8
HIGHEST = lax.Precision.HIGHEST
SMALL = 24 * 1024 * 1024
VMEM = pl.BlockSpec(memory_space=pltpu.VMEM)
SMEM = pl.BlockSpec(memory_space=pltpu.SMEM)


def project_piece(act, grad, down, sketch, o_ref):
    rows = act.shape[0] // PIECE
    half = rows // 2
    out = jnp.dot(grad, sketch, preferred_element_type=jnp.float32)
    rank = jnp.dot(act, down, preferred_element_type=jnp.float32)
    low = lax.broadcasted_iota(jnp.int32, (half, down.shape[1]), 1) < down.shape[1] // 2
    for unit in range(PIECE):
        start = unit * rows
        o_ref[unit, :rows, :] = out[start : start + rows]
        o_ref[unit, rows:, :] = jnp.where(low, rank[start : start + half], rank[start + half : start + rows])


def first_kernel(feat, act_ref, grad_ref, adapter_ref, rank_ref, sketch_ref, held_ref, *o_refs):
    del feat
    *piece_refs, down_ref, square_ref = o_refs
    step = pl.program_id(0)

    @pl.when(step == 0)
    def _():
        down = lax.dot_general(
            adapter_ref[...], rank_ref[...], (((1,), (1,)), ((), ())), preferred_element_type=jnp.float32
        )
        down_ref[...] = jnp.concatenate([down, down], axis=1).astype(jnp.bfloat16)
        held = held_ref[...]
        square_ref[...] = jnp.sum(held * held, axis=1, keepdims=True)

    for index, ref in enumerate(piece_refs):

        @pl.when(step == index)
        def _(ref=ref):
            project_piece(act_ref[...], grad_ref[...], down_ref[...], sketch_ref[...], ref)


def more_kernel(feat, act_ref, grad_ref, down_ref, sketch_ref, *piece_refs):
    del feat
    step = pl.program_id(0)
    for index, ref in enumerate(piece_refs):

        @pl.when(step == index)
        def _(ref=ref):
            project_piece(act_ref[...], grad_ref[...], down_ref[...], sketch_ref[...], ref)


def whole(shape):
    return pl.BlockSpec(shape, lambda i, feat: (0,) * len(shape))


def chunk_of(turn, feat):
    left = feat < 2
    far, near = jnp.where(left, 3, 0), jnp.where(left, 2, 1)
    return jnp.where(turn == 0, far, jnp.where(turn == 1, near, jnp.where(turn == 2, feat ^ 1, feat)))


def project(kernel, feat, first, count, acts, grads, operands, extra):
    ko = operands[-1 if kernel is more_kernel else 2].shape[1]
    width = acts.shape[1]
    rows = acts.shape[0] // PIECES
    piece = (PIECE, rows // PIECE * 3 // 2, ko)
    block = pl.BlockSpec((rows, width), lambda i, feat: (chunk_of((first + i) // 2, feat[0]) * 2 + (first + i) % 2, 0))
    return pl.pallas_call(
        kernel,
        out_shape=[jax.ShapeDtypeStruct(piece, jnp.float32)] * count + extra,
        grid_spec=pltpu.PrefetchScalarGridSpec(
            num_scalar_prefetch=1,
            grid=(count,),
            in_specs=[block, block] + [whole(x.shape) for x in operands],
            out_specs=[whole(piece)] * count + [whole(x.shape) for x in extra],
        ),
        cost_estimate=pl.CostEstimate(
            flops=count * rows * width * ko * 4,
            bytes_accessed=count * rows * (width * 4 + ko * 6),
            transcendentals=0,
        ),
        compiler_params=pltpu.CompilerParams(vmem_limit_bytes=SMALL),
        name="project",
    )(feat, acts, grads, *operands)


def lang_kernel(me_ref, held_ref, lang_ref, *refs):
    *square_refs, other_ref = refs[:5]
    own_refs = refs[5:]
    count = len(own_refs)
    rows, width = held_ref.shape
    piece = width // (2 * count)
    hit = lang_ref[...] == lax.broadcasted_iota(jnp.int32, (LANGS, rows), 0)
    hit = jnp.where(hit, 1.0, 0.0)
    hit = jnp.concatenate([hit, hit], axis=1).astype(jnp.bfloat16)
    inverse = lax.rsqrt(sum(ref[...] for ref in square_refs) + 1e-06)

    def sums(part):
        columns = pl.ds(pl.multiple_of(part * piece, piece), piece)
        unit = held_ref[:, columns] * inverse
        high = unit.astype(jnp.bfloat16)
        rest = (unit - high.astype(jnp.float32)).astype(jnp.bfloat16)
        both = jnp.concatenate([high, rest], axis=0)
        return jnp.dot(hit, both, preferred_element_type=jnp.float32)

    for index in range(count):
        other_ref[index] = sums(me_ref[0] ^ 1 ^ (2 * index))
        own_refs[index][...] = sums(me_ref[0] ^ (2 * index))


def lang_parts(me, held, squares, lang, n_ex):
    rows, width = held.shape
    piece = width // n_ex
    half = n_ex // 2
    return pl.pallas_call(
        lang_kernel,
        out_shape=[jax.ShapeDtypeStruct((half, LANGS, piece), jnp.float32)]
        + [jax.ShapeDtypeStruct((LANGS, piece), jnp.float32)] * half,
        in_specs=[SMEM] + [VMEM] * 6,
        out_specs=[VMEM] * (1 + half),
        compiler_params=pltpu.CompilerParams(vmem_limit_bytes=SMALL),
        name="lang_parts",
    )(me, held, lang.reshape(1, rows), *squares)


def product_kernel(middle_ref, own_ref, end_ref, near_ref, o_ref, square_ref, grad_ref):
    middle = middle_ref[0] == 1
    rows = own_ref.shape[1] * 2 // 3
    seq = rows // UNIT
    wide = own_ref.shape[2]
    low = lax.broadcasted_iota(jnp.int32, (seq, wide), 1) < wide // 2

    def split(x, order):
        high = x.astype(jnp.bfloat16)
        rest = (x - high.astype(jnp.float32)).astype(jnp.bfloat16)
        return jnp.concatenate([high, rest, high] if order else [high, high, rest], axis=0)

    def total(unit, start):
        block = (unit, pl.ds(start, seq), slice(None))
        return own_ref[block] + end_ref[block] + jnp.where(middle, near_ref[block], 0.0)

    for unit in range(PIECE):
        for pair in range(UNIT // 2):
            both = total(unit, rows + pair * seq)
            turned = pltpu.roll(both, wide // 2, 1)
            for side in range(2):
                example = pair + side * (UNIT // 2)
                rank = jnp.where(low, turned, both) if side else jnp.where(low, both, turned)
                grad_ref[unit * UNIT + example] = lax.dot_general(
                    split(total(unit, example * seq), True),
                    split(rank, False),
                    (((0,), (0,)), ((), ())),
                    preferred_element_type=jnp.float32,
                )
    count = PIECE * UNIT
    low = lax.broadcasted_iota(jnp.int32, (count, wide), 1) < wide // 2
    square = jnp.zeros((count, 2 * wide), jnp.float32)
    for index in range(o_ref.shape[0]):
        rows_of = [grad_ref[:, 4 * index + j, :] for j in range(4)]
        part = jnp.concatenate(
            [jnp.where(low, rows_of[0], rows_of[1]), jnp.where(low, rows_of[2], rows_of[3])], axis=1
        )
        square += part * part
        rest = part - part.astype(jnp.bfloat16).astype(jnp.float32)
        o_ref[index] = jnp.concatenate([part, rest], axis=0).astype(jnp.bfloat16)
    square_ref[...] = jnp.sum(square, axis=1, keepdims=True)


def product(middle, parts):
    count, wide = PIECE * UNIT, parts[0].shape[2]
    return pl.pallas_call(
        product_kernel,
        out_shape=[
            jax.ShapeDtypeStruct((wide // 4, 2 * count, 2 * wide), jnp.bfloat16),
            jax.ShapeDtypeStruct((count, 1), jnp.float32),
        ],
        in_specs=[SMEM] + [VMEM] * len(parts),
        out_specs=[VMEM] * 2,
        scratch_shapes=[pltpu.VMEM((count, wide, wide), jnp.float32)],
        compiler_params=pltpu.CompilerParams(vmem_limit_bytes=SMALL),
        name="product",
    )(middle, *parts)


def score_kernel(middle_ref, feat_ref, ex_ref, *refs, scale, n_lang):
    lang_refs, (grad_a, square_a, *part_refs, o_ref, grad_b, square_b, grad_ref) = refs[:n_lang], refs[n_lang:]
    product_kernel(middle_ref, *part_refs, grad_b, square_b, grad_ref)
    grad_refs, square_refs = [grad_a, grad_b], [square_a, square_b]
    total = None
    feat, ex = feat_ref[0], ex_ref[0]
    middle = (feat == 1) | (feat == 2)
    second = feat ^ jnp.where(middle, 3, 2)
    rows_from = [feat, feat ^ 1, second, second ^ 1]
    masks = [*range(0, n_lang, 2), *range(1, n_lang, 2)]
    for j, ref in enumerate(lang_refs):
        for m in range(4):
            index = rows_from[m] * n_lang + (ex ^ masks[j])
            lang = ref[m]
            rest = lang - lang.astype(jnp.bfloat16).astype(jnp.float32)
            lang = jnp.concatenate([lang, rest], axis=0).astype(jnp.bfloat16)
            grad = jnp.concatenate([g[index] for g in grad_refs], axis=0)
            term = lax.dot_general(
                grad, lang, (((1,), (1,)), ((), ())), preferred_element_type=jnp.float32
            )
            total = term if total is None else total + term
    total = total + pltpu.roll(total, LANGS, 1)
    count = square_refs[0].shape[0]
    for index, square_ref in enumerate(square_refs):
        start = 2 * count * index
        inner = total[start : start + count, :LANGS] + total[start + count : start + 2 * count, :LANGS]
        o_ref[index * count : (index + 1) * count] = inner * (lax.rsqrt(square_ref[...] + 1e-06) * scale)


def score(middle, feat, ex, langs, first, parts, scale):
    grad, square = first
    operands = [*langs, *first, *parts]
    wide = parts[0].shape[2]
    return pl.pallas_call(
        functools.partial(score_kernel, scale=scale, n_lang=len(langs)),
        out_shape=jax.ShapeDtypeStruct((2 * square.shape[0], LANGS), jnp.float32),
        in_specs=[SMEM] * 3 + [VMEM] * len(operands),
        out_specs=VMEM,
        scratch_shapes=[
            pltpu.VMEM(grad.shape, grad.dtype),
            pltpu.VMEM(square.shape, square.dtype),
            pltpu.VMEM((square.shape[0], wide, wide), jnp.float32),
        ],
        compiler_params=pltpu.CompilerParams(vmem_limit_bytes=SMALL),
        name="score",
    )(middle, feat, ex, *operands)


def small(kernel, shape, middle, operands):
    return pl.pallas_call(
        kernel,
        out_shape=jax.ShapeDtypeStruct(shape, jnp.float32),
        in_specs=[SMEM] + [VMEM] * len(operands),
        out_specs=VMEM,
        compiler_params=pltpu.CompilerParams(vmem_limit_bytes=SMALL),
    )(middle, *operands)


def onward_kernel(middle_ref, raw_ref, got_ref, o_ref):
    o_ref[...] = raw_ref[...] + jnp.where(middle_ref[0] == 1, got_ref[...], 0.0)


def stack_kernel(middle_ref, one_ref, two_ref, o_ref):
    del middle_ref
    o_ref[0] = one_ref[...]
    o_ref[1] = two_ref[...]


def join_kernel(middle_ref, pair_ref, inner_ref, outer_ref, o_ref):
    o_ref[:2] = pair_ref[...]
    o_ref[2:] = jnp.where(middle_ref[0] == 1, inner_ref[...], outer_ref[...])


def place_kernel(me_ref, *refs):
    *parts, o_ref = refs
    rows = parts[0].shape[0]
    for mask, ref in enumerate(parts):
        o_ref[pl.ds(pl.multiple_of((me_ref[0] ^ mask) * rows, rows), rows), :] = ref[...]


def place(me, parts):
    rows, columns = parts[0].shape
    return pl.pallas_call(
        place_kernel,
        out_shape=jax.ShapeDtypeStruct((rows * len(parts), columns), jnp.float32),
        in_specs=[SMEM] + [VMEM] * len(parts),
        out_specs=VMEM,
        compiler_params=pltpu.CompilerParams(vmem_limit_bytes=SMALL),
        name="place",
    )(me, *parts)


def swap(x, axis, mask):
    return lax.ppermute(x, axis, [(i, i ^ mask) for i in range(lax.axis_size(axis))])


def after(x, *others):
    return lax.optimization_barrier((x, *others))[0]


def fast(*args):
    return ordered(*args)


def ordered(acts, grads, adapter, rank_sketch, out_sketch, held, perm):
    feat, ex = lax.axis_index("feat"), lax.axis_index("ex")
    n_ex = lax.axis_size("ex")
    _, _, width = acts.shape
    middle = (feat == 1) | (feat == 2)
    me_ex = ex.astype(jnp.int32).reshape(1)
    me_feat = feat.astype(jnp.int32).reshape(1)
    acts2, grads2 = acts.reshape(-1, width), grads.reshape(-1, width)
    adapter, rank_sketch, out_sketch, held_far, acts2, grads2 = (
        pltpu.with_memory_space_constraint(x, pltpu.HBM)
        for x in (adapter, rank_sketch.T, out_sketch, held, acts2, grads2)
    )
    down_like = jax.ShapeDtypeStruct((width, 2 * rank_sketch.shape[0]), jnp.bfloat16)
    square_like = jax.ShapeDtypeStruct((held.shape[0], 1), jnp.float32)
    inward = [(0, 1), (3, 2)]
    inner = [(1, 2), (2, 1), (0, 0), (3, 3)]
    is_middle = middle.astype(jnp.int32).reshape(1)

    def onward(raw, got):
        return small(onward_kernel, raw.shape, is_middle, [raw, got])

    raw0_a, down, own_square = project(
        first_kernel, me_feat, 0, 1, acts2, grads2, [adapter, rank_sketch, out_sketch, held_far], [down_like, square_like]
    )
    got1 = [swap(raw0_a, "feat", 1)]
    squares = [own_square] + [swap(own_square, "feat", mask) for mask in (1, 2, 3)]
    raw0_b, *raw1 = project(more_kernel, me_feat, 1, 3, acts2, grads2, [down, out_sketch], [])
    got1.append(swap(raw0_b, "feat", 1))
    got2 = [swap(raw1[0], "feat", 1)]
    sent1 = [onward(after(raw0_a, raw1[1]), got1[0])]
    far = [lax.ppermute(sent1[0], "feat", inner)]

    squares[1:] = [after(x, sent1[0]) for x in squares[1:]]
    other, *parts = lang_parts(me_ex, held, squares, perm % LANGS, n_ex)
    other = swap(other, "ex", 1)
    parts = [x + other[i] for i, x in enumerate(parts)]
    scattered = [swap(parts[i], "ex", 2 * i) for i in range(1, n_ex // 2)]
    sent1.append(onward(after(raw0_b, parts[0]), got1[1]))
    far.append(lax.ppermute(sent1[1], "feat", inner))
    lang = after(parts[0], sent1[1]) + sum(scattered)
    other = swap(lang, "feat", 1)
    raw2 = project(more_kernel, me_feat, 4, 2, acts2, grads2, [after(down, lang), out_sketch], [])
    got2.append(lax.ppermute(after(raw1[1], raw2[0]), "feat", inward))
    pair = small(stack_kernel, (2, *lang.shape), is_middle, [lang, after(other, raw2[0])])
    far_pair = [lax.ppermute(pair, "feat", pairs) for pairs in (inner, [(1, 3), (2, 0)])]
    sent2 = [onward(after(raw1[0], pair), got2[0])]
    near = [lax.ppermute(sent2[0], "feat", inner)]
    sent3 = [onward(after(raw2[0], sent2[0]), far[0])]
    got3 = [swap(sent3[0], "feat", 1)]
    pair = after(pair, sent3[0])
    langs = [small(join_kernel, (4, *lang.shape), is_middle, [pair, *far_pair])]
    langs = langs + [swap(langs[0], "ex", mask) for mask in range(2, n_ex, 2)]
    sent3.append(onward(after(raw2[1], langs[0]), far[1]))
    got3.append(swap(sent3[1], "feat", 1))
    sent2.append(onward(after(raw1[1], sent3[1]), got2[1]))
    near.append(lax.ppermute(sent2[1], "feat", inner))
    own_a, own_b = project(more_kernel, me_feat, 6, 2, acts2, grads2, [after(down, sent2[1]), out_sketch], [])
    grad_a, square_a = product(is_middle, [own_a, got3[0], near[0]])
    langs[1:] = [after(x, square_a) for x in langs[1:]]
    langs = langs + [swap(x, "ex", 1) for x in langs]
    per_lang = perm.shape[0] * n_ex // LANGS
    scale = (KF * per_lang) ** 0.5 / per_lang
    mine = score(is_middle, me_feat, me_ex, langs, [grad_a, square_a], [own_b, got3[1], near[1]], scale)
    return place(me_feat, [mine] + [swap(mine, "feat", mask) for mask in (1, 2, 3)])


def general(acts, grads, adapter, rank_sketch, out_sketch, held, perm):
    ex_dev = acts.shape[0]
    down = jnp.dot(adapter, rank_sketch, preferred_element_type=jnp.float32).astype(jnp.bfloat16)
    rank_part = jnp.einsum("esd,dr->esr", acts, down, preferred_element_type=jnp.float32)
    rank_side = lax.psum(rank_part, "feat")
    out_part = jnp.einsum("esd,dk->esk", grads, out_sketch, preferred_element_type=jnp.float32)
    out_side = lax.psum_scatter(out_part, "feat", scatter_dimension=2, tiled=True)
    grad = jnp.einsum("esk,esr->ekr", out_side, rank_side, precision=HIGHEST).reshape(ex_dev, -1)
    squares = lax.psum(jnp.sum(held * held, axis=1), "feat")
    unit = held * lax.rsqrt(squares + 1e-06)[:, None]
    onehot = ((perm % LANGS)[:, None] == jnp.arange(LANGS, dtype=jnp.int32)[None, :]).astype(jnp.float32)
    per_lang = perm.shape[0] * lax.axis_size("ex") // LANGS
    lang_mean = lax.psum(jnp.dot(onehot.T, unit, precision=HIGHEST), "ex") / per_lang
    inner, norm = lax.psum(
        (jnp.dot(grad, lang_mean.T, precision=HIGHEST), jnp.sum(grad * grad, axis=1)), "feat"
    )
    scale = jnp.sqrt(jnp.float32(KF * per_lang))
    return scale * inner * lax.rsqrt(norm + 1e-06)[:, None]


def solution(mesh):
    placed = (
        P("ex", None, "feat"),
        P("ex", None, "feat"),
        P("feat", None),
        P(),
        P("feat", None),
        P("ex", "feat"),
        P("ex"),
    )
    is_fast = mesh.shape["feat"] == 4 and mesh.shape["ex"] == 8
    body = fast if is_fast else general
    return jax.shard_map(body, mesh=mesh, in_specs=placed, out_specs=P("ex", None), check_vma=False)
```

```python
import functools

import jax
import jax.numpy as jnp
from jax import lax
from jax.experimental import pallas as pl
from jax.experimental.pallas import tpu as pltpu
from jax.sharding import PartitionSpec as P


KF = 8192
LANGS = 64
UNIT = 4
PIECE = 2
PIECES = 8
HIGHEST = lax.Precision.HIGHEST
SMALL = 24 * 1024 * 1024
VMEM = pl.BlockSpec(memory_space=pltpu.VMEM)
SMEM = pl.BlockSpec(memory_space=pltpu.SMEM)


def project_piece(act, grad, down, sketch, o_ref):
    rows = act.shape[0] // PIECE
    half = rows // 2
    out = jnp.dot(grad, sketch, preferred_element_type=jnp.float32)
    rank = jnp.dot(act, down, preferred_element_type=jnp.float32)
    low = lax.broadcasted_iota(jnp.int32, (half, down.shape[1]), 1) < down.shape[1] // 2
    for unit in range(PIECE):
        start = unit * rows
        o_ref[unit, :rows, :] = out[start : start + rows]
        o_ref[unit, rows:, :] = jnp.where(low, rank[start : start + half], rank[start + half : start + rows])


def first_kernel(feat, act_ref, grad_ref, adapter_ref, rank_ref, sketch_ref, held_ref, *o_refs):
    del feat
    *piece_refs, down_ref, square_ref = o_refs
    step = pl.program_id(0)

    @pl.when(step == 0)
    def _():
        down = lax.dot_general(
            adapter_ref[...], rank_ref[...], (((1,), (1,)), ((), ())), preferred_element_type=jnp.float32
        )
        down_ref[...] = jnp.concatenate([down, down], axis=1).astype(jnp.bfloat16)
        held = held_ref[...]
        square_ref[...] = jnp.sum(held * held, axis=1, keepdims=True)

    for index, ref in enumerate(piece_refs):

        @pl.when(step == index)
        def _(ref=ref):
            project_piece(act_ref[...], grad_ref[...], down_ref[...], sketch_ref[...], ref)


def more_kernel(feat, act_ref, grad_ref, down_ref, sketch_ref, *piece_refs):
    del feat
    step = pl.program_id(0)
    for index, ref in enumerate(piece_refs):

        @pl.when(step == index)
        def _(ref=ref):
            project_piece(act_ref[...], grad_ref[...], down_ref[...], sketch_ref[...], ref)


def whole(shape):
    return pl.BlockSpec(shape, lambda i, feat: (0,) * len(shape))


def chunk_of(turn, feat):
    left = feat < 2
    far, near = jnp.where(left, 3, 0), jnp.where(left, 2, 1)
    return jnp.where(turn == 0, far, jnp.where(turn == 1, near, jnp.where(turn == 2, feat ^ 1, feat)))


def project(kernel, feat, first, count, acts, grads, operands, extra):
    ko = operands[-1 if kernel is more_kernel else 2].shape[1]
    width = acts.shape[1]
    rows = acts.shape[0] // PIECES
    piece = (PIECE, rows // PIECE * 3 // 2, ko)
    block = pl.BlockSpec((rows, width), lambda i, feat: (chunk_of((first + i) // 2, feat[0]) * 2 + (first + i) % 2, 0))
    return pl.pallas_call(
        kernel,
        out_shape=[jax.ShapeDtypeStruct(piece, jnp.float32)] * count + extra,
        grid_spec=pltpu.PrefetchScalarGridSpec(
            num_scalar_prefetch=1,
            grid=(count,),
            in_specs=[block, block] + [whole(x.shape) for x in operands],
            out_specs=[whole(piece)] * count + [whole(x.shape) for x in extra],
        ),
        cost_estimate=pl.CostEstimate(
            flops=count * rows * width * ko * 4,
            bytes_accessed=count * rows * (width * 4 + ko * 6),
            transcendentals=0,
        ),
        compiler_params=pltpu.CompilerParams(vmem_limit_bytes=SMALL),
        name="project",
    )(feat, acts, grads, *operands)


def lang_kernel(me_ref, held_ref, lang_ref, *refs):
    *square_refs, other_ref = refs[:5]
    own_refs = refs[5:]
    count = len(own_refs)
    rows, width = held_ref.shape
    piece = width // (2 * count)
    hit = lang_ref[...] == lax.broadcasted_iota(jnp.int32, (LANGS, rows), 0)
    hit = jnp.where(hit, 1.0, 0.0)
    hit = jnp.concatenate([hit, hit], axis=1).astype(jnp.bfloat16)
    inverse = lax.rsqrt(sum(ref[...] for ref in square_refs) + 1e-06)

    def sums(part):
        columns = pl.ds(pl.multiple_of(part * piece, piece), piece)
        unit = held_ref[:, columns] * inverse
        high = unit.astype(jnp.bfloat16)
        rest = (unit - high.astype(jnp.float32)).astype(jnp.bfloat16)
        both = jnp.concatenate([high, rest], axis=0)
        return jnp.dot(hit, both, preferred_element_type=jnp.float32)

    for index in range(count):
        other_ref[index] = sums(me_ref[0] ^ 1 ^ (2 * index))
        own_refs[index][...] = sums(me_ref[0] ^ (2 * index))


def lang_parts(me, held, squares, lang, n_ex):
    rows, width = held.shape
    piece = width // n_ex
    half = n_ex // 2
    return pl.pallas_call(
        lang_kernel,
        out_shape=[jax.ShapeDtypeStruct((half, LANGS, piece), jnp.float32)]
        + [jax.ShapeDtypeStruct((LANGS, piece), jnp.float32)] * half,
        in_specs=[SMEM] + [VMEM] * 6,
        out_specs=[VMEM] * (1 + half),
        compiler_params=pltpu.CompilerParams(vmem_limit_bytes=SMALL),
        name="lang_parts",
    )(me, held, lang.reshape(1, rows), *squares)


def product_kernel(middle_ref, own_ref, end_ref, near_ref, o_ref, square_ref, grad_ref):
    middle = middle_ref[0] == 1
    rows = own_ref.shape[1] * 2 // 3
    seq = rows // UNIT
    wide = own_ref.shape[2]
    low = lax.broadcasted_iota(jnp.int32, (seq, wide), 1) < wide // 2

    def split(x, order):
        high = x.astype(jnp.bfloat16)
        rest = (x - high.astype(jnp.float32)).astype(jnp.bfloat16)
        return jnp.concatenate([high, rest, high] if order else [high, high, rest], axis=0)

    def total(unit, start):
        block = (unit, pl.ds(start, seq), slice(None))
        return own_ref[block] + end_ref[block] + jnp.where(middle, near_ref[block], 0.0)

    for unit in range(PIECE):
        for pair in range(UNIT // 2):
            both = total(unit, rows + pair * seq)
            turned = pltpu.roll(both, wide // 2, 1)
            for side in range(2):
                example = pair + side * (UNIT // 2)
                rank = jnp.where(low, turned, both) if side else jnp.where(low, both, turned)
                grad_ref[unit * UNIT + example] = lax.dot_general(
                    split(total(unit, example * seq), True),
                    split(rank, False),
                    (((0,), (0,)), ((), ())),
                    preferred_element_type=jnp.float32,
                )
    count = PIECE * UNIT
    low = lax.broadcasted_iota(jnp.int32, (count, wide), 1) < wide // 2
    square = jnp.zeros((count, 2 * wide), jnp.float32)
    for index in range(o_ref.shape[0]):
        rows_of = [grad_ref[:, 4 * index + j, :] for j in range(4)]
        part = jnp.concatenate(
            [jnp.where(low, rows_of[0], rows_of[1]), jnp.where(low, rows_of[2], rows_of[3])], axis=1
        )
        square += part * part
        rest = part - part.astype(jnp.bfloat16).astype(jnp.float32)
        o_ref[index] = jnp.concatenate([part, rest], axis=0).astype(jnp.bfloat16)
    square_ref[...] = jnp.sum(square, axis=1, keepdims=True)


def product(middle, parts):
    count, wide = PIECE * UNIT, parts[0].shape[2]
    return pl.pallas_call(
        product_kernel,
        out_shape=[
            jax.ShapeDtypeStruct((wide // 4, 2 * count, 2 * wide), jnp.bfloat16),
            jax.ShapeDtypeStruct((count, 1), jnp.float32),
        ],
        in_specs=[SMEM] + [VMEM] * len(parts),
        out_specs=[VMEM] * 2,
        scratch_shapes=[pltpu.VMEM((count, wide, wide), jnp.float32)],
        compiler_params=pltpu.CompilerParams(vmem_limit_bytes=SMALL),
        name="product",
    )(middle, *parts)


def split_kernel(feat_ref, ex_ref, *refs):
    *lang_refs, o_ref = refs
    feat, ex = feat_ref[0], ex_ref[0]
    middle = (feat == 1) | (feat == 2)
    second = feat ^ jnp.where(middle, 3, 2)
    rows_from = [feat, feat ^ 1, second, second ^ 1]
    n_ex = len(lang_refs)
    masks = [*range(0, n_ex, 2), *range(1, n_ex, 2)]
    for j, ref in enumerate(lang_refs):
        for m in range(4):
            lang = ref[m]
            rest = lang - lang.astype(jnp.bfloat16).astype(jnp.float32)
            o_ref[rows_from[m] * n_ex + (ex ^ masks[j])] = jnp.concatenate([lang, rest], axis=0).astype(jnp.bfloat16)


def split(feat, ex, langs):
    rows, count, piece = langs[0].shape
    return pl.pallas_call(
        split_kernel,
        out_shape=jax.ShapeDtypeStruct((rows * len(langs), 2 * count, piece), jnp.bfloat16),
        in_specs=[SMEM] * 2 + [VMEM] * len(langs),
        out_specs=VMEM,
        compiler_params=pltpu.CompilerParams(vmem_limit_bytes=SMALL),
        name="split",
    )(feat, ex, *langs)


def score_kernel(middle_ref, lang_ref, grad_a, square_a, *refs, scale):
    *part_refs, o_ref, grad_b, square_b, grad_ref = refs
    product_kernel(middle_ref, *part_refs, grad_b, square_b, grad_ref)
    total = None
    for index in range(lang_ref.shape[0]):
        grad = jnp.concatenate([grad_a[index], grad_b[index]], axis=0)
        term = lax.dot_general(
            grad, lang_ref[index], (((1,), (1,)), ((), ())), preferred_element_type=jnp.float32
        )
        total = term if total is None else total + term
    total = total + pltpu.roll(total, LANGS, 1)
    count = square_a.shape[0]
    for index, square_ref in enumerate([square_a, square_b]):
        start = 2 * count * index
        inner = total[start : start + count, :LANGS] + total[start + count : start + 2 * count, :LANGS]
        o_ref[index * count : (index + 1) * count] = inner * (lax.rsqrt(square_ref[...] + 1e-06) * scale)


def score(middle, langs, first, parts, scale):
    grad, square = first
    operands = [langs, *first, *parts]
    wide = parts[0].shape[2]
    return pl.pallas_call(
        functools.partial(score_kernel, scale=scale),
        out_shape=jax.ShapeDtypeStruct((2 * square.shape[0], LANGS), jnp.float32),
        in_specs=[SMEM] + [VMEM] * len(operands),
        out_specs=VMEM,
        scratch_shapes=[
            pltpu.VMEM(grad.shape, grad.dtype),
            pltpu.VMEM(square.shape, square.dtype),
            pltpu.VMEM((square.shape[0], wide, wide), jnp.float32),
        ],
        compiler_params=pltpu.CompilerParams(vmem_limit_bytes=SMALL),
        name="score",
    )(middle, *operands)


def small(kernel, shape, middle, operands):
    return pl.pallas_call(
        kernel,
        out_shape=jax.ShapeDtypeStruct(shape, jnp.float32),
        in_specs=[SMEM] + [VMEM] * len(operands),
        out_specs=VMEM,
        compiler_params=pltpu.CompilerParams(vmem_limit_bytes=SMALL),
    )(middle, *operands)


def onward_kernel(middle_ref, raw_ref, got_ref, o_ref):
    o_ref[...] = raw_ref[...] + jnp.where(middle_ref[0] == 1, got_ref[...], 0.0)


def stack_kernel(middle_ref, one_ref, two_ref, o_ref):
    del middle_ref
    o_ref[0] = one_ref[...]
    o_ref[1] = two_ref[...]


def join_kernel(middle_ref, pair_ref, inner_ref, outer_ref, o_ref):
    o_ref[:2] = pair_ref[...]
    o_ref[2:] = jnp.where(middle_ref[0] == 1, inner_ref[...], outer_ref[...])


def place_kernel(me_ref, *refs):
    *parts, o_ref = refs
    rows = parts[0].shape[0]
    for mask, ref in enumerate(parts):
        o_ref[pl.ds(pl.multiple_of((me_ref[0] ^ mask) * rows, rows), rows), :] = ref[...]


def place(me, parts):
    rows, columns = parts[0].shape
    return pl.pallas_call(
        place_kernel,
        out_shape=jax.ShapeDtypeStruct((rows * len(parts), columns), jnp.float32),
        in_specs=[SMEM] + [VMEM] * len(parts),
        out_specs=VMEM,
        compiler_params=pltpu.CompilerParams(vmem_limit_bytes=SMALL),
        name="place",
    )(me, *parts)


def swap(x, axis, mask):
    return lax.ppermute(x, axis, [(i, i ^ mask) for i in range(lax.axis_size(axis))])


def after(x, *others):
    return lax.optimization_barrier((x, *others))[0]


def fast(*args):
    return ordered(*args)


def ordered(acts, grads, adapter, rank_sketch, out_sketch, held, perm):
    feat, ex = lax.axis_index("feat"), lax.axis_index("ex")
    n_ex = lax.axis_size("ex")
    _, _, width = acts.shape
    middle = (feat == 1) | (feat == 2)
    me_ex = ex.astype(jnp.int32).reshape(1)
    me_feat = feat.astype(jnp.int32).reshape(1)
    acts2, grads2 = acts.reshape(-1, width), grads.reshape(-1, width)
    adapter, rank_sketch, out_sketch, held_far, acts2, grads2 = (
        pltpu.with_memory_space_constraint(x, pltpu.HBM)
        for x in (adapter, rank_sketch.T, out_sketch, held, acts2, grads2)
    )
    down_like = jax.ShapeDtypeStruct((width, 2 * rank_sketch.shape[0]), jnp.bfloat16)
    square_like = jax.ShapeDtypeStruct((held.shape[0], 1), jnp.float32)
    inward = [(0, 1), (3, 2)]
    inner = [(1, 2), (2, 1), (0, 0), (3, 3)]
    is_middle = middle.astype(jnp.int32).reshape(1)

    def onward(raw, got):
        return small(onward_kernel, raw.shape, is_middle, [raw, got])

    raw0_a, down, own_square = project(
        first_kernel, me_feat, 0, 1, acts2, grads2, [adapter, rank_sketch, out_sketch, held_far], [down_like, square_like]
    )
    got1 = [swap(raw0_a, "feat", 1)]
    squares = [own_square] + [swap(own_square, "feat", mask) for mask in (1, 2, 3)]
    raw0_b, *raw1 = project(more_kernel, me_feat, 1, 3, acts2, grads2, [down, out_sketch], [])
    got1.append(swap(raw0_b, "feat", 1))
    got2 = [swap(raw1[0], "feat", 1)]
    sent1 = [onward(after(raw0_a, raw1[1]), got1[0])]
    far = [lax.ppermute(sent1[0], "feat", inner)]

    squares[1:] = [after(x, sent1[0]) for x in squares[1:]]
    other, *parts = lang_parts(me_ex, held, squares, perm % LANGS, n_ex)
    other = swap(other, "ex", 1)
    parts = [x + other[i] for i, x in enumerate(parts)]
    scattered = [swap(parts[i], "ex", 2 * i) for i in range(1, n_ex // 2)]
    sent1.append(onward(after(raw0_b, parts[0]), got1[1]))
    far.append(lax.ppermute(sent1[1], "feat", inner))
    lang = after(parts[0], sent1[1]) + sum(scattered)
    other = swap(lang, "feat", 1)
    got2.append(lax.ppermute(after(raw1[1], lang), "feat", inward))
    raw2 = project(more_kernel, me_feat, 4, 2, acts2, grads2, [after(down, lang), out_sketch], [])
    pair = small(stack_kernel, (2, *lang.shape), is_middle, [lang, after(other, raw2[0])])
    far_pair = [lax.ppermute(pair, "feat", pairs) for pairs in (inner, [(1, 3), (2, 0)])]
    sent2 = [onward(after(raw1[0], pair), got2[0])]
    near = [lax.ppermute(sent2[0], "feat", inner)]
    sent3 = [onward(after(raw2[0], sent2[0]), far[0])]
    got3 = [swap(sent3[0], "feat", 1)]
    pair = after(pair, sent3[0])
    langs = [small(join_kernel, (4, *lang.shape), is_middle, [pair, *far_pair])]
    langs = langs + [swap(langs[0], "ex", mask) for mask in range(2, n_ex, 2)]
    sent3.append(onward(after(raw2[1], langs[0]), far[1]))
    got3.append(swap(sent3[1], "feat", 1))
    sent2.append(onward(after(raw1[1], sent3[1]), got2[1]))
    near.append(lax.ppermute(sent2[1], "feat", inner))
    own_a, own_b = project(more_kernel, me_feat, 6, 2, acts2, grads2, [after(down, sent2[1]), out_sketch], [])
    grad_a, square_a = product(is_middle, [own_a, got3[0], near[0]])
    langs[1:] = [after(x, square_a) for x in langs[1:]]
    langs = langs + [swap(x, "ex", 1) for x in langs]
    per_lang = perm.shape[0] * n_ex // LANGS
    scale = (KF * per_lang) ** 0.5 / per_lang
    halves = split(me_feat, me_ex, langs)
    late = [after(got3[1], halves), after(near[1], halves)]
    mine = score(is_middle, halves, [grad_a, square_a], [own_b, *late], scale)
    gathered = [mine]
    for mask in (1, 2, 3):
        gathered.append(swap(mine, "feat", mask))
    return place(me_feat, gathered)


def general(acts, grads, adapter, rank_sketch, out_sketch, held, perm):
    ex_dev = acts.shape[0]
    down = jnp.dot(adapter, rank_sketch, preferred_element_type=jnp.float32).astype(jnp.bfloat16)
    rank_part = jnp.einsum("esd,dr->esr", acts, down, preferred_element_type=jnp.float32)
    rank_side = lax.psum(rank_part, "feat")
    out_part = jnp.einsum("esd,dk->esk", grads, out_sketch, preferred_element_type=jnp.float32)
    out_side = lax.psum_scatter(out_part, "feat", scatter_dimension=2, tiled=True)
    grad = jnp.einsum("esk,esr->ekr", out_side, rank_side, precision=HIGHEST).reshape(ex_dev, -1)
    squares = lax.psum(jnp.sum(held * held, axis=1), "feat")
    unit = held * lax.rsqrt(squares + 1e-06)[:, None]
    onehot = ((perm % LANGS)[:, None] == jnp.arange(LANGS, dtype=jnp.int32)[None, :]).astype(jnp.float32)
    per_lang = perm.shape[0] * lax.axis_size("ex") // LANGS
    lang_mean = lax.psum(jnp.dot(onehot.T, unit, precision=HIGHEST), "ex") / per_lang
    inner, norm = lax.psum(
        (jnp.dot(grad, lang_mean.T, precision=HIGHEST), jnp.sum(grad * grad, axis=1)), "feat"
    )
    scale = jnp.sqrt(jnp.float32(KF * per_lang))
    return scale * inner * lax.rsqrt(norm + 1e-06)[:, None]


def solution(mesh):
    placed = (
        P("ex", None, "feat"),
        P("ex", None, "feat"),
        P("feat", None),
        P(),
        P("feat", None),
        P("ex", "feat"),
        P("ex"),
    )
    is_fast = mesh.shape["feat"] == 4 and mesh.shape["ex"] == 8
    body = fast if is_fast else general
    return jax.shard_map(body, mesh=mesh, in_specs=placed, out_specs=P("ex", None), check_vma=False)
```

```python
import functools

import jax
import jax.numpy as jnp
from jax import lax
from jax.experimental import pallas as pl
from jax.experimental.pallas import tpu as pltpu
from jax.sharding import PartitionSpec as P


KF = 8192
LANGS = 64
UNIT = 4
PIECE = 2
PIECES = 8
HIGHEST = lax.Precision.HIGHEST
SMALL = 24 * 1024 * 1024
VMEM = pl.BlockSpec(memory_space=pltpu.VMEM)
SMEM = pl.BlockSpec(memory_space=pltpu.SMEM)


def project_piece(act, grad, down, sketch, o_ref):
    rows = act.shape[0] // PIECE
    half = rows // 2
    out = jnp.dot(grad, sketch, preferred_element_type=jnp.float32)
    rank = jnp.dot(act, down, preferred_element_type=jnp.float32)
    low = lax.broadcasted_iota(jnp.int32, (half, down.shape[1]), 1) < down.shape[1] // 2
    for unit in range(PIECE):
        start = unit * rows
        o_ref[unit, :rows, :] = out[start : start + rows]
        o_ref[unit, rows:, :] = jnp.where(low, rank[start : start + half], rank[start + half : start + rows])


def first_kernel(feat, act_ref, grad_ref, adapter_ref, rank_ref, sketch_ref, held_ref, *o_refs):
    del feat
    *piece_refs, down_ref, square_ref = o_refs
    step = pl.program_id(0)

    @pl.when(step == 0)
    def _():
        down = lax.dot_general(
            adapter_ref[...], rank_ref[...], (((1,), (1,)), ((), ())), preferred_element_type=jnp.float32
        )
        down_ref[...] = jnp.concatenate([down, down], axis=1).astype(jnp.bfloat16)
        held = held_ref[...]
        square_ref[...] = jnp.sum(held * held, axis=1, keepdims=True)

    for index, ref in enumerate(piece_refs):

        @pl.when(step == index)
        def _(ref=ref):
            project_piece(act_ref[...], grad_ref[...], down_ref[...], sketch_ref[...], ref)


def more_kernel(feat, act_ref, grad_ref, down_ref, sketch_ref, *piece_refs):
    del feat
    step = pl.program_id(0)
    for index, ref in enumerate(piece_refs):

        @pl.when(step == index)
        def _(ref=ref):
            project_piece(act_ref[...], grad_ref[...], down_ref[...], sketch_ref[...], ref)


def whole(shape):
    return pl.BlockSpec(shape, lambda i, feat: (0,) * len(shape))


def chunk_of(turn, feat):
    left = feat < 2
    far, near = jnp.where(left, 3, 0), jnp.where(left, 2, 1)
    return jnp.where(turn == 0, far, jnp.where(turn == 1, near, jnp.where(turn == 2, feat ^ 1, feat)))


def project(kernel, feat, first, count, acts, grads, operands, extra):
    ko = operands[-1 if kernel is more_kernel else 2].shape[1]
    width = acts.shape[1]
    rows = acts.shape[0] // PIECES
    piece = (PIECE, rows // PIECE * 3 // 2, ko)
    block = pl.BlockSpec((rows, width), lambda i, feat: (chunk_of((first + i) // 2, feat[0]) * 2 + (first + i) % 2, 0))
    return pl.pallas_call(
        kernel,
        out_shape=[jax.ShapeDtypeStruct(piece, jnp.float32)] * count + extra,
        grid_spec=pltpu.PrefetchScalarGridSpec(
            num_scalar_prefetch=1,
            grid=(count,),
            in_specs=[block, block] + [whole(x.shape) for x in operands],
            out_specs=[whole(piece)] * count + [whole(x.shape) for x in extra],
        ),
        cost_estimate=pl.CostEstimate(
            flops=count * rows * width * ko * 4,
            bytes_accessed=count * rows * (width * 4 + ko * 6),
            transcendentals=0,
        ),
        compiler_params=pltpu.CompilerParams(vmem_limit_bytes=SMALL),
        name="project",
    )(feat, acts, grads, *operands)


def lang_kernel(me_ref, held_ref, lang_ref, *refs):
    *square_refs, other_ref = refs[:5]
    own_refs = refs[5:]
    count = len(own_refs)
    rows, width = held_ref.shape
    piece = width // (2 * count)
    hit = lang_ref[...] == lax.broadcasted_iota(jnp.int32, (LANGS, rows), 0)
    hit = jnp.where(hit, 1.0, 0.0)
    hit = jnp.concatenate([hit, hit], axis=1).astype(jnp.bfloat16)
    inverse = lax.rsqrt(sum(ref[...] for ref in square_refs) + 1e-06)

    def sums(part):
        columns = pl.ds(pl.multiple_of(part * piece, piece), piece)
        unit = held_ref[:, columns] * inverse
        high = unit.astype(jnp.bfloat16)
        rest = (unit - high.astype(jnp.float32)).astype(jnp.bfloat16)
        both = jnp.concatenate([high, rest], axis=0)
        return jnp.dot(hit, both, preferred_element_type=jnp.float32)

    for index in range(count):
        other_ref[index] = sums(me_ref[0] ^ 1 ^ (2 * index))
        own_refs[index][...] = sums(me_ref[0] ^ (2 * index))


def lang_parts(me, held, squares, lang, n_ex):
    rows, width = held.shape
    piece = width // n_ex
    half = n_ex // 2
    return pl.pallas_call(
        lang_kernel,
        out_shape=[jax.ShapeDtypeStruct((half, LANGS, piece), jnp.float32)]
        + [jax.ShapeDtypeStruct((LANGS, piece), jnp.float32)] * half,
        in_specs=[SMEM] + [VMEM] * 6,
        out_specs=[VMEM] * (1 + half),
        compiler_params=pltpu.CompilerParams(vmem_limit_bytes=SMALL),
        name="lang_parts",
    )(me, held, lang.reshape(1, rows), *squares)


def product_kernel(middle_ref, own_ref, end_ref, near_ref, o_ref, square_ref, grad_ref):
    middle = middle_ref[0] == 1
    rows = own_ref.shape[1] * 2 // 3
    seq = rows // UNIT
    wide = own_ref.shape[2]
    low = lax.broadcasted_iota(jnp.int32, (seq, wide), 1) < wide // 2

    def split(x, order):
        high = x.astype(jnp.bfloat16)
        rest = (x - high.astype(jnp.float32)).astype(jnp.bfloat16)
        return jnp.concatenate([high, rest, high] if order else [high, high, rest], axis=0)

    def total(unit, start):
        block = (unit, pl.ds(start, seq), slice(None))
        return own_ref[block] + end_ref[block] + jnp.where(middle, near_ref[block], 0.0)

    for unit in range(PIECE):
        for pair in range(UNIT // 2):
            both = total(unit, rows + pair * seq)
            turned = pltpu.roll(both, wide // 2, 1)
            for side in range(2):
                example = pair + side * (UNIT // 2)
                rank = jnp.where(low, turned, both) if side else jnp.where(low, both, turned)
                grad_ref[unit * UNIT + example] = lax.dot_general(
                    split(total(unit, example * seq), True),
                    split(rank, False),
                    (((0,), (0,)), ((), ())),
                    preferred_element_type=jnp.float32,
                )
    count = PIECE * UNIT
    low = lax.broadcasted_iota(jnp.int32, (count, wide), 1) < wide // 2
    square = jnp.zeros((count, 2 * wide), jnp.float32)
    for index in range(o_ref.shape[0]):
        rows_of = [grad_ref[:, 4 * index + j, :] for j in range(4)]
        part = jnp.concatenate(
            [jnp.where(low, rows_of[0], rows_of[1]), jnp.where(low, rows_of[2], rows_of[3])], axis=1
        )
        square += part * part
        rest = part - part.astype(jnp.bfloat16).astype(jnp.float32)
        o_ref[index] = jnp.concatenate([part, rest], axis=0).astype(jnp.bfloat16)
    square_ref[...] = jnp.sum(square, axis=1, keepdims=True)


def product(middle, parts):
    count, wide = PIECE * UNIT, parts[0].shape[2]
    return pl.pallas_call(
        product_kernel,
        out_shape=[
            jax.ShapeDtypeStruct((wide // 4, 2 * count, 2 * wide), jnp.bfloat16),
            jax.ShapeDtypeStruct((count, 1), jnp.float32),
        ],
        in_specs=[SMEM] + [VMEM] * len(parts),
        out_specs=[VMEM] * 2,
        scratch_shapes=[pltpu.VMEM((count, wide, wide), jnp.float32)],
        compiler_params=pltpu.CompilerParams(vmem_limit_bytes=SMALL),
        name="product",
    )(middle, *parts)


def split_kernel(feat_ref, ex_ref, *refs):
    *lang_refs, o_ref = refs
    feat, ex = feat_ref[0], ex_ref[0]
    middle = (feat == 1) | (feat == 2)
    second = feat ^ jnp.where(middle, 3, 2)
    rows_from = [feat, feat ^ 1, second, second ^ 1]
    n_ex = len(lang_refs)
    masks = [*range(0, n_ex, 2), *range(1, n_ex, 2)]
    for j, ref in enumerate(lang_refs):
        for m in range(4):
            lang = ref[m]
            rest = lang - lang.astype(jnp.bfloat16).astype(jnp.float32)
            o_ref[rows_from[m] * n_ex + (ex ^ masks[j])] = jnp.concatenate([lang, rest], axis=0).astype(jnp.bfloat16)


def split(feat, ex, langs):
    rows, count, piece = langs[0].shape
    return pl.pallas_call(
        split_kernel,
        out_shape=jax.ShapeDtypeStruct((rows * len(langs), 2 * count, piece), jnp.bfloat16),
        in_specs=[SMEM] * 2 + [VMEM] * len(langs),
        out_specs=VMEM,
        compiler_params=pltpu.CompilerParams(vmem_limit_bytes=SMALL),
        name="split",
    )(feat, ex, *langs)


def score_kernel(middle_ref, lang_ref, grad_a, square_a, *refs, scale):
    *part_refs, o_ref, grad_b, square_b, grad_ref = refs
    product_kernel(middle_ref, *part_refs, grad_b, square_b, grad_ref)
    total = None
    for index in range(lang_ref.shape[0]):
        grad = jnp.concatenate([grad_a[index], grad_b[index]], axis=0)
        term = lax.dot_general(
            grad, lang_ref[index], (((1,), (1,)), ((), ())), preferred_element_type=jnp.float32
        )
        total = term if total is None else total + term
    total = total + pltpu.roll(total, LANGS, 1)
    count = square_a.shape[0]
    for index, square_ref in enumerate([square_a, square_b]):
        start = 2 * count * index
        inner = total[start : start + count, :LANGS] + total[start + count : start + 2 * count, :LANGS]
        o_ref[index * count : (index + 1) * count] = inner * (lax.rsqrt(square_ref[...] + 1e-06) * scale)


def score(middle, langs, first, parts, scale):
    grad, square = first
    operands = [langs, *first, *parts]
    wide = parts[0].shape[2]
    return pl.pallas_call(
        functools.partial(score_kernel, scale=scale),
        out_shape=jax.ShapeDtypeStruct((2 * square.shape[0], LANGS), jnp.float32),
        in_specs=[SMEM] + [VMEM] * len(operands),
        out_specs=VMEM,
        scratch_shapes=[
            pltpu.VMEM(grad.shape, grad.dtype),
            pltpu.VMEM(square.shape, square.dtype),
            pltpu.VMEM((square.shape[0], wide, wide), jnp.float32),
        ],
        compiler_params=pltpu.CompilerParams(vmem_limit_bytes=SMALL),
        name="score",
    )(middle, *operands)


def small(kernel, shape, middle, operands):
    return pl.pallas_call(
        kernel,
        out_shape=jax.ShapeDtypeStruct(shape, jnp.float32),
        in_specs=[SMEM] + [VMEM] * len(operands),
        out_specs=VMEM,
        compiler_params=pltpu.CompilerParams(vmem_limit_bytes=SMALL),
    )(middle, *operands)


def onward_kernel(middle_ref, raw_ref, got_ref, o_ref):
    o_ref[...] = raw_ref[...] + jnp.where(middle_ref[0] == 1, got_ref[...], 0.0)


def stack_kernel(middle_ref, one_ref, two_ref, o_ref):
    del middle_ref
    o_ref[0] = one_ref[...]
    o_ref[1] = two_ref[...]


def join_kernel(middle_ref, pair_ref, inner_ref, outer_ref, o_ref):
    o_ref[:2] = pair_ref[...]
    o_ref[2:] = jnp.where(middle_ref[0] == 1, inner_ref[...], outer_ref[...])


def place_kernel(me_ref, *refs):
    *parts, o_ref = refs
    rows = parts[0].shape[0]
    for mask, ref in enumerate(parts):
        o_ref[pl.ds(pl.multiple_of((me_ref[0] ^ mask) * rows, rows), rows), :] = ref[...]


def place(me, parts):
    rows, columns = parts[0].shape
    return pl.pallas_call(
        place_kernel,
        out_shape=jax.ShapeDtypeStruct((rows * len(parts), columns), jnp.float32),
        in_specs=[SMEM] + [VMEM] * len(parts),
        out_specs=VMEM,
        compiler_params=pltpu.CompilerParams(vmem_limit_bytes=SMALL),
        name="place",
    )(me, *parts)


def swap(x, axis, mask):
    return lax.ppermute(x, axis, [(i, i ^ mask) for i in range(lax.axis_size(axis))])


def after(x, *others):
    return lax.optimization_barrier((x, *others))[0]


def fast(*args):
    return ordered(*args)


def ordered(acts, grads, adapter, rank_sketch, out_sketch, held, perm):
    feat, ex = lax.axis_index("feat"), lax.axis_index("ex")
    n_ex = lax.axis_size("ex")
    _, _, width = acts.shape
    middle = (feat == 1) | (feat == 2)
    me_ex = ex.astype(jnp.int32).reshape(1)
    me_feat = feat.astype(jnp.int32).reshape(1)
    acts2, grads2 = acts.reshape(-1, width), grads.reshape(-1, width)
    adapter, rank_sketch, out_sketch, held_far, acts2, grads2 = (
        pltpu.with_memory_space_constraint(x, pltpu.HBM)
        for x in (adapter, rank_sketch.T, out_sketch, held, acts2, grads2)
    )
    down_like = jax.ShapeDtypeStruct((width, 2 * rank_sketch.shape[0]), jnp.bfloat16)
    square_like = jax.ShapeDtypeStruct((held.shape[0], 1), jnp.float32)
    inward = [(0, 1), (3, 2)]
    inner = [(1, 2), (2, 1), (0, 0), (3, 3)]
    is_middle = middle.astype(jnp.int32).reshape(1)

    def onward(raw, got):
        return small(onward_kernel, raw.shape, is_middle, [raw, got])

    raw0_a, down, own_square = project(
        first_kernel, me_feat, 0, 1, acts2, grads2, [adapter, rank_sketch, out_sketch, held_far], [down_like, square_like]
    )
    got1 = [swap(raw0_a, "feat", 1)]
    squares = [own_square] + [swap(own_square, "feat", mask) for mask in (1, 2, 3)]
    raw0_b, *raw1 = project(more_kernel, me_feat, 1, 3, acts2, grads2, [down, out_sketch], [])
    got1.append(swap(raw0_b, "feat", 1))
    got2 = [swap(raw1[0], "feat", 1)]
    sent1 = [onward(after(raw0_a, raw1[1]), got1[0])]
    far = [lax.ppermute(sent1[0], "feat", inner)]

    squares[1:] = [after(x, sent1[0]) for x in squares[1:]]
    other, *parts = lang_parts(me_ex, held, squares, perm % LANGS, n_ex)
    other = swap(other, "ex", 1)
    parts = [x + other[i] for i, x in enumerate(parts)]
    scattered = [swap(parts[i], "ex", 2 * i) for i in range(1, n_ex // 2)]
    raw2 = project(more_kernel, me_feat, 4, 2, acts2, grads2, [after(down, parts[0]), out_sketch], [])
    sent1.append(onward(after(raw0_b, raw2[0]), got1[1]))
    far.append(lax.ppermute(sent1[1], "feat", inner))
    lang = after(parts[0], sent1[1]) + sum(scattered)
    other = swap(lang, "feat", 1)
    got2.append(lax.ppermute(after(raw1[1], lang), "feat", inward))
    sent3 = [onward(after(raw2[0], lang), far[0])]
    got3 = [swap(sent3[0], "feat", 1)]
    pair = small(stack_kernel, (2, *lang.shape), is_middle, [lang, after(other, sent3[0])])
    far_pair = [lax.ppermute(pair, "feat", pairs) for pairs in (inner, [(1, 3), (2, 0)])]
    sent2 = [onward(after(raw1[0], pair), got2[0])]
    near = [lax.ppermute(sent2[0], "feat", inner)]
    pair = after(pair, sent2[0])
    langs = [small(join_kernel, (4, *lang.shape), is_middle, [pair, *far_pair])]
    langs = langs + [swap(langs[0], "ex", mask) for mask in range(2, n_ex, 2)]
    sent3.append(onward(after(raw2[1], langs[0]), far[1]))
    got3.append(swap(sent3[1], "feat", 1))
    sent2.append(onward(after(raw1[1], sent3[1]), got2[1]))
    near.append(lax.ppermute(sent2[1], "feat", inner))
    own_a, own_b = project(more_kernel, me_feat, 6, 2, acts2, grads2, [after(down, sent2[1]), out_sketch], [])
    grad_a, square_a = product(is_middle, [own_a, got3[0], near[0]])
    langs[1:] = [after(x, square_a) for x in langs[1:]]
    langs = langs + [swap(x, "ex", 1) for x in langs]
    per_lang = perm.shape[0] * n_ex // LANGS
    scale = (KF * per_lang) ** 0.5 / per_lang
    halves = split(me_feat, me_ex, langs)
    late = [after(got3[1], halves), after(near[1], halves)]
    mine = score(is_middle, halves, [grad_a, square_a], [own_b, *late], scale)
    gathered = [mine]
    for mask in (1, 2, 3):
        gathered.append(swap(mine, "feat", mask))
    return place(me_feat, gathered)


def general(acts, grads, adapter, rank_sketch, out_sketch, held, perm):
    ex_dev = acts.shape[0]
    down = jnp.dot(adapter, rank_sketch, preferred_element_type=jnp.float32).astype(jnp.bfloat16)
    rank_part = jnp.einsum("esd,dr->esr", acts, down, preferred_element_type=jnp.float32)
    rank_side = lax.psum(rank_part, "feat")
    out_part = jnp.einsum("esd,dk->esk", grads, out_sketch, preferred_element_type=jnp.float32)
    out_side = lax.psum_scatter(out_part, "feat", scatter_dimension=2, tiled=True)
    grad = jnp.einsum("esk,esr->ekr", out_side, rank_side, precision=HIGHEST).reshape(ex_dev, -1)
    squares = lax.psum(jnp.sum(held * held, axis=1), "feat")
    unit = held * lax.rsqrt(squares + 1e-06)[:, None]
    onehot = ((perm % LANGS)[:, None] == jnp.arange(LANGS, dtype=jnp.int32)[None, :]).astype(jnp.float32)
    per_lang = perm.shape[0] * lax.axis_size("ex") // LANGS
    lang_mean = lax.psum(jnp.dot(onehot.T, unit, precision=HIGHEST), "ex") / per_lang
    inner, norm = lax.psum(
        (jnp.dot(grad, lang_mean.T, precision=HIGHEST), jnp.sum(grad * grad, axis=1)), "feat"
    )
    scale = jnp.sqrt(jnp.float32(KF * per_lang))
    return scale * inner * lax.rsqrt(norm + 1e-06)[:, None]


def solution(mesh):
    placed = (
        P("ex", None, "feat"),
        P("ex", None, "feat"),
        P("feat", None),
        P(),
        P("feat", None),
        P("ex", "feat"),
        P("ex"),
    )
    is_fast = mesh.shape["feat"] == 4 and mesh.shape["ex"] == 8
    body = fast if is_fast else general
    return jax.shard_map(body, mesh=mesh, in_specs=placed, out_specs=P("ex", None), check_vma=False)
```

```python
import functools

import jax
import jax.numpy as jnp
from jax import lax
from jax.experimental import pallas as pl
from jax.experimental.pallas import tpu as pltpu
from jax.sharding import PartitionSpec as P


KF = 8192
LANGS = 64
UNIT = 4
PIECE = 2
PIECES = 8
HIGHEST = lax.Precision.HIGHEST
SMALL = 24 * 1024 * 1024
VMEM = pl.BlockSpec(memory_space=pltpu.VMEM)
SMEM = pl.BlockSpec(memory_space=pltpu.SMEM)


def project_piece(act, grad, down, sketch, o_ref):
    rows = act.shape[0] // PIECE
    half = rows // 2
    out = jnp.dot(grad, sketch, preferred_element_type=jnp.float32)
    rank = jnp.dot(act, down, preferred_element_type=jnp.float32)
    low = lax.broadcasted_iota(jnp.int32, (half, down.shape[1]), 1) < down.shape[1] // 2
    for unit in range(PIECE):
        start = unit * rows
        o_ref[unit, :rows, :] = out[start : start + rows]
        o_ref[unit, rows:, :] = jnp.where(low, rank[start : start + half], rank[start + half : start + rows])


def first_kernel(feat, act_ref, grad_ref, adapter_ref, rank_ref, sketch_ref, held_ref, *o_refs):
    del feat
    *piece_refs, down_ref, square_ref = o_refs
    step = pl.program_id(0)

    @pl.when(step == 0)
    def _():
        down = lax.dot_general(
            adapter_ref[...], rank_ref[...], (((1,), (1,)), ((), ())), preferred_element_type=jnp.float32
        )
        down_ref[...] = jnp.concatenate([down, down], axis=1).astype(jnp.bfloat16)
        held = held_ref[...]
        square_ref[...] = jnp.sum(held * held, axis=1, keepdims=True)

    for index, ref in enumerate(piece_refs):

        @pl.when(step == index)
        def _(ref=ref):
            project_piece(act_ref[...], grad_ref[...], down_ref[...], sketch_ref[...], ref)


def more_kernel(feat, act_ref, grad_ref, down_ref, sketch_ref, *piece_refs):
    del feat
    step = pl.program_id(0)
    for index, ref in enumerate(piece_refs):

        @pl.when(step == index)
        def _(ref=ref):
            project_piece(act_ref[...], grad_ref[...], down_ref[...], sketch_ref[...], ref)


def whole(shape):
    return pl.BlockSpec(shape, lambda i, feat: (0,) * len(shape))


def chunk_of(turn, feat):
    left = feat < 2
    far, near = jnp.where(left, 3, 0), jnp.where(left, 2, 1)
    return jnp.where(turn == 0, far, jnp.where(turn == 1, near, jnp.where(turn == 2, feat ^ 1, feat)))


def project(kernel, feat, first, count, acts, grads, operands, extra):
    ko = operands[-1 if kernel is more_kernel else 2].shape[1]
    width = acts.shape[1]
    rows = acts.shape[0] // PIECES
    piece = (PIECE, rows // PIECE * 3 // 2, ko)
    block = pl.BlockSpec((rows, width), lambda i, feat: (chunk_of((first + i) // 2, feat[0]) * 2 + (first + i) % 2, 0))
    return pl.pallas_call(
        kernel,
        out_shape=[jax.ShapeDtypeStruct(piece, jnp.float32)] * count + extra,
        grid_spec=pltpu.PrefetchScalarGridSpec(
            num_scalar_prefetch=1,
            grid=(count,),
            in_specs=[block, block] + [whole(x.shape) for x in operands],
            out_specs=[whole(piece)] * count + [whole(x.shape) for x in extra],
        ),
        cost_estimate=pl.CostEstimate(
            flops=count * rows * width * ko * 4,
            bytes_accessed=count * rows * (width * 4 + ko * 6),
            transcendentals=0,
        ),
        compiler_params=pltpu.CompilerParams(vmem_limit_bytes=SMALL),
        name="project",
    )(feat, acts, grads, *operands)


def lang_kernel(me_ref, held_ref, lang_ref, *refs):
    *square_refs, other_ref = refs[:5]
    own_refs = refs[5:]
    count = len(own_refs)
    rows, width = held_ref.shape
    piece = width // (2 * count)
    hit = lang_ref[...] == lax.broadcasted_iota(jnp.int32, (LANGS, rows), 0)
    hit = jnp.where(hit, 1.0, 0.0)
    hit = jnp.concatenate([hit, hit], axis=1).astype(jnp.bfloat16)
    inverse = lax.rsqrt(sum(ref[...] for ref in square_refs) + 1e-06)

    def sums(part):
        columns = pl.ds(pl.multiple_of(part * piece, piece), piece)
        unit = held_ref[:, columns] * inverse
        high = unit.astype(jnp.bfloat16)
        rest = (unit - high.astype(jnp.float32)).astype(jnp.bfloat16)
        both = jnp.concatenate([high, rest], axis=0)
        return jnp.dot(hit, both, preferred_element_type=jnp.float32)

    for index in range(count):
        other_ref[index] = sums(me_ref[0] ^ 1 ^ (2 * index))
        own_refs[index][...] = sums(me_ref[0] ^ (2 * index))


def lang_parts(me, held, squares, lang, n_ex):
    rows, width = held.shape
    piece = width // n_ex
    half = n_ex // 2
    return pl.pallas_call(
        lang_kernel,
        out_shape=[jax.ShapeDtypeStruct((half, LANGS, piece), jnp.float32)]
        + [jax.ShapeDtypeStruct((LANGS, piece), jnp.float32)] * half,
        in_specs=[SMEM] + [VMEM] * 6,
        out_specs=[VMEM] * (1 + half),
        compiler_params=pltpu.CompilerParams(vmem_limit_bytes=SMALL),
        name="lang_parts",
    )(me, held, lang.reshape(1, rows), *squares)


def product_kernel(middle_ref, own_ref, end_ref, near_ref, o_ref, square_ref, grad_ref):
    middle = middle_ref[0] == 1
    rows = own_ref.shape[1] * 2 // 3
    seq = rows // UNIT
    wide = own_ref.shape[2]
    low = lax.broadcasted_iota(jnp.int32, (seq, wide), 1) < wide // 2

    def split(x, order):
        high = x.astype(jnp.bfloat16)
        rest = (x - high.astype(jnp.float32)).astype(jnp.bfloat16)
        return jnp.concatenate([high, rest, high] if order else [high, high, rest], axis=0)

    def total(unit, start):
        block = (unit, pl.ds(start, seq), slice(None))
        return own_ref[block] + end_ref[block] + jnp.where(middle, near_ref[block], 0.0)

    for unit in range(PIECE):
        for pair in range(UNIT // 2):
            both = total(unit, rows + pair * seq)
            turned = pltpu.roll(both, wide // 2, 1)
            for side in range(2):
                example = pair + side * (UNIT // 2)
                rank = jnp.where(low, turned, both) if side else jnp.where(low, both, turned)
                grad_ref[unit * UNIT + example] = lax.dot_general(
                    split(total(unit, example * seq), True),
                    split(rank, False),
                    (((0,), (0,)), ((), ())),
                    preferred_element_type=jnp.float32,
                )
    count = PIECE * UNIT
    low = lax.broadcasted_iota(jnp.int32, (count, wide), 1) < wide // 2
    square = jnp.zeros((count, 2 * wide), jnp.float32)
    for index in range(o_ref.shape[0]):
        rows_of = [grad_ref[:, 4 * index + j, :] for j in range(4)]
        part = jnp.concatenate(
            [jnp.where(low, rows_of[0], rows_of[1]), jnp.where(low, rows_of[2], rows_of[3])], axis=1
        )
        square += part * part
        rest = part - part.astype(jnp.bfloat16).astype(jnp.float32)
        o_ref[index] = jnp.concatenate([part, rest], axis=0).astype(jnp.bfloat16)
    square_ref[...] = jnp.sum(square, axis=1, keepdims=True)


def product(middle, parts):
    count, wide = PIECE * UNIT, parts[0].shape[2]
    return pl.pallas_call(
        product_kernel,
        out_shape=[
            jax.ShapeDtypeStruct((wide // 4, 2 * count, 2 * wide), jnp.bfloat16),
            jax.ShapeDtypeStruct((count, 1), jnp.float32),
        ],
        in_specs=[SMEM] + [VMEM] * len(parts),
        out_specs=[VMEM] * 2,
        scratch_shapes=[pltpu.VMEM((count, wide, wide), jnp.float32)],
        compiler_params=pltpu.CompilerParams(vmem_limit_bytes=SMALL),
        name="product",
    )(middle, *parts)


def split_kernel(feat_ref, ex_ref, *refs):
    *lang_refs, o_ref = refs
    feat, ex = feat_ref[0], ex_ref[0]
    middle = (feat == 1) | (feat == 2)
    second = feat ^ jnp.where(middle, 3, 2)
    rows_from = [feat, feat ^ 1, second, second ^ 1]
    n_ex = len(lang_refs)
    masks = [*range(0, n_ex, 2), *range(1, n_ex, 2)]
    for j, ref in enumerate(lang_refs):
        for m in range(4):
            lang = ref[m]
            rest = lang - lang.astype(jnp.bfloat16).astype(jnp.float32)
            o_ref[rows_from[m] * n_ex + (ex ^ masks[j])] = jnp.concatenate([lang, rest], axis=0).astype(jnp.bfloat16)


def split(feat, ex, langs):
    rows, count, piece = langs[0].shape
    return pl.pallas_call(
        split_kernel,
        out_shape=jax.ShapeDtypeStruct((rows * len(langs), 2 * count, piece), jnp.bfloat16),
        in_specs=[SMEM] * 2 + [VMEM] * len(langs),
        out_specs=VMEM,
        compiler_params=pltpu.CompilerParams(vmem_limit_bytes=SMALL),
        name="split",
    )(feat, ex, *langs)


def score_kernel(middle_ref, lang_ref, grad_a, square_a, *refs, scale):
    *part_refs, o_ref, grad_b, square_b, grad_ref = refs
    product_kernel(middle_ref, *part_refs, grad_b, square_b, grad_ref)
    total = None
    for index in range(lang_ref.shape[0]):
        grad = jnp.concatenate([grad_a[index], grad_b[index]], axis=0)
        term = lax.dot_general(
            grad, lang_ref[index], (((1,), (1,)), ((), ())), preferred_element_type=jnp.float32
        )
        total = term if total is None else total + term
    total = total + pltpu.roll(total, LANGS, 1)
    count = square_a.shape[0]
    for index, square_ref in enumerate([square_a, square_b]):
        start = 2 * count * index
        inner = total[start : start + count, :LANGS] + total[start + count : start + 2 * count, :LANGS]
        o_ref[index * count : (index + 1) * count] = inner * (lax.rsqrt(square_ref[...] + 1e-06) * scale)


def score(middle, langs, first, parts, scale):
    grad, square = first
    operands = [langs, *first, *parts]
    wide = parts[0].shape[2]
    return pl.pallas_call(
        functools.partial(score_kernel, scale=scale),
        out_shape=jax.ShapeDtypeStruct((2 * square.shape[0], LANGS), jnp.float32),
        in_specs=[SMEM] + [VMEM] * len(operands),
        out_specs=VMEM,
        scratch_shapes=[
            pltpu.VMEM(grad.shape, grad.dtype),
            pltpu.VMEM(square.shape, square.dtype),
            pltpu.VMEM((square.shape[0], wide, wide), jnp.float32),
        ],
        compiler_params=pltpu.CompilerParams(vmem_limit_bytes=SMALL),
        name="score",
    )(middle, *operands)


def small(kernel, shape, middle, operands):
    return pl.pallas_call(
        kernel,
        out_shape=jax.ShapeDtypeStruct(shape, jnp.float32),
        in_specs=[SMEM] + [VMEM] * len(operands),
        out_specs=VMEM,
        compiler_params=pltpu.CompilerParams(vmem_limit_bytes=SMALL),
    )(middle, *operands)


def onward_kernel(middle_ref, raw_ref, got_ref, o_ref):
    o_ref[...] = raw_ref[...] + jnp.where(middle_ref[0] == 1, got_ref[...], 0.0)


def stack_kernel(middle_ref, one_ref, two_ref, o_ref):
    del middle_ref
    o_ref[0] = one_ref[...]
    o_ref[1] = two_ref[...]


def join_kernel(middle_ref, pair_ref, inner_ref, outer_ref, o_ref):
    o_ref[:2] = pair_ref[...]
    o_ref[2:] = jnp.where(middle_ref[0] == 1, inner_ref[...], outer_ref[...])


def place_kernel(me_ref, *refs):
    *parts, o_ref = refs
    rows = parts[0].shape[0]
    for mask, ref in enumerate(parts):
        o_ref[pl.ds(pl.multiple_of((me_ref[0] ^ mask) * rows, rows), rows), :] = ref[...]


def place(me, parts):
    rows, columns = parts[0].shape
    return pl.pallas_call(
        place_kernel,
        out_shape=jax.ShapeDtypeStruct((rows * len(parts), columns), jnp.float32),
        in_specs=[SMEM] + [VMEM] * len(parts),
        out_specs=VMEM,
        compiler_params=pltpu.CompilerParams(vmem_limit_bytes=SMALL),
        name="place",
    )(me, *parts)


def swap(x, axis, mask):
    return lax.ppermute(x, axis, [(i, i ^ mask) for i in range(lax.axis_size(axis))])


def after(x, *others):
    return lax.optimization_barrier((x, *others))[0]


def fast(*args):
    return ordered(*args)


def ordered(acts, grads, adapter, rank_sketch, out_sketch, held, perm):
    feat, ex = lax.axis_index("feat"), lax.axis_index("ex")
    n_ex = lax.axis_size("ex")
    _, _, width = acts.shape
    middle = (feat == 1) | (feat == 2)
    me_ex = ex.astype(jnp.int32).reshape(1)
    me_feat = feat.astype(jnp.int32).reshape(1)
    acts2, grads2 = acts.reshape(-1, width), grads.reshape(-1, width)
    adapter, rank_sketch, out_sketch, held_far, acts2, grads2 = (
        pltpu.with_memory_space_constraint(x, pltpu.HBM)
        for x in (adapter, rank_sketch.T, out_sketch, held, acts2, grads2)
    )
    down_like = jax.ShapeDtypeStruct((width, 2 * rank_sketch.shape[0]), jnp.bfloat16)
    square_like = jax.ShapeDtypeStruct((held.shape[0], 1), jnp.float32)
    inward = [(0, 1), (3, 2)]
    inner = [(1, 2), (2, 1), (0, 0), (3, 3)]
    is_middle = middle.astype(jnp.int32).reshape(1)

    def onward(raw, got):
        return small(onward_kernel, raw.shape, is_middle, [raw, got])

    raw0_a, down, own_square = project(
        first_kernel, me_feat, 0, 1, acts2, grads2, [adapter, rank_sketch, out_sketch, held_far], [down_like, square_like]
    )
    got1 = [swap(raw0_a, "feat", 1)]
    squares = [own_square] + [swap(own_square, "feat", mask) for mask in (1, 2, 3)]
    raw0_b, *raw1 = project(more_kernel, me_feat, 1, 3, acts2, grads2, [down, out_sketch], [])
    got1.append(swap(raw0_b, "feat", 1))
    got2 = [swap(raw1[0], "feat", 1)]
    sent1 = [onward(after(raw0_a, raw1[1]), got1[0])]
    far = [lax.ppermute(sent1[0], "feat", inner)]

    squares[1:] = [after(x, sent1[0]) for x in squares[1:]]
    other, *parts = lang_parts(me_ex, held, squares, perm % LANGS, n_ex)
    other = swap(other, "ex", 1)
    parts = [x + other[i] for i, x in enumerate(parts)]
    scattered = [swap(parts[i], "ex", 2 * i) for i in range(1, n_ex // 2)]
    sent1.append(onward(after(raw0_b, parts[0]), got1[1]))
    far.append(lax.ppermute(sent1[1], "feat", inner))
    lang = after(parts[0], sent1[1]) + sum(scattered)
    other = swap(lang, "feat", 1)
    got2.append(lax.ppermute(after(raw1[1], lang), "feat", inward))
    raw2 = project(more_kernel, me_feat, 4, 2, acts2, grads2, [after(down, lang), out_sketch], [])
    sent3 = [onward(raw2[0], far[0])]
    got3 = [swap(sent3[0], "feat", 1)]
    pair = small(stack_kernel, (2, *lang.shape), is_middle, [lang, after(other, sent3[0])])
    far_pair = [lax.ppermute(pair, "feat", inner)]
    far_pair.append(lax.ppermute(pair, "feat", [(1, 3), (2, 0)]))
    sent2 = [onward(after(raw1[0], pair), got2[0])]
    near = [lax.ppermute(sent2[0], "feat", inner)]
    pair = after(pair, sent2[0])
    langs = [small(join_kernel, (4, *lang.shape), is_middle, [pair, *far_pair])]
    langs = langs + [swap(langs[0], "ex", mask) for mask in range(2, n_ex, 2)]
    sent3.append(onward(after(raw2[1], langs[0]), far[1]))
    got3.append(swap(sent3[1], "feat", 1))
    sent2.append(onward(after(raw1[1], sent3[1]), got2[1]))
    near.append(lax.ppermute(sent2[1], "feat", inner))
    own_a, own_b = project(more_kernel, me_feat, 6, 2, acts2, grads2, [after(down, sent2[1]), out_sketch], [])
    grad_a, square_a = product(is_middle, [own_a, got3[0], near[0]])
    langs[1:] = [after(x, square_a) for x in langs[1:]]
    langs = langs + [swap(x, "ex", 1) for x in langs]
    per_lang = perm.shape[0] * n_ex // LANGS
    scale = (KF * per_lang) ** 0.5 / per_lang
    halves = split(me_feat, me_ex, langs)
    late = [after(got3[1], halves), after(near[1], halves)]
    mine = score(is_middle, halves, [grad_a, square_a], [own_b, *late], scale)
    gathered = [mine]
    for mask in (1, 2, 3):
        gathered.append(swap(mine, "feat", mask))
    return place(me_feat, gathered)


def general(acts, grads, adapter, rank_sketch, out_sketch, held, perm):
    ex_dev = acts.shape[0]
    down = jnp.dot(adapter, rank_sketch, preferred_element_type=jnp.float32).astype(jnp.bfloat16)
    rank_part = jnp.einsum("esd,dr->esr", acts, down, preferred_element_type=jnp.float32)
    rank_side = lax.psum(rank_part, "feat")
    out_part = jnp.einsum("esd,dk->esk", grads, out_sketch, preferred_element_type=jnp.float32)
    out_side = lax.psum_scatter(out_part, "feat", scatter_dimension=2, tiled=True)
    grad = jnp.einsum("esk,esr->ekr", out_side, rank_side, precision=HIGHEST).reshape(ex_dev, -1)
    squares = lax.psum(jnp.sum(held * held, axis=1), "feat")
    unit = held * lax.rsqrt(squares + 1e-06)[:, None]
    onehot = ((perm % LANGS)[:, None] == jnp.arange(LANGS, dtype=jnp.int32)[None, :]).astype(jnp.float32)
    per_lang = perm.shape[0] * lax.axis_size("ex") // LANGS
    lang_mean = lax.psum(jnp.dot(onehot.T, unit, precision=HIGHEST), "ex") / per_lang
    inner, norm = lax.psum(
        (jnp.dot(grad, lang_mean.T, precision=HIGHEST), jnp.sum(grad * grad, axis=1)), "feat"
    )
    scale = jnp.sqrt(jnp.float32(KF * per_lang))
    return scale * inner * lax.rsqrt(norm + 1e-06)[:, None]


def solution(mesh):
    placed = (
        P("ex", None, "feat"),
        P("ex", None, "feat"),
        P("feat", None),
        P(),
        P("feat", None),
        P("ex", "feat"),
        P("ex"),
    )
    is_fast = mesh.shape["feat"] == 4 and mesh.shape["ex"] == 8
    body = fast if is_fast else general
    return jax.shard_map(body, mesh=mesh, in_specs=placed, out_specs=P("ex", None), check_vma=False)
```

```python
import functools

import jax
import jax.numpy as jnp
from jax import lax
from jax.experimental import pallas as pl
from jax.experimental.pallas import tpu as pltpu
from jax.sharding import PartitionSpec as P


KF = 8192
LANGS = 64
UNIT = 4
PIECE = 2
PIECES = 8
HIGHEST = lax.Precision.HIGHEST
SMALL = 24 * 1024 * 1024
VMEM = pl.BlockSpec(memory_space=pltpu.VMEM)
SMEM = pl.BlockSpec(memory_space=pltpu.SMEM)


def project_piece(act, grad, down, sketch, o_ref):
    rows = act.shape[0] // PIECE
    half = rows // 2
    out = jnp.dot(grad, sketch, preferred_element_type=jnp.float32)
    rank = jnp.dot(act, down, preferred_element_type=jnp.float32)
    low = lax.broadcasted_iota(jnp.int32, (half, down.shape[1]), 1) < down.shape[1] // 2
    for unit in range(PIECE):
        start = unit * rows
        o_ref[unit, :rows, :] = out[start : start + rows]
        o_ref[unit, rows:, :] = jnp.where(low, rank[start : start + half], rank[start + half : start + rows])


def first_kernel(feat, act_ref, grad_ref, adapter_ref, rank_ref, sketch_ref, held_ref, *o_refs):
    del feat
    *piece_refs, down_ref, square_ref = o_refs
    step = pl.program_id(0)

    @pl.when(step == 0)
    def _():
        down = lax.dot_general(
            adapter_ref[...], rank_ref[...], (((1,), (1,)), ((), ())), preferred_element_type=jnp.float32
        )
        down_ref[...] = jnp.concatenate([down, down], axis=1).astype(jnp.bfloat16)
        held = held_ref[...]
        square_ref[...] = jnp.sum(held * held, axis=1, keepdims=True)

    for index, ref in enumerate(piece_refs):

        @pl.when(step == index)
        def _(ref=ref):
            project_piece(act_ref[...], grad_ref[...], down_ref[...], sketch_ref[...], ref)


def more_kernel(feat, act_ref, grad_ref, down_ref, sketch_ref, *piece_refs):
    del feat
    step = pl.program_id(0)
    for index, ref in enumerate(piece_refs):

        @pl.when(step == index)
        def _(ref=ref):
            project_piece(act_ref[...], grad_ref[...], down_ref[...], sketch_ref[...], ref)


def whole(shape):
    return pl.BlockSpec(shape, lambda i, feat: (0,) * len(shape))


def chunk_of(turn, feat):
    left = feat < 2
    far, near = jnp.where(left, 3, 0), jnp.where(left, 2, 1)
    return jnp.where(turn == 0, far, jnp.where(turn == 1, near, jnp.where(turn == 2, feat ^ 1, feat)))


def project(kernel, feat, first, count, acts, grads, operands, extra):
    ko = operands[-1 if kernel is more_kernel else 2].shape[1]
    width = acts.shape[1]
    rows = acts.shape[0] // PIECES
    piece = (PIECE, rows // PIECE * 3 // 2, ko)
    block = pl.BlockSpec((rows, width), lambda i, feat: (chunk_of((first + i) // 2, feat[0]) * 2 + (first + i) % 2, 0))
    return pl.pallas_call(
        kernel,
        out_shape=[jax.ShapeDtypeStruct(piece, jnp.float32)] * count + extra,
        grid_spec=pltpu.PrefetchScalarGridSpec(
            num_scalar_prefetch=1,
            grid=(count,),
            in_specs=[block, block] + [whole(x.shape) for x in operands],
            out_specs=[whole(piece)] * count + [whole(x.shape) for x in extra],
        ),
        cost_estimate=pl.CostEstimate(
            flops=count * rows * width * ko * 4,
            bytes_accessed=count * rows * (width * 4 + ko * 6),
            transcendentals=0,
        ),
        compiler_params=pltpu.CompilerParams(vmem_limit_bytes=SMALL),
        name="project",
    )(feat, acts, grads, *operands)


def lang_kernel(me_ref, held_ref, lang_ref, *refs):
    *square_refs, other_ref = refs[:5]
    own_refs = refs[5:]
    count = len(own_refs)
    rows, width = held_ref.shape
    piece = width // (2 * count)
    hit = lang_ref[...] == lax.broadcasted_iota(jnp.int32, (LANGS, rows), 0)
    hit = jnp.where(hit, 1.0, 0.0)
    hit = jnp.concatenate([hit, hit], axis=1).astype(jnp.bfloat16)
    inverse = lax.rsqrt(sum(ref[...] for ref in square_refs) + 1e-06)

    def sums(part):
        columns = pl.ds(pl.multiple_of(part * piece, piece), piece)
        unit = held_ref[:, columns] * inverse
        high = unit.astype(jnp.bfloat16)
        rest = (unit - high.astype(jnp.float32)).astype(jnp.bfloat16)
        both = jnp.concatenate([high, rest], axis=0)
        return jnp.dot(hit, both, preferred_element_type=jnp.float32)

    for index in range(count):
        other_ref[index] = sums(me_ref[0] ^ 1 ^ (2 * index))
        own_refs[index][...] = sums(me_ref[0] ^ (2 * index))


def lang_parts(me, held, squares, lang, n_ex):
    rows, width = held.shape
    piece = width // n_ex
    half = n_ex // 2
    return pl.pallas_call(
        lang_kernel,
        out_shape=[jax.ShapeDtypeStruct((half, LANGS, piece), jnp.float32)]
        + [jax.ShapeDtypeStruct((LANGS, piece), jnp.float32)] * half,
        in_specs=[SMEM] + [VMEM] * 6,
        out_specs=[VMEM] * (1 + half),
        compiler_params=pltpu.CompilerParams(vmem_limit_bytes=SMALL),
        name="lang_parts",
    )(me, held, lang.reshape(1, rows), *squares)


def product_kernel(middle_ref, own_ref, end_ref, near_ref, o_ref, square_ref, grad_ref):
    middle = middle_ref[0] == 1
    rows = own_ref.shape[1] * 2 // 3
    seq = rows // UNIT
    wide = own_ref.shape[2]
    low = lax.broadcasted_iota(jnp.int32, (seq, wide), 1) < wide // 2

    def split(x, order):
        high = x.astype(jnp.bfloat16)
        rest = (x - high.astype(jnp.float32)).astype(jnp.bfloat16)
        return jnp.concatenate([high, rest, high] if order else [high, high, rest], axis=0)

    def total(unit, start):
        block = (unit, pl.ds(start, seq), slice(None))
        return own_ref[block] + end_ref[block] + jnp.where(middle, near_ref[block], 0.0)

    for unit in range(PIECE):
        for pair in range(UNIT // 2):
            both = total(unit, rows + pair * seq)
            turned = pltpu.roll(both, wide // 2, 1)
            for side in range(2):
                example = pair + side * (UNIT // 2)
                rank = jnp.where(low, turned, both) if side else jnp.where(low, both, turned)
                grad_ref[unit * UNIT + example] = lax.dot_general(
                    split(total(unit, example * seq), True),
                    split(rank, False),
                    (((0,), (0,)), ((), ())),
                    preferred_element_type=jnp.float32,
                )
    count = PIECE * UNIT
    low = lax.broadcasted_iota(jnp.int32, (count, wide), 1) < wide // 2
    square = jnp.zeros((count, 2 * wide), jnp.float32)
    for index in range(o_ref.shape[0]):
        rows_of = [grad_ref[:, 4 * index + j, :] for j in range(4)]
        part = jnp.concatenate(
            [jnp.where(low, rows_of[0], rows_of[1]), jnp.where(low, rows_of[2], rows_of[3])], axis=1
        )
        square += part * part
        rest = part - part.astype(jnp.bfloat16).astype(jnp.float32)
        o_ref[index] = jnp.concatenate([part, rest], axis=0).astype(jnp.bfloat16)
    square_ref[...] = jnp.sum(square, axis=1, keepdims=True)


def product(middle, parts):
    count, wide = PIECE * UNIT, parts[0].shape[2]
    return pl.pallas_call(
        product_kernel,
        out_shape=[
            jax.ShapeDtypeStruct((wide // 4, 2 * count, 2 * wide), jnp.bfloat16),
            jax.ShapeDtypeStruct((count, 1), jnp.float32),
        ],
        in_specs=[SMEM] + [VMEM] * len(parts),
        out_specs=[VMEM] * 2,
        scratch_shapes=[pltpu.VMEM((count, wide, wide), jnp.float32)],
        compiler_params=pltpu.CompilerParams(vmem_limit_bytes=SMALL),
        name="product",
    )(middle, *parts)


def split_kernel(feat_ref, ex_ref, *refs):
    *lang_refs, o_ref = refs
    feat, ex = feat_ref[0], ex_ref[0]
    middle = (feat == 1) | (feat == 2)
    second = feat ^ jnp.where(middle, 3, 2)
    rows_from = [feat, feat ^ 1, second, second ^ 1]
    n_ex = len(lang_refs)
    masks = [*range(0, n_ex, 2), *range(1, n_ex, 2)]
    for j, ref in enumerate(lang_refs):
        for m in range(4):
            lang = ref[m]
            rest = lang - lang.astype(jnp.bfloat16).astype(jnp.float32)
            o_ref[rows_from[m] * n_ex + (ex ^ masks[j])] = jnp.concatenate([lang, rest], axis=0).astype(jnp.bfloat16)


def split(feat, ex, langs):
    rows, count, piece = langs[0].shape
    return pl.pallas_call(
        split_kernel,
        out_shape=jax.ShapeDtypeStruct((rows * len(langs), 2 * count, piece), jnp.bfloat16),
        in_specs=[SMEM] * 2 + [VMEM] * len(langs),
        out_specs=VMEM,
        compiler_params=pltpu.CompilerParams(vmem_limit_bytes=SMALL),
        name="split",
    )(feat, ex, *langs)


def score_kernel(middle_ref, lang_ref, grad_a, square_a, *refs, scale):
    *part_refs, o_ref, grad_b, square_b, grad_ref = refs
    product_kernel(middle_ref, *part_refs, grad_b, square_b, grad_ref)
    total = None
    for index in range(lang_ref.shape[0]):
        grad = jnp.concatenate([grad_a[index], grad_b[index]], axis=0)
        term = lax.dot_general(
            grad, lang_ref[index], (((1,), (1,)), ((), ())), preferred_element_type=jnp.float32
        )
        total = term if total is None else total + term
    total = total + pltpu.roll(total, LANGS, 1)
    count = square_a.shape[0]
    for index, square_ref in enumerate([square_a, square_b]):
        start = 2 * count * index
        inner = total[start : start + count, :LANGS] + total[start + count : start + 2 * count, :LANGS]
        o_ref[index * count : (index + 1) * count] = inner * (lax.rsqrt(square_ref[...] + 1e-06) * scale)


def score(middle, langs, first, parts, scale):
    grad, square = first
    operands = [langs, *first, *parts]
    wide = parts[0].shape[2]
    return pl.pallas_call(
        functools.partial(score_kernel, scale=scale),
        out_shape=jax.ShapeDtypeStruct((2 * square.shape[0], LANGS), jnp.float32),
        in_specs=[SMEM] + [VMEM] * len(operands),
        out_specs=VMEM,
        scratch_shapes=[
            pltpu.VMEM(grad.shape, grad.dtype),
            pltpu.VMEM(square.shape, square.dtype),
            pltpu.VMEM((square.shape[0], wide, wide), jnp.float32),
        ],
        compiler_params=pltpu.CompilerParams(vmem_limit_bytes=SMALL),
        name="score",
    )(middle, *operands)


def small(kernel, shape, middle, operands):
    return pl.pallas_call(
        kernel,
        out_shape=jax.ShapeDtypeStruct(shape, jnp.float32),
        in_specs=[SMEM] + [VMEM] * len(operands),
        out_specs=VMEM,
        compiler_params=pltpu.CompilerParams(vmem_limit_bytes=SMALL),
    )(middle, *operands)


def onward_kernel(middle_ref, raw_ref, got_ref, o_ref):
    o_ref[...] = raw_ref[...] + jnp.where(middle_ref[0] == 1, got_ref[...], 0.0)


def stack_kernel(middle_ref, one_ref, two_ref, o_ref):
    del middle_ref
    o_ref[0] = one_ref[...]
    o_ref[1] = two_ref[...]


def join_kernel(middle_ref, pair_ref, inner_ref, outer_ref, o_ref):
    o_ref[:2] = pair_ref[...]
    o_ref[2:] = jnp.where(middle_ref[0] == 1, inner_ref[...], outer_ref[...])


def place_kernel(me_ref, *refs):
    *parts, o_ref = refs
    rows = parts[0].shape[0]
    for mask, ref in enumerate(parts):
        o_ref[pl.ds(pl.multiple_of((me_ref[0] ^ mask) * rows, rows), rows), :] = ref[...]


def place(me, parts):
    rows, columns = parts[0].shape
    return pl.pallas_call(
        place_kernel,
        out_shape=jax.ShapeDtypeStruct((rows * len(parts), columns), jnp.float32),
        in_specs=[SMEM] + [VMEM] * len(parts),
        out_specs=VMEM,
        compiler_params=pltpu.CompilerParams(vmem_limit_bytes=SMALL),
        name="place",
    )(me, *parts)


def swap(x, axis, mask):
    return lax.ppermute(x, axis, [(i, i ^ mask) for i in range(lax.axis_size(axis))])


def after(x, *others):
    return lax.optimization_barrier((x, *others))[0]


def fast(*args):
    return ordered(*args)


def ordered(acts, grads, adapter, rank_sketch, out_sketch, held, perm):
    feat, ex = lax.axis_index("feat"), lax.axis_index("ex")
    n_ex = lax.axis_size("ex")
    _, _, width = acts.shape
    middle = (feat == 1) | (feat == 2)
    me_ex = ex.astype(jnp.int32).reshape(1)
    me_feat = feat.astype(jnp.int32).reshape(1)
    acts2, grads2 = acts.reshape(-1, width), grads.reshape(-1, width)
    adapter, rank_sketch, out_sketch, held_far, acts2, grads2 = (
        pltpu.with_memory_space_constraint(x, pltpu.HBM)
        for x in (adapter, rank_sketch.T, out_sketch, held, acts2, grads2)
    )
    down_like = jax.ShapeDtypeStruct((width, 2 * rank_sketch.shape[0]), jnp.bfloat16)
    square_like = jax.ShapeDtypeStruct((held.shape[0], 1), jnp.float32)
    inward = [(0, 1), (3, 2)]
    inner = [(1, 2), (2, 1), (0, 0), (3, 3)]
    is_middle = middle.astype(jnp.int32).reshape(1)

    def onward(raw, got):
        return small(onward_kernel, raw.shape, is_middle, [raw, got])

    raw0_a, down, own_square = project(
        first_kernel, me_feat, 0, 1, acts2, grads2, [adapter, rank_sketch, out_sketch, held_far], [down_like, square_like]
    )
    got1 = [swap(raw0_a, "feat", 1)]
    squares = [own_square] + [swap(own_square, "feat", mask) for mask in (1, 2, 3)]
    raw0_b, *raw1 = project(more_kernel, me_feat, 1, 3, acts2, grads2, [down, out_sketch], [])
    got1.append(swap(raw0_b, "feat", 1))
    got2 = [swap(raw1[0], "feat", 1)]
    sent1 = [onward(after(raw0_a, raw1[1]), got1[0])]
    far = [lax.ppermute(sent1[0], "feat", inner)]

    squares[1:] = [after(x, sent1[0]) for x in squares[1:]]
    other, *parts = lang_parts(me_ex, held, squares, perm % LANGS, n_ex)
    other = swap(other, "ex", 1)
    parts = [x + other[i] for i, x in enumerate(parts)]
    scattered = [swap(parts[i], "ex", 2 * i) for i in range(1, n_ex // 2)]
    sent1.append(onward(after(raw0_b, parts[0]), got1[1]))
    far.append(lax.ppermute(sent1[1], "feat", inner))
    lang = after(parts[0], sent1[1]) + sum(scattered)
    other = swap(lang, "feat", 1)
    got2.append(lax.ppermute(after(raw1[1], lang), "feat", inward))
    raw2 = project(more_kernel, me_feat, 4, 2, acts2, grads2, [after(down, lang), out_sketch], [])
    pair = small(stack_kernel, (2, *lang.shape), is_middle, [lang, after(other, raw2[0])])
    far_pair = [lax.ppermute(pair, "feat", inner)]
    far_pair.append(lax.ppermute(pair, "feat", [(1, 3), (2, 0)]))
    sent3 = [onward(after(raw2[0], pair), far[0])]
    got3 = [swap(sent3[0], "feat", 1)]
    sent2 = [onward(after(raw1[0], sent3[0]), got2[0])]
    near = [lax.ppermute(sent2[0], "feat", inner)]
    pair = after(pair, sent2[0])
    langs = [small(join_kernel, (4, *lang.shape), is_middle, [pair, *far_pair])]
    langs = langs + [swap(langs[0], "ex", mask) for mask in range(2, n_ex, 2)]
    sent3.append(onward(after(raw2[1], langs[0]), far[1]))
    got3.append(swap(sent3[1], "feat", 1))
    sent2.append(onward(after(raw1[1], sent3[1]), got2[1]))
    near.append(lax.ppermute(sent2[1], "feat", inner))
    own_a, own_b = project(more_kernel, me_feat, 6, 2, acts2, grads2, [after(down, sent2[1]), out_sketch], [])
    grad_a, square_a = product(is_middle, [own_a, got3[0], near[0]])
    langs[1:] = [after(x, square_a) for x in langs[1:]]
    langs = langs + [swap(x, "ex", 1) for x in langs]
    per_lang = perm.shape[0] * n_ex // LANGS
    scale = (KF * per_lang) ** 0.5 / per_lang
    halves = split(me_feat, me_ex, langs)
    late = [after(got3[1], halves), after(near[1], halves)]
    mine = score(is_middle, halves, [grad_a, square_a], [own_b, *late], scale)
    gathered = [mine]
    for mask in (1, 2, 3):
        gathered.append(swap(mine, "feat", mask))
    return place(me_feat, gathered)


def general(acts, grads, adapter, rank_sketch, out_sketch, held, perm):
    ex_dev = acts.shape[0]
    down = jnp.dot(adapter, rank_sketch, preferred_element_type=jnp.float32).astype(jnp.bfloat16)
    rank_part = jnp.einsum("esd,dr->esr", acts, down, preferred_element_type=jnp.float32)
    rank_side = lax.psum(rank_part, "feat")
    out_part = jnp.einsum("esd,dk->esk", grads, out_sketch, preferred_element_type=jnp.float32)
    out_side = lax.psum_scatter(out_part, "feat", scatter_dimension=2, tiled=True)
    grad = jnp.einsum("esk,esr->ekr", out_side, rank_side, precision=HIGHEST).reshape(ex_dev, -1)
    squares = lax.psum(jnp.sum(held * held, axis=1), "feat")
    unit = held * lax.rsqrt(squares + 1e-06)[:, None]
    onehot = ((perm % LANGS)[:, None] == jnp.arange(LANGS, dtype=jnp.int32)[None, :]).astype(jnp.float32)
    per_lang = perm.shape[0] * lax.axis_size("ex") // LANGS
    lang_mean = lax.psum(jnp.dot(onehot.T, unit, precision=HIGHEST), "ex") / per_lang
    inner, norm = lax.psum(
        (jnp.dot(grad, lang_mean.T, precision=HIGHEST), jnp.sum(grad * grad, axis=1)), "feat"
    )
    scale = jnp.sqrt(jnp.float32(KF * per_lang))
    return scale * inner * lax.rsqrt(norm + 1e-06)[:, None]


def solution(mesh):
    placed = (
        P("ex", None, "feat"),
        P("ex", None, "feat"),
        P("feat", None),
        P(),
        P("feat", None),
        P("ex", "feat"),
        P("ex"),
    )
    is_fast = mesh.shape["feat"] == 4 and mesh.shape["ex"] == 8
    body = fast if is_fast else general
    return jax.shard_map(body, mesh=mesh, in_specs=placed, out_specs=P("ex", None), check_vma=False)
```

```python
import functools

import jax
import jax.numpy as jnp
from jax import lax
from jax.experimental import pallas as pl
from jax.experimental.pallas import tpu as pltpu
from jax.sharding import PartitionSpec as P


KF = 8192
LANGS = 64
UNIT = 4
PIECE = 2
PIECES = 8
HIGHEST = lax.Precision.HIGHEST
SMALL = 24 * 1024 * 1024
VMEM = pl.BlockSpec(memory_space=pltpu.VMEM)
SMEM = pl.BlockSpec(memory_space=pltpu.SMEM)


def project_piece(act, grad, down, sketch, o_ref):
    rows = act.shape[0] // PIECE
    half = rows // 2
    out = jnp.dot(grad, sketch, preferred_element_type=jnp.float32)
    rank = jnp.dot(act, down, preferred_element_type=jnp.float32)
    low = lax.broadcasted_iota(jnp.int32, (half, down.shape[1]), 1) < down.shape[1] // 2
    for unit in range(PIECE):
        start = unit * rows
        o_ref[unit, :rows, :] = out[start : start + rows]
        o_ref[unit, rows:, :] = jnp.where(low, rank[start : start + half], rank[start + half : start + rows])


def first_kernel(feat, act_ref, grad_ref, adapter_ref, rank_ref, sketch_ref, held_ref, *o_refs):
    del feat
    *piece_refs, down_ref, square_ref = o_refs
    step = pl.program_id(0)

    @pl.when(step == 0)
    def _():
        down = lax.dot_general(
            adapter_ref[...], rank_ref[...], (((1,), (1,)), ((), ())), preferred_element_type=jnp.float32
        )
        down_ref[...] = jnp.concatenate([down, down], axis=1).astype(jnp.bfloat16)
        held = held_ref[...]
        square_ref[...] = jnp.sum(held * held, axis=1, keepdims=True)

    for index, ref in enumerate(piece_refs):

        @pl.when(step == index)
        def _(ref=ref):
            project_piece(act_ref[...], grad_ref[...], down_ref[...], sketch_ref[...], ref)


def more_kernel(feat, act_ref, grad_ref, down_ref, sketch_ref, *piece_refs):
    del feat
    step = pl.program_id(0)
    for index, ref in enumerate(piece_refs):

        @pl.when(step == index)
        def _(ref=ref):
            project_piece(act_ref[...], grad_ref[...], down_ref[...], sketch_ref[...], ref)


def whole(shape):
    return pl.BlockSpec(shape, lambda i, feat: (0,) * len(shape))


def chunk_of(turn, feat):
    left = feat < 2
    far, near = jnp.where(left, 3, 0), jnp.where(left, 2, 1)
    return jnp.where(turn == 0, far, jnp.where(turn == 1, near, jnp.where(turn == 2, feat ^ 1, feat)))


def project(kernel, feat, first, count, acts, grads, operands, extra):
    ko = operands[-1 if kernel is more_kernel else 2].shape[1]
    width = acts.shape[1]
    rows = acts.shape[0] // PIECES
    piece = (PIECE, rows // PIECE * 3 // 2, ko)
    block = pl.BlockSpec((rows, width), lambda i, feat: (chunk_of((first + i) // 2, feat[0]) * 2 + (first + i) % 2, 0))
    return pl.pallas_call(
        kernel,
        out_shape=[jax.ShapeDtypeStruct(piece, jnp.float32)] * count + extra,
        grid_spec=pltpu.PrefetchScalarGridSpec(
            num_scalar_prefetch=1,
            grid=(count,),
            in_specs=[block, block] + [whole(x.shape) for x in operands],
            out_specs=[whole(piece)] * count + [whole(x.shape) for x in extra],
        ),
        cost_estimate=pl.CostEstimate(
            flops=count * rows * width * ko * 4,
            bytes_accessed=count * rows * (width * 4 + ko * 6),
            transcendentals=0,
        ),
        compiler_params=pltpu.CompilerParams(vmem_limit_bytes=SMALL),
        name="project",
    )(feat, acts, grads, *operands)


def lang_kernel(me_ref, held_ref, lang_ref, *refs):
    *square_refs, other_ref = refs[:5]
    own_refs = refs[5:]
    count = len(own_refs)
    rows, width = held_ref.shape
    piece = width // (2 * count)
    hit = lang_ref[...] == lax.broadcasted_iota(jnp.int32, (LANGS, rows), 0)
    hit = jnp.where(hit, 1.0, 0.0)
    hit = jnp.concatenate([hit, hit], axis=1).astype(jnp.bfloat16)
    inverse = lax.rsqrt(sum(ref[...] for ref in square_refs) + 1e-06)

    def sums(part):
        columns = pl.ds(pl.multiple_of(part * piece, piece), piece)
        unit = held_ref[:, columns] * inverse
        high = unit.astype(jnp.bfloat16)
        rest = (unit - high.astype(jnp.float32)).astype(jnp.bfloat16)
        both = jnp.concatenate([high, rest], axis=0)
        return jnp.dot(hit, both, preferred_element_type=jnp.float32)

    for index in range(count):
        other_ref[index] = sums(me_ref[0] ^ 1 ^ (2 * index))
        own_refs[index][...] = sums(me_ref[0] ^ (2 * index))


def lang_parts(me, held, squares, lang, n_ex):
    rows, width = held.shape
    piece = width // n_ex
    half = n_ex // 2
    return pl.pallas_call(
        lang_kernel,
        out_shape=[jax.ShapeDtypeStruct((half, LANGS, piece), jnp.float32)]
        + [jax.ShapeDtypeStruct((LANGS, piece), jnp.float32)] * half,
        in_specs=[SMEM] + [VMEM] * 6,
        out_specs=[VMEM] * (1 + half),
        compiler_params=pltpu.CompilerParams(vmem_limit_bytes=SMALL),
        name="lang_parts",
    )(me, held, lang.reshape(1, rows), *squares)


def product_kernel(middle_ref, own_ref, end_ref, near_ref, o_ref, square_ref, grad_ref):
    middle = middle_ref[0] == 1
    rows = own_ref.shape[1] * 2 // 3
    seq = rows // UNIT
    wide = own_ref.shape[2]
    low = lax.broadcasted_iota(jnp.int32, (seq, wide), 1) < wide // 2

    def split(x, order):
        high = x.astype(jnp.bfloat16)
        rest = (x - high.astype(jnp.float32)).astype(jnp.bfloat16)
        return jnp.concatenate([high, rest, high] if order else [high, high, rest], axis=0)

    def total(unit, start):
        block = (unit, pl.ds(start, seq), slice(None))
        return own_ref[block] + end_ref[block] + jnp.where(middle, near_ref[block], 0.0)

    for unit in range(PIECE):
        for pair in range(UNIT // 2):
            both = total(unit, rows + pair * seq)
            turned = pltpu.roll(both, wide // 2, 1)
            for side in range(2):
                example = pair + side * (UNIT // 2)
                rank = jnp.where(low, turned, both) if side else jnp.where(low, both, turned)
                grad_ref[unit * UNIT + example] = lax.dot_general(
                    split(total(unit, example * seq), True),
                    split(rank, False),
                    (((0,), (0,)), ((), ())),
                    preferred_element_type=jnp.float32,
                )
    count = PIECE * UNIT
    low = lax.broadcasted_iota(jnp.int32, (count, wide), 1) < wide // 2
    square = jnp.zeros((count, 2 * wide), jnp.float32)
    for index in range(o_ref.shape[0]):
        rows_of = [grad_ref[:, 4 * index + j, :] for j in range(4)]
        part = jnp.concatenate(
            [jnp.where(low, rows_of[0], rows_of[1]), jnp.where(low, rows_of[2], rows_of[3])], axis=1
        )
        square += part * part
        rest = part - part.astype(jnp.bfloat16).astype(jnp.float32)
        o_ref[index] = jnp.concatenate([part, rest], axis=0).astype(jnp.bfloat16)
    square_ref[...] = jnp.sum(square, axis=1, keepdims=True)


def product(middle, parts):
    count, wide = PIECE * UNIT, parts[0].shape[2]
    return pl.pallas_call(
        product_kernel,
        out_shape=[
            jax.ShapeDtypeStruct((wide // 4, 2 * count, 2 * wide), jnp.bfloat16),
            jax.ShapeDtypeStruct((count, 1), jnp.float32),
        ],
        in_specs=[SMEM] + [VMEM] * len(parts),
        out_specs=[VMEM] * 2,
        scratch_shapes=[pltpu.VMEM((count, wide, wide), jnp.float32)],
        compiler_params=pltpu.CompilerParams(vmem_limit_bytes=SMALL),
        name="product",
    )(middle, *parts)


def split_kernel(feat_ref, ex_ref, *refs):
    *lang_refs, o_ref = refs
    feat, ex = feat_ref[0], ex_ref[0]
    middle = (feat == 1) | (feat == 2)
    second = feat ^ jnp.where(middle, 3, 2)
    rows_from = [feat, feat ^ 1, second, second ^ 1]
    n_ex = len(lang_refs)
    masks = [*range(0, n_ex, 2), *range(1, n_ex, 2)]
    for j, ref in enumerate(lang_refs):
        for m in range(4):
            lang = ref[m]
            rest = lang - lang.astype(jnp.bfloat16).astype(jnp.float32)
            o_ref[rows_from[m] * n_ex + (ex ^ masks[j])] = jnp.concatenate([lang, rest], axis=0).astype(jnp.bfloat16)


def split(feat, ex, langs):
    rows, count, piece = langs[0].shape
    return pl.pallas_call(
        split_kernel,
        out_shape=jax.ShapeDtypeStruct((rows * len(langs), 2 * count, piece), jnp.bfloat16),
        in_specs=[SMEM] * 2 + [VMEM] * len(langs),
        out_specs=VMEM,
        compiler_params=pltpu.CompilerParams(vmem_limit_bytes=SMALL),
        name="split",
    )(feat, ex, *langs)


def score_kernel(middle_ref, lang_ref, grad_a, square_a, *refs, scale):
    *part_refs, o_ref, grad_b, square_b, grad_ref = refs
    product_kernel(middle_ref, *part_refs, grad_b, square_b, grad_ref)
    total = None
    for index in range(lang_ref.shape[0]):
        grad = jnp.concatenate([grad_a[index], grad_b[index]], axis=0)
        term = lax.dot_general(
            grad, lang_ref[index], (((1,), (1,)), ((), ())), preferred_element_type=jnp.float32
        )
        total = term if total is None else total + term
    total = total + pltpu.roll(total, LANGS, 1)
    count = square_a.shape[0]
    for index, square_ref in enumerate([square_a, square_b]):
        start = 2 * count * index
        inner = total[start : start + count, :LANGS] + total[start + count : start + 2 * count, :LANGS]
        o_ref[index * count : (index + 1) * count] = inner * (lax.rsqrt(square_ref[...] + 1e-06) * scale)


def score(middle, langs, first, parts, scale):
    grad, square = first
    operands = [langs, *first, *parts]
    wide = parts[0].shape[2]
    return pl.pallas_call(
        functools.partial(score_kernel, scale=scale),
        out_shape=jax.ShapeDtypeStruct((2 * square.shape[0], LANGS), jnp.float32),
        in_specs=[SMEM] + [VMEM] * len(operands),
        out_specs=VMEM,
        scratch_shapes=[
            pltpu.VMEM(grad.shape, grad.dtype),
            pltpu.VMEM(square.shape, square.dtype),
            pltpu.VMEM((square.shape[0], wide, wide), jnp.float32),
        ],
        compiler_params=pltpu.CompilerParams(vmem_limit_bytes=SMALL),
        name="score",
    )(middle, *operands)


def small(kernel, shape, middle, operands):
    return pl.pallas_call(
        kernel,
        out_shape=jax.ShapeDtypeStruct(shape, jnp.float32),
        in_specs=[SMEM] + [VMEM] * len(operands),
        out_specs=VMEM,
        compiler_params=pltpu.CompilerParams(vmem_limit_bytes=SMALL),
    )(middle, *operands)


def onward_kernel(middle_ref, raw_ref, got_ref, o_ref):
    o_ref[...] = raw_ref[...] + jnp.where(middle_ref[0] == 1, got_ref[...], 0.0)


def stack_kernel(middle_ref, one_ref, two_ref, o_ref):
    del middle_ref
    o_ref[0] = one_ref[...]
    o_ref[1] = two_ref[...]


def join_kernel(middle_ref, pair_ref, inner_ref, outer_ref, o_ref):
    o_ref[:2] = pair_ref[...]
    o_ref[2:] = jnp.where(middle_ref[0] == 1, inner_ref[...], outer_ref[...])


def place_kernel(me_ref, *refs):
    *parts, o_ref = refs
    rows = parts[0].shape[0]
    for mask, ref in enumerate(parts):
        o_ref[pl.ds(pl.multiple_of((me_ref[0] ^ mask) * rows, rows), rows), :] = ref[...]


def place(me, parts):
    rows, columns = parts[0].shape
    return pl.pallas_call(
        place_kernel,
        out_shape=jax.ShapeDtypeStruct((rows * len(parts), columns), jnp.float32),
        in_specs=[SMEM] + [VMEM] * len(parts),
        out_specs=VMEM,
        compiler_params=pltpu.CompilerParams(vmem_limit_bytes=SMALL),
        name="place",
    )(me, *parts)


def swap(x, axis, mask):
    return lax.ppermute(x, axis, [(i, i ^ mask) for i in range(lax.axis_size(axis))])


def after(x, *others):
    return lax.optimization_barrier((x, *others))[0]


def fast(*args):
    return ordered(*args)


def ordered(acts, grads, adapter, rank_sketch, out_sketch, held, perm):
    feat, ex = lax.axis_index("feat"), lax.axis_index("ex")
    n_ex = lax.axis_size("ex")
    _, _, width = acts.shape
    middle = (feat == 1) | (feat == 2)
    me_ex = ex.astype(jnp.int32).reshape(1)
    me_feat = feat.astype(jnp.int32).reshape(1)
    acts2, grads2 = acts.reshape(-1, width), grads.reshape(-1, width)
    adapter, rank_sketch, out_sketch, held_far, acts2, grads2 = (
        pltpu.with_memory_space_constraint(x, pltpu.HBM)
        for x in (adapter, rank_sketch.T, out_sketch, held, acts2, grads2)
    )
    down_like = jax.ShapeDtypeStruct((width, 2 * rank_sketch.shape[0]), jnp.bfloat16)
    square_like = jax.ShapeDtypeStruct((held.shape[0], 1), jnp.float32)
    inward = [(0, 1), (3, 2)]
    inner = [(1, 2), (2, 1), (0, 0), (3, 3)]
    is_middle = middle.astype(jnp.int32).reshape(1)

    def onward(raw, got):
        return small(onward_kernel, raw.shape, is_middle, [raw, got])

    raw0_a, down, own_square = project(
        first_kernel, me_feat, 0, 1, acts2, grads2, [adapter, rank_sketch, out_sketch, held_far], [down_like, square_like]
    )
    got1 = [swap(raw0_a, "feat", 1)]
    squares = [own_square] + [swap(own_square, "feat", mask) for mask in (1, 2, 3)]
    [raw0_b] = project(more_kernel, me_feat, 1, 1, acts2, grads2, [down, out_sketch], [])
    got1.append(swap(raw0_b, "feat", 1))
    raw1 = project(more_kernel, me_feat, 2, 2, acts2, grads2, [after(down, raw0_b), out_sketch], [])
    got2 = [swap(raw1[0], "feat", 1)]
    sent1 = [onward(after(raw0_a, raw1[1]), got1[0])]
    far = [lax.ppermute(sent1[0], "feat", inner)]

    squares[1:] = [after(x, sent1[0]) for x in squares[1:]]
    other, *parts = lang_parts(me_ex, held, squares, perm % LANGS, n_ex)
    other = swap(other, "ex", 1)
    parts = [x + other[i] for i, x in enumerate(parts)]
    scattered = [swap(parts[i], "ex", 2 * i) for i in range(1, n_ex // 2)]
    sent1.append(onward(after(raw0_b, parts[0]), got1[1]))
    far.append(lax.ppermute(sent1[1], "feat", inner))
    lang = after(parts[0], sent1[1]) + sum(scattered)
    other = swap(lang, "feat", 1)
    got2.append(lax.ppermute(after(raw1[1], lang), "feat", inward))
    *raw2, own_a, own_b = project(
        more_kernel, me_feat, 4, 4, acts2, grads2, [after(down, lang), out_sketch], []
    )
    pair = small(stack_kernel, (2, *lang.shape), is_middle, [lang, after(other, raw2[0])])
    far_pair = [lax.ppermute(pair, "feat", inner)]
    far_pair.append(lax.ppermute(pair, "feat", [(1, 3), (2, 0)]))
    sent3 = [onward(after(raw2[0], pair), far[0])]
    got3 = [swap(sent3[0], "feat", 1)]
    sent2 = [onward(after(raw1[0], sent3[0]), got2[0])]
    near = [lax.ppermute(sent2[0], "feat", inner)]
    pair = after(pair, sent2[0])
    langs = [small(join_kernel, (4, *lang.shape), is_middle, [pair, *far_pair])]
    langs = langs + [swap(langs[0], "ex", mask) for mask in range(2, n_ex, 2)]
    sent3.append(onward(after(raw2[1], langs[0]), far[1]))
    got3.append(swap(sent3[1], "feat", 1))
    sent2.append(onward(after(raw1[1], sent3[1]), got2[1]))
    near.append(lax.ppermute(sent2[1], "feat", inner))
    grad_a, square_a = product(is_middle, [after(own_a, sent2[1]), got3[0], near[0]])
    langs[1:] = [after(x, square_a) for x in langs[1:]]
    langs = langs + [swap(x, "ex", 1) for x in langs]
    per_lang = perm.shape[0] * n_ex // LANGS
    scale = (KF * per_lang) ** 0.5 / per_lang
    halves = split(me_feat, me_ex, langs)
    late = [after(got3[1], halves), after(near[1], halves)]
    mine = score(is_middle, halves, [grad_a, square_a], [own_b, *late], scale)
    gathered = [mine]
    for mask in (1, 2, 3):
        gathered.append(swap(mine, "feat", mask))
    return place(me_feat, gathered)


def general(acts, grads, adapter, rank_sketch, out_sketch, held, perm):
    ex_dev = acts.shape[0]
    down = jnp.dot(adapter, rank_sketch, preferred_element_type=jnp.float32).astype(jnp.bfloat16)
    rank_part = jnp.einsum("esd,dr->esr", acts, down, preferred_element_type=jnp.float32)
    rank_side = lax.psum(rank_part, "feat")
    out_part = jnp.einsum("esd,dk->esk", grads, out_sketch, preferred_element_type=jnp.float32)
    out_side = lax.psum_scatter(out_part, "feat", scatter_dimension=2, tiled=True)
    grad = jnp.einsum("esk,esr->ekr", out_side, rank_side, precision=HIGHEST).reshape(ex_dev, -1)
    squares = lax.psum(jnp.sum(held * held, axis=1), "feat")
    unit = held * lax.rsqrt(squares + 1e-06)[:, None]
    onehot = ((perm % LANGS)[:, None] == jnp.arange(LANGS, dtype=jnp.int32)[None, :]).astype(jnp.float32)
    per_lang = perm.shape[0] * lax.axis_size("ex") // LANGS
    lang_mean = lax.psum(jnp.dot(onehot.T, unit, precision=HIGHEST), "ex") / per_lang
    inner, norm = lax.psum(
        (jnp.dot(grad, lang_mean.T, precision=HIGHEST), jnp.sum(grad * grad, axis=1)), "feat"
    )
    scale = jnp.sqrt(jnp.float32(KF * per_lang))
    return scale * inner * lax.rsqrt(norm + 1e-06)[:, None]


def solution(mesh):
    placed = (
        P("ex", None, "feat"),
        P("ex", None, "feat"),
        P("feat", None),
        P(),
        P("feat", None),
        P("ex", "feat"),
        P("ex"),
    )
    is_fast = mesh.shape["feat"] == 4 and mesh.shape["ex"] == 8
    body = fast if is_fast else general
    return jax.shard_map(body, mesh=mesh, in_specs=placed, out_specs=P("ex", None), check_vma=False)
```

```python
import functools

import jax
import jax.numpy as jnp
from jax import lax
from jax.experimental import pallas as pl
from jax.experimental.pallas import tpu as pltpu
from jax.sharding import PartitionSpec as P


KF = 8192
LANGS = 64
UNIT = 4
PIECE = 2
PIECES = 8
HIGHEST = lax.Precision.HIGHEST
SMALL = 24 * 1024 * 1024
VMEM = pl.BlockSpec(memory_space=pltpu.VMEM)
SMEM = pl.BlockSpec(memory_space=pltpu.SMEM)


def project_piece(act, grad, down, sketch, o_ref):
    rows = act.shape[0] // PIECE
    half = rows // 2
    out = jnp.dot(grad, sketch, preferred_element_type=jnp.float32)
    rank = jnp.dot(act, down, preferred_element_type=jnp.float32)
    low = lax.broadcasted_iota(jnp.int32, (half, down.shape[1]), 1) < down.shape[1] // 2
    for unit in range(PIECE):
        start = unit * rows
        o_ref[unit, :rows, :] = out[start : start + rows]
        o_ref[unit, rows:, :] = jnp.where(low, rank[start : start + half], rank[start + half : start + rows])


def first_kernel(feat, act_ref, grad_ref, adapter_ref, rank_ref, sketch_ref, held_ref, *o_refs):
    del feat
    *piece_refs, down_ref, square_ref = o_refs
    step = pl.program_id(0)

    @pl.when(step == 0)
    def _():
        down = lax.dot_general(
            adapter_ref[...], rank_ref[...], (((1,), (1,)), ((), ())), preferred_element_type=jnp.float32
        )
        down_ref[...] = jnp.concatenate([down, down], axis=1).astype(jnp.bfloat16)
        held = held_ref[...]
        square_ref[...] = jnp.sum(held * held, axis=1, keepdims=True)

    for index, ref in enumerate(piece_refs):

        @pl.when(step == index)
        def _(ref=ref):
            project_piece(act_ref[...], grad_ref[...], down_ref[...], sketch_ref[...], ref)


def more_kernel(feat, act_ref, grad_ref, down_ref, sketch_ref, *piece_refs):
    del feat
    step = pl.program_id(0)
    for index, ref in enumerate(piece_refs):

        @pl.when(step == index)
        def _(ref=ref):
            project_piece(act_ref[...], grad_ref[...], down_ref[...], sketch_ref[...], ref)


def whole(shape):
    return pl.BlockSpec(shape, lambda i, feat: (0,) * len(shape))


def chunk_of(turn, feat):
    left = feat < 2
    far, near = jnp.where(left, 3, 0), jnp.where(left, 2, 1)
    return jnp.where(turn == 0, far, jnp.where(turn == 1, near, jnp.where(turn == 2, feat ^ 1, feat)))


def project(kernel, feat, first, count, acts, grads, operands, extra):
    ko = operands[-1 if kernel is more_kernel else 2].shape[1]
    width = acts.shape[1]
    rows = acts.shape[0] // PIECES
    piece = (PIECE, rows // PIECE * 3 // 2, ko)
    block = pl.BlockSpec((rows, width), lambda i, feat: (chunk_of((first + i) // 2, feat[0]) * 2 + (first + i) % 2, 0))
    return pl.pallas_call(
        kernel,
        out_shape=[jax.ShapeDtypeStruct(piece, jnp.float32)] * count + extra,
        grid_spec=pltpu.PrefetchScalarGridSpec(
            num_scalar_prefetch=1,
            grid=(count,),
            in_specs=[block, block] + [whole(x.shape) for x in operands],
            out_specs=[whole(piece)] * count + [whole(x.shape) for x in extra],
        ),
        cost_estimate=pl.CostEstimate(
            flops=count * rows * width * ko * 4,
            bytes_accessed=count * rows * (width * 4 + ko * 6),
            transcendentals=0,
        ),
        compiler_params=pltpu.CompilerParams(vmem_limit_bytes=SMALL),
        name="project",
    )(feat, acts, grads, *operands)


def lang_kernel(me_ref, held_ref, lang_ref, *refs):
    *square_refs, other_ref = refs[:5]
    own_refs = refs[5:]
    count = len(own_refs)
    rows, width = held_ref.shape
    piece = width // (2 * count)
    hit = lang_ref[...] == lax.broadcasted_iota(jnp.int32, (LANGS, rows), 0)
    hit = jnp.where(hit, 1.0, 0.0)
    hit = jnp.concatenate([hit, hit], axis=1).astype(jnp.bfloat16)
    inverse = lax.rsqrt(sum(ref[...] for ref in square_refs) + 1e-06)

    def sums(part):
        columns = pl.ds(pl.multiple_of(part * piece, piece), piece)
        unit = held_ref[:, columns] * inverse
        high = unit.astype(jnp.bfloat16)
        rest = (unit - high.astype(jnp.float32)).astype(jnp.bfloat16)
        both = jnp.concatenate([high, rest], axis=0)
        return jnp.dot(hit, both, preferred_element_type=jnp.float32)

    for index in range(count):
        other_ref[index] = sums(me_ref[0] ^ 1 ^ (2 * index))
        own_refs[index][...] = sums(me_ref[0] ^ (2 * index))


def lang_parts(me, held, squares, lang, n_ex):
    rows, width = held.shape
    piece = width // n_ex
    half = n_ex // 2
    return pl.pallas_call(
        lang_kernel,
        out_shape=[jax.ShapeDtypeStruct((half, LANGS, piece), jnp.float32)]
        + [jax.ShapeDtypeStruct((LANGS, piece), jnp.float32)] * half,
        in_specs=[SMEM] + [VMEM] * 6,
        out_specs=[VMEM] * (1 + half),
        compiler_params=pltpu.CompilerParams(vmem_limit_bytes=SMALL),
        name="lang_parts",
    )(me, held, lang.reshape(1, rows), *squares)


def product_kernel(middle_ref, own_ref, end_ref, near_ref, o_ref, square_ref, grad_ref):
    middle = middle_ref[0] == 1
    rows = own_ref.shape[1] * 2 // 3
    seq = rows // UNIT
    wide = own_ref.shape[2]
    low = lax.broadcasted_iota(jnp.int32, (seq, wide), 1) < wide // 2

    def split(x, order):
        high = x.astype(jnp.bfloat16)
        rest = (x - high.astype(jnp.float32)).astype(jnp.bfloat16)
        return jnp.concatenate([high, rest, high] if order else [high, high, rest], axis=0)

    def total(unit, start):
        block = (unit, pl.ds(start, seq), slice(None))
        return own_ref[block] + end_ref[block] + jnp.where(middle, near_ref[block], 0.0)

    for unit in range(PIECE):
        for pair in range(UNIT // 2):
            both = total(unit, rows + pair * seq)
            turned = pltpu.roll(both, wide // 2, 1)
            for side in range(2):
                example = pair + side * (UNIT // 2)
                rank = jnp.where(low, turned, both) if side else jnp.where(low, both, turned)
                grad_ref[unit * UNIT + example] = lax.dot_general(
                    split(total(unit, example * seq), True),
                    split(rank, False),
                    (((0,), (0,)), ((), ())),
                    preferred_element_type=jnp.float32,
                )
    count = PIECE * UNIT
    low = lax.broadcasted_iota(jnp.int32, (count, wide), 1) < wide // 2
    square = jnp.zeros((count, 2 * wide), jnp.float32)
    for index in range(o_ref.shape[0]):
        rows_of = [grad_ref[:, 4 * index + j, :] for j in range(4)]
        part = jnp.concatenate(
            [jnp.where(low, rows_of[0], rows_of[1]), jnp.where(low, rows_of[2], rows_of[3])], axis=1
        )
        square += part * part
        rest = part - part.astype(jnp.bfloat16).astype(jnp.float32)
        o_ref[index] = jnp.concatenate([part, rest], axis=0).astype(jnp.bfloat16)
    square_ref[...] = jnp.sum(square, axis=1, keepdims=True)


def product(middle, parts):
    count, wide = PIECE * UNIT, parts[0].shape[2]
    return pl.pallas_call(
        product_kernel,
        out_shape=[
            jax.ShapeDtypeStruct((wide // 4, 2 * count, 2 * wide), jnp.bfloat16),
            jax.ShapeDtypeStruct((count, 1), jnp.float32),
        ],
        in_specs=[SMEM] + [VMEM] * len(parts),
        out_specs=[VMEM] * 2,
        scratch_shapes=[pltpu.VMEM((count, wide, wide), jnp.float32)],
        compiler_params=pltpu.CompilerParams(vmem_limit_bytes=SMALL),
        name="product",
    )(middle, *parts)


def split_kernel(feat_ref, ex_ref, *refs):
    *lang_refs, o_ref = refs
    feat, ex = feat_ref[0], ex_ref[0]
    middle = (feat == 1) | (feat == 2)
    second = feat ^ jnp.where(middle, 3, 2)
    rows_from = [feat, feat ^ 1, second, second ^ 1]
    n_ex = len(lang_refs)
    masks = [*range(0, n_ex, 2), *range(1, n_ex, 2)]
    for j, ref in enumerate(lang_refs):
        for m in range(4):
            lang = ref[m]
            rest = lang - lang.astype(jnp.bfloat16).astype(jnp.float32)
            o_ref[rows_from[m] * n_ex + (ex ^ masks[j])] = jnp.concatenate([lang, rest], axis=0).astype(jnp.bfloat16)


def split(feat, ex, langs):
    rows, count, piece = langs[0].shape
    return pl.pallas_call(
        split_kernel,
        out_shape=jax.ShapeDtypeStruct((rows * len(langs), 2 * count, piece), jnp.bfloat16),
        in_specs=[SMEM] * 2 + [VMEM] * len(langs),
        out_specs=VMEM,
        compiler_params=pltpu.CompilerParams(vmem_limit_bytes=SMALL),
        name="split",
    )(feat, ex, *langs)


def score_kernel(middle_ref, lang_ref, grad_a, square_a, *refs, scale):
    *part_refs, o_ref, grad_b, square_b, grad_ref = refs
    product_kernel(middle_ref, *part_refs, grad_b, square_b, grad_ref)
    total = None
    for index in range(lang_ref.shape[0]):
        grad = jnp.concatenate([grad_a[index], grad_b[index]], axis=0)
        term = lax.dot_general(
            grad, lang_ref[index], (((1,), (1,)), ((), ())), preferred_element_type=jnp.float32
        )
        total = term if total is None else total + term
    total = total + pltpu.roll(total, LANGS, 1)
    count = square_a.shape[0]
    for index, square_ref in enumerate([square_a, square_b]):
        start = 2 * count * index
        inner = total[start : start + count, :LANGS] + total[start + count : start + 2 * count, :LANGS]
        o_ref[index * count : (index + 1) * count] = inner * (lax.rsqrt(square_ref[...] + 1e-06) * scale)


def score(middle, langs, first, parts, scale):
    grad, square = first
    operands = [langs, *first, *parts]
    wide = parts[0].shape[2]
    return pl.pallas_call(
        functools.partial(score_kernel, scale=scale),
        out_shape=jax.ShapeDtypeStruct((2 * square.shape[0], LANGS), jnp.float32),
        in_specs=[SMEM] + [VMEM] * len(operands),
        out_specs=VMEM,
        scratch_shapes=[
            pltpu.VMEM(grad.shape, grad.dtype),
            pltpu.VMEM(square.shape, square.dtype),
            pltpu.VMEM((square.shape[0], wide, wide), jnp.float32),
        ],
        compiler_params=pltpu.CompilerParams(vmem_limit_bytes=SMALL),
        name="score",
    )(middle, *operands)


def small(kernel, shape, middle, operands):
    return pl.pallas_call(
        kernel,
        out_shape=jax.ShapeDtypeStruct(shape, jnp.float32),
        in_specs=[SMEM] + [VMEM] * len(operands),
        out_specs=VMEM,
        compiler_params=pltpu.CompilerParams(vmem_limit_bytes=SMALL),
    )(middle, *operands)


def onward_kernel(middle_ref, raw_ref, got_ref, o_ref):
    o_ref[...] = raw_ref[...] + jnp.where(middle_ref[0] == 1, got_ref[...], 0.0)


def stack_kernel(middle_ref, one_ref, two_ref, o_ref):
    del middle_ref
    o_ref[0] = one_ref[...]
    o_ref[1] = two_ref[...]


def join_kernel(middle_ref, pair_ref, inner_ref, outer_ref, o_ref):
    o_ref[:2] = pair_ref[...]
    o_ref[2:] = jnp.where(middle_ref[0] == 1, inner_ref[...], outer_ref[...])


def place_kernel(me_ref, *refs):
    *parts, o_ref = refs
    rows = parts[0].shape[0]
    for mask, ref in enumerate(parts):
        o_ref[pl.ds(pl.multiple_of((me_ref[0] ^ mask) * rows, rows), rows), :] = ref[...]


def place(me, parts):
    rows, columns = parts[0].shape
    return pl.pallas_call(
        place_kernel,
        out_shape=jax.ShapeDtypeStruct((rows * len(parts), columns), jnp.float32),
        in_specs=[SMEM] + [VMEM] * len(parts),
        out_specs=VMEM,
        compiler_params=pltpu.CompilerParams(vmem_limit_bytes=SMALL),
        name="place",
    )(me, *parts)


def swap(x, axis, mask):
    return lax.ppermute(x, axis, [(i, i ^ mask) for i in range(lax.axis_size(axis))])


def after(x, *others):
    return lax.optimization_barrier((x, *others))[0]


def fast(*args):
    return ordered(*args)


def ordered(acts, grads, adapter, rank_sketch, out_sketch, held, perm):
    feat, ex = lax.axis_index("feat"), lax.axis_index("ex")
    n_ex = lax.axis_size("ex")
    _, _, width = acts.shape
    middle = (feat == 1) | (feat == 2)
    me_ex = ex.astype(jnp.int32).reshape(1)
    me_feat = feat.astype(jnp.int32).reshape(1)
    acts2, grads2 = acts.reshape(-1, width), grads.reshape(-1, width)
    adapter, rank_sketch, out_sketch, held_far, acts2, grads2 = (
        pltpu.with_memory_space_constraint(x, pltpu.HBM)
        for x in (adapter, rank_sketch.T, out_sketch, held, acts2, grads2)
    )
    down_like = jax.ShapeDtypeStruct((width, 2 * rank_sketch.shape[0]), jnp.bfloat16)
    square_like = jax.ShapeDtypeStruct((held.shape[0], 1), jnp.float32)
    inward = [(0, 1), (3, 2)]
    inner = [(1, 2), (2, 1), (0, 0), (3, 3)]
    is_middle = middle.astype(jnp.int32).reshape(1)

    def onward(raw, got):
        return small(onward_kernel, raw.shape, is_middle, [raw, got])

    raw0_a, down, own_square = project(
        first_kernel, me_feat, 0, 1, acts2, grads2, [adapter, rank_sketch, out_sketch, held_far], [down_like, square_like]
    )
    got1 = [swap(raw0_a, "feat", 1)]
    squares = [own_square] + [swap(own_square, "feat", mask) for mask in (1, 2, 3)]
    [raw0_b] = project(more_kernel, me_feat, 1, 1, acts2, grads2, [down, out_sketch], [])
    got1.append(swap(raw0_b, "feat", 1))
    raw1 = project(more_kernel, me_feat, 2, 2, acts2, grads2, [after(down, raw0_b), out_sketch], [])
    got2 = [swap(raw1[0], "feat", 1)]
    sent1 = [onward(after(raw0_a, raw1[1]), got1[0])]
    far = [lax.ppermute(sent1[0], "feat", inner)]

    squares[1:] = [after(x, sent1[0]) for x in squares[1:]]
    other, *parts = lang_parts(me_ex, held, squares, perm % LANGS, n_ex)
    other = swap(other, "ex", 1)
    parts = [x + other[i] for i, x in enumerate(parts)]
    scattered = [swap(parts[i], "ex", 2 * i) for i in range(1, n_ex // 2)]
    sent1.append(onward(after(raw0_b, parts[0]), got1[1]))
    far.append(lax.ppermute(sent1[1], "feat", inner))
    lang = after(parts[0], sent1[1]) + sum(scattered)
    other = swap(lang, "feat", 1)
    got2.append(lax.ppermute(after(raw1[1], lang), "feat", inward))
    raw2 = project(more_kernel, me_feat, 4, 2, acts2, grads2, [after(down, lang), out_sketch], [])
    pair = small(stack_kernel, (2, *lang.shape), is_middle, [lang, after(other, raw2[0])])
    far_pair = [lax.ppermute(pair, "feat", inner)]
    far_pair.append(lax.ppermute(pair, "feat", [(1, 3), (2, 0)]))
    sent3 = [onward(after(raw2[0], pair), far[0])]
    got3 = [swap(sent3[0], "feat", 1)]
    sent2 = [onward(after(raw1[0], sent3[0]), got2[0])]
    near = [lax.ppermute(sent2[0], "feat", inner)]
    pair = after(pair, sent2[0])
    langs = [small(join_kernel, (4, *lang.shape), is_middle, [pair, *far_pair])]
    langs = langs + [swap(langs[0], "ex", mask) for mask in range(2, n_ex, 2)]
    sent2.append(onward(after(raw1[1], langs[0]), got2[1]))
    near.append(lax.ppermute(sent2[1], "feat", inner))
    sent3.append(onward(after(raw2[1], sent2[1]), far[1]))
    got3.append(swap(sent3[1], "feat", 1))
    own_a, own_b = project(more_kernel, me_feat, 6, 2, acts2, grads2, [after(down, sent3[1]), out_sketch], [])
    grad_a, square_a = product(is_middle, [own_a, got3[0], near[0]])
    langs[1:] = [after(x, square_a) for x in langs[1:]]
    langs = langs + [swap(x, "ex", 1) for x in langs]
    per_lang = perm.shape[0] * n_ex // LANGS
    scale = (KF * per_lang) ** 0.5 / per_lang
    halves = split(me_feat, me_ex, langs)
    late = [after(got3[1], halves), after(near[1], halves)]
    mine = score(is_middle, halves, [grad_a, square_a], [own_b, *late], scale)
    gathered = [mine]
    for mask in (1, 2, 3):
        gathered.append(swap(mine, "feat", mask))
    return place(me_feat, gathered)


def general(acts, grads, adapter, rank_sketch, out_sketch, held, perm):
    ex_dev = acts.shape[0]
    down = jnp.dot(adapter, rank_sketch, preferred_element_type=jnp.float32).astype(jnp.bfloat16)
    rank_part = jnp.einsum("esd,dr->esr", acts, down, preferred_element_type=jnp.float32)
    rank_side = lax.psum(rank_part, "feat")
    out_part = jnp.einsum("esd,dk->esk", grads, out_sketch, preferred_element_type=jnp.float32)
    out_side = lax.psum_scatter(out_part, "feat", scatter_dimension=2, tiled=True)
    grad = jnp.einsum("esk,esr->ekr", out_side, rank_side, precision=HIGHEST).reshape(ex_dev, -1)
    squares = lax.psum(jnp.sum(held * held, axis=1), "feat")
    unit = held * lax.rsqrt(squares + 1e-06)[:, None]
    onehot = ((perm % LANGS)[:, None] == jnp.arange(LANGS, dtype=jnp.int32)[None, :]).astype(jnp.float32)
    per_lang = perm.shape[0] * lax.axis_size("ex") // LANGS
    lang_mean = lax.psum(jnp.dot(onehot.T, unit, precision=HIGHEST), "ex") / per_lang
    inner, norm = lax.psum(
        (jnp.dot(grad, lang_mean.T, precision=HIGHEST), jnp.sum(grad * grad, axis=1)), "feat"
    )
    scale = jnp.sqrt(jnp.float32(KF * per_lang))
    return scale * inner * lax.rsqrt(norm + 1e-06)[:, None]


def solution(mesh):
    placed = (
        P("ex", None, "feat"),
        P("ex", None, "feat"),
        P("feat", None),
        P(),
        P("feat", None),
        P("ex", "feat"),
        P("ex"),
    )
    is_fast = mesh.shape["feat"] == 4 and mesh.shape["ex"] == 8
    body = fast if is_fast else general
    return jax.shard_map(body, mesh=mesh, in_specs=placed, out_specs=P("ex", None), check_vma=False)
```
